32 devices in a mesh: dp: 16 (over z, y, x), tensor: 2 (over core).
Axes of the slice: x: 2, y: 2, z: 4, core: 2. Of those that a mesh axis runs over, the one named last changes fastest.
Arguments:
- tokens: bfloat16 [4096, 1024], P('dp'), may hold values from -6 to 6
- encoder_states: bfloat16 [4096, 1024], P('dp'), may hold values from -6 to 6
- cotangent: bfloat16 [4096, 1024], P('dp'), may hold values from -6 to 6
- lengths: int32 [16], replicated, may hold values from 1 to 256, 3686 in all
- deal_order: int32 [16], replicated, may hold values from 0 to 15, each once
- bucket_index: int32 [256], replicated, may hold values from 0 to 31, as said below
- rel_table: float32 [32, 16], P(None, 'tensor'), may hold values from -4 to 4
- gain_self: float32 [1024], replicated, may hold values from 0.5 to 1.5
- self_query: bfloat16 [1024, 1024], P('dp', 'tensor'), may hold values from -0.046875 to 0.046875
- self_key: bfloat16 [1024, 1024], P('dp', 'tensor'), may hold values from -0.1875 to 0.1875
- self_value: bfloat16 [1024, 1024], P('dp', 'tensor'), may hold values from -0.1875 to 0.1875
- self_output: bfloat16 [1024, 1024], P('dp', 'tensor'), may hold values from -0.75 to 0.75
- gain_cross: float32 [1024], replicated, may hold values from 0.5 to 1.5
- cross_query: bfloat16 [1024, 1024], P('dp', 'tensor'), may hold values from -0.046875 to 0.046875
- cross_key: bfloat16 [1024, 1024], P('dp', 'tensor'), may hold values from -0.1875 to 0.1875
- cross_value: bfloat16 [1024, 1024], P('dp', 'tensor'), may hold values from -0.1875 to 0.1875
- cross_output: bfloat16 [1024, 1024], P('dp', 'tensor'), may hold values from -0.75 to 0.75
- gain_feed: float32 [1024], replicated, may hold values from 0.5 to 1.5
- feed_gate: bfloat16 [1024, 2816], P('dp', 'tensor'), may hold values from -0.1875 to 0.1875
- feed_value: bfloat16 [1024, 2816], P('dp', 'tensor'), may hold values from -0.1875 to 0.1875
- feed_output: bfloat16 [1024, 2816], P('dp', 'tensor'), may hold values from -0.109375 to 0.109375
Outputs:
- layer_out: bfloat16 [4096, 1024], P('dp')
- tokens_grad: bfloat16 [4096, 1024], P('dp')
- encoder_grad: bfloat16 [4096, 1024], P(('dp', 'tensor'))
- rel_table_grad: float32 [32, 16], P(None, 'tensor')
- gain_self_grad: float32 [1024], replicated
- self_query_grad: float32 [1024, 1024], P('dp', 'tensor')
- self_key_grad: float32 [1024, 1024], P('dp', 'tensor')
- self_value_grad: float32 [1024, 1024], P('dp', 'tensor')
- self_output_grad: float32 [1024, 1024], P('dp', 'tensor')
- gain_cross_grad: float32 [1024], replicated
- cross_query_grad: float32 [1024, 1024], P('dp', 'tensor')
- cross_key_grad: float32 [1024, 1024], P('dp', 'tensor')
- cross_value_grad: float32 [1024, 1024], P('dp', 'tensor')
- cross_output_grad: float32 [1024, 1024], P('dp', 'tensor')
- gain_feed_grad: float32 [1024], replicated
- feed_gate_grad: float32 [1024, 2816], P('dp', 'tensor')
- feed_value_grad: float32 [1024, 2816], P('dp', 'tensor')
- feed_output_grad: float32 [1024, 2816], P('dp', 'tensor')
The draws below stay inside these ranges and needn't reach their ends.
Inputs may be any that keep to these rules, and one draw needn't show every extreme that they name: `lengths`: one sequence has exactly 256 tokens. `deal_order`: each dp index receives exactly one sequence. `bucket_index`: never falls as the distance grows; distance 0 has bucket 0 and distance 256 - 1 has bucket 32 - 1.
All inputs are finite; a program needn't handle non-finite values.
Results may differ from the reference program's by a relative error of at most 0.04.
Values may be sent and summed in bfloat16 or wider, within the bound.
No kernel may reach another device: no remote copies, remote signals or barrier semaphores. Data moves between devices by JAX's collectives and lax.ppermute only.
A program may use at most 192 MiB of HBM per device.

```python
import math
import jax
import jax.numpy as jnp
import numpy as np
from jax import lax

D = 1024
H = 16
DK = 64
FF = 2816
NB = 32
LEN = 256
ENC = 256
INNER = 1024
TOKENS = 4096
ENC_ALL = 4096
N_DP = 16
N_TENSOR = 2


def draw_bucket_index(key, part):
    distance = jnp.arange(LEN, dtype=jnp.int32)
    chance = jax.random.randint(key, (LEN,), 0, 1024, dtype=jnp.int32)
    threshold = jnp.where(distance < 16, 900, jnp.minimum(1024, 8192 // jnp.maximum(distance, 1)))
    increment = jnp.where((chance < threshold) & (distance > 0), 1, 0).astype(jnp.int32)
    bucket = jnp.minimum(jnp.cumsum(increment), NB - 1)
    return jnp.where(distance == LEN - 1, NB - 1, bucket).astype(jnp.int32)


def block_scale(own_key, extent, cuts, least, high):
    loudness, own = 1.0, jax.random.fold_in(own_key, 6)
    for axis_at, shards_of in cuts:
        draws = jnp.exp(jax.random.uniform(jax.random.fold_in(own, axis_at), (shards_of,), jnp.float32, least / len(cuts), high / len(cuts)))
        loudness = loudness * jnp.repeat(draws, extent[axis_at] // shards_of).reshape([-1 if axis == axis_at else 1 for axis in range(len(extent))])
    return loudness


def length_profile(amount, total, most, slope):
    weights = [(1 << 20) // math.isqrt(grade ** slope) + 1 for grade in range(2, amount + 1)]
    surplus, counts = total - most - (amount - 1), [1] * (amount - 1)
    while surplus > 0:
        free = [i for i in range(amount - 1) if counts[i] < most]
        mass, left = sum([weights[i] for i in free]), surplus
        for i in free:
            extra = min(most - counts[i], max(1, left * weights[i] // mass), surplus)
            counts[i] = counts[i] + extra
            surplus = surplus - extra
    return np.array([most] + counts)


def ragged_sizes(own_key, number_of, total, most, skew):
    if number_of == 2:
        one = jax.random.randint(own_key, (), max(1, total - most), min(most, total - 1) + 1)
        return jnp.stack([one, total - one])
    sizes = jnp.asarray(length_profile(number_of, total, most, skew), jnp.int32)
    pairs = (number_of - 1) // 2
    giver, sink = sizes[1:1 + 2 * pairs:2], sizes[2:2 + 2 * pairs:2]
    margin = jnp.minimum(giver - 1, most - sink)
    moved = jax.random.randint(jax.random.fold_in(own_key, 1), (pairs,), 0, 1 << 20) % (margin + 1)
    sizes = sizes.at[1:1 + 2 * pairs:2].set(giver - moved).at[2:2 + 2 * pairs:2].set(sink + moved)
    return sizes[jax.random.permutation(jax.random.fold_in(own_key, 2), number_of)]


def noise(rng, shape, spread, most, shards=(), held_as=jnp.bfloat16):
    drawn = jax.random.normal(rng, shape, jnp.float32) * spread
    if len(shards) > 0:
        drawn = block_scale(rng, shape, shards, -0.22, 0.18) * drawn
    return jnp.clip(drawn, min=-most, max=most).astype(held_as)


def setup_inputs(seed: int = 0) -> dict:
    key_list = jax.random.split(jax.random.key(seed), 22)
    return {
        "tokens": noise(key_list[0], (TOKENS, D), 1.0, 6.0, ((0, 16),)),
        "encoder_states": noise(key_list[1], (ENC_ALL, D), 1.0, 6.0, ((0, 16),)),
        "cotangent": noise(key_list[2], (TOKENS, D), 1.0, 6.0, ((0, 16),)),
        "lengths": ragged_sizes(key_list[3], N_DP, N_DP * LEN * 9 // 10, LEN, 1).astype(jnp.int32),
        "deal_order": jax.random.permutation(key_list[4], N_DP).astype(jnp.int32),
        "bucket_index": draw_bucket_index(jax.random.fold_in(key_list[21], 71), 0),
        "rel_table": noise(key_list[6], (NB, H), 1.0, 4.0, ((1, 2),), jnp.float32),
        "gain_self": jnp.clip(1.0 + 0.1 * jax.random.normal(key_list[7], (D,), jnp.float32), 0.5, 1.5),
        "self_query": noise(key_list[8], (D, INNER), (D * DK // 4) ** -0.5, 0.046875, ((0, 16), (1, 2))),
        "self_key": noise(key_list[9], (D, INNER), D ** -0.5, 0.1875, ((0, 16), (1, 2))),
        "self_value": noise(key_list[10], (D, INNER), D ** -0.5, 0.1875, ((0, 16), (1, 2))),
        "self_output": noise(key_list[11], (D, INNER), (INNER // 16) ** -0.5, 0.75, ((0, 16), (1, 2))),
        "gain_cross": jnp.clip(1.0 + 0.1 * jax.random.normal(key_list[12], (D,), jnp.float32), 0.5, 1.5),
        "cross_query": noise(key_list[13], (D, INNER), (D * DK // 4) ** -0.5, 0.046875, ((0, 16), (1, 2))),
        "cross_key": noise(key_list[14], (D, INNER), D ** -0.5, 0.1875, ((0, 16), (1, 2))),
        "cross_value": noise(key_list[15], (D, INNER), D ** -0.5, 0.1875, ((0, 16), (1, 2))),
        "cross_output": noise(key_list[16], (D, INNER), (INNER // 16) ** -0.5, 0.75, ((0, 16), (1, 2))),
        "gain_feed": jnp.clip(1.0 + 0.1 * jax.random.normal(key_list[17], (D,), jnp.float32), 0.5, 1.5),
        "feed_gate": noise(key_list[18], (D, FF), D ** -0.5, 0.1875, ((0, 16), (1, 2))),
        "feed_value": noise(key_list[19], (D, FF), D ** -0.5, 0.1875, ((0, 16), (1, 2))),
        "feed_output": noise(key_list[20], (D, FF), FF ** -0.5, 0.109375, ((0, 16), (1, 2))),
    }


EPSILON = 1e-06
MASKED = -1e+30
HIGHEST = lax.Precision.HIGHEST

@jax.custom_vjp
def low(v):
    return lax.optimization_barrier(v.astype(jnp.bfloat16)).astype(jnp.float32)

@jax.custom_vjp
def low_back(v):
    return v

def low_keep(v):
    return (low(v), None)

def low_pass(kept, grad):
    return (grad,)

def back_keep(v):
    return (v, None)

def back_low(kept, grad):
    return (low(grad),)
low.defvjp(low_keep, low_pass)
low_back.defvjp(back_keep, back_low)

def rounded_both(activation):
    return low_back(low(activation))

def rms_norm(activation, gain_in):
    return activation * lax.rsqrt(lax.optimization_barrier(jnp.mean(activation * activation, axis=-1, keepdims=True)) + EPSILON) * gain_in

def product(left, right):
    return jnp.dot(left, right, precision=HIGHEST)

def attention(query_in, key_in, value_in, extra_bias, allowed):
    row_count = query_in.shape[0]
    query_heads = query_in.reshape(row_count, H, DK)
    key_heads = key_in.reshape(key_in.shape[0], H, DK)
    value_heads = value_in.reshape(value_in.shape[0], H, DK)
    scores = low_back(jnp.einsum('qhe,khe->hqk', query_heads, key_heads, precision=HIGHEST) + extra_bias)
    scores = jnp.where(allowed, scores, MASKED)
    chance = low(jax.nn.softmax(scores, axis=-1))
    mixed_out = jnp.einsum('hqk,khe->qhe', chance, value_heads, precision=HIGHEST)
    return rounded_both(mixed_out.reshape(row_count, H * DK))

def project_out(mixed_in, weight):
    row_count = mixed_in.shape[0]
    partials = jnp.einsum('ltx,dtx->tld', mixed_in.reshape(row_count, N_TENSOR, -1), weight.reshape(weight.shape[0], N_TENSOR, -1), precision=HIGHEST)
    return low_back(lax.optimization_barrier(jnp.sum(low(partials), axis=0)))

def layer(source, memory, params, valid_rows, allowed, bucket_matrix):
    rel_table, gain_self, self_query, self_key, self_value, self_output, gain_cross, cross_query, cross_key, cross_value, cross_output, gain_feed, feed_gate, feed_value, feed_output = params
    masked_input = source * valid_rows
    normed_self = low(rms_norm(masked_input, gain_self))
    query_self = rounded_both(product(normed_self, self_query))
    key_self = rounded_both(product(normed_self, self_key))
    value_self = rounded_both(product(normed_self, self_value))
    bias_full = jnp.transpose(rel_table[bucket_matrix], (2, 0, 1))
    mixed_self = attention(query_self, key_self, value_self, bias_full, allowed[None])
    hidden_one = masked_input + project_out(mixed_self, self_output)
    normed_cross = low(rms_norm(hidden_one, gain_cross))
    query_cross = rounded_both(product(normed_cross, cross_query))
    key_cross = rounded_both(product(memory, cross_key))
    value_cross = rounded_both(product(memory, cross_value))
    mixed_cross = attention(query_cross, key_cross, value_cross, 0.0, True)
    hidden_two = hidden_one + project_out(mixed_cross, cross_output)
    normed_feed = low(rms_norm(hidden_two, gain_feed))
    gate_pre = low_back(product(normed_feed, feed_gate))
    lift_pre = low_back(product(normed_feed, feed_value))
    hidden_feed = rounded_both(jax.nn.gelu(gate_pre, approximate=True) * lift_pre)
    hidden_three = hidden_two + project_out(hidden_feed, feed_output)
    return hidden_three * valid_rows

def reference(tokens, encoder_states, cotangent, lengths, deal_order, bucket_index, rel_table, gain_self, self_query, self_key, self_value, self_output, gain_cross, cross_query, cross_key, cross_value, cross_output, gain_feed, feed_gate, feed_value, feed_output):
    params = tuple((item.astype(jnp.float32) for item in (rel_table, gain_self, self_query, self_key, self_value, self_output, gain_cross, cross_query, cross_key, cross_value, cross_output, gain_feed, feed_gate, feed_value, feed_output)))
    positions = jnp.arange(LEN, dtype=jnp.int32)
    distance = jnp.clip(positions[:, None] - positions[None, :], 0, LEN - 1).astype(jnp.int32)
    bucket_matrix = bucket_index[distance]
    causal = positions[None, :] <= positions[:, None]
    token_seq = tokens.reshape(N_DP, LEN, D)
    cotangent_seq = cotangent.reshape(N_DP, LEN, D)
    memory_seq = encoder_states.reshape(N_DP, ENC, D)

    def per_sequence(running, number):
        length = lengths[number]
        valid_rows = (positions < length).astype(jnp.float32)[:, None]
        allowed = causal & (positions[None, :] < length)
        source = token_seq[number].astype(jnp.float32)
        memory = memory_seq[deal_order[number]].astype(jnp.float32)

        def forward(source_in, memory_in, params_in):
            return layer(source_in, memory_in, params_in, valid_rows, allowed, bucket_matrix)
        result, pullback = jax.vjp(forward, source, memory, params)
        source_grad, memory_grad, param_grads = pullback(cotangent_seq[number].astype(jnp.float32))
        running = jax.tree.map(lambda running_sum, update: running_sum + update, running, param_grads)
        return (running, (result.astype(jnp.bfloat16), source_grad.astype(jnp.bfloat16), memory_grad.astype(jnp.bfloat16)))
    zero_grads = jax.tree.map(jnp.zeros_like, params)
    totals, (outputs, source_grads, memory_grads) = lax.scan(per_sequence, zero_grads, jnp.arange(N_DP, dtype=jnp.int32))
    placed = jnp.zeros_like(memory_grads).at[deal_order].set(memory_grads)
    return (outputs.reshape(N_DP * LEN, D), source_grads.reshape(N_DP * LEN, D), placed.reshape(N_DP * ENC, D), totals[0], totals[1], totals[2], totals[3], totals[4], totals[5], totals[6], totals[7], totals[8], totals[9], totals[10], totals[11], totals[12], totals[13], totals[14])
```

```python
import functools

import jax
import jax.numpy as jnp
import numpy as np
from jax import lax
from jax.experimental import pallas as pl
from jax.experimental.pallas import tpu as pltpu
from jax.sharding import PartitionSpec as P

EPSILON = 1e-06
MASKED = -1e30
HIGHEST = lax.Precision.HIGHEST
HEAD = 64
PAIR = 2 * HEAD


def exchange_masks(devices):
    width = devices.bit_length() - 1
    upper = [1 << bit for bit in range(width - 1, 1, -1)]
    if devices == 16:
        upper = [12, 4]
    lower = [mask for mask in (1, 2) if mask < devices]
    return {
        "a": upper + lower,
        "b": upper + lower[::-1],
        "z": lower + upper,
    }


def block_offsets(masks):
    offsets = [0]
    for mask in masks:
        offsets = offsets + [offset ^ mask for offset in offsets]
    return offsets


def swap_dp(value, mask, devices):
    return lax.ppermute(value, "dp", [(one, one ^ mask) for one in range(devices)])


def swap_tensor(value):
    return lax.ppermute(value, "tensor", [(0, 1), (1, 0)])


def reorder_blocks(value, from_masks, to_masks):
    before = block_offsets(from_masks)
    after = block_offsets(to_masks)
    rows = value.shape[0] // len(before)
    places = [before.index(offset) for offset in after]
    runs = []
    for place in places:
        if runs and runs[-1][1] == place:
            runs[-1][1] = place + 1
        else:
            runs.append([place, place + 1])
    if len(runs) == 1:
        return value
    return jnp.concatenate(
        [value[first * rows : last * rows] for first, last in runs], axis=0
    )


def gather_rows(value, masks, devices):
    for mask in masks:
        value = jnp.concatenate([value, swap_dp(value, mask, devices)], axis=0)
    return value


def reduce_rows(value, masks, devices):
    for mask in masks[::-1]:
        half = value.shape[0] // 2
        away = value[half:].astype(jnp.bfloat16)
        value = value[:half].astype(jnp.float32) + swap_dp(away, mask, devices).astype(
            jnp.float32
        )
    return value


def total_small(value, devices):
    mask = 1
    while mask < devices:
        value = value + swap_dp(value, mask, devices)
        mask = 2 * mask
    return value


def product_plain(left, right):
    return jnp.dot(left, right, preferred_element_type=jnp.float32)


def product_right(left, right):
    return lax.dot_general(
        left, right, (((1,), (1,)), ((), ())), preferred_element_type=jnp.float32
    )


def product_left(left, right):
    return lax.dot_general(
        left, right, (((0,), (0,)), ((), ())), preferred_element_type=jnp.float32
    )


def norm_forward(activation, gain_in):
    inv_root = lax.rsqrt(jnp.mean(activation * activation, axis=-1, keepdims=True) + EPSILON)
    return (activation * inv_root * gain_in, inv_root)


def norm_backward(activation, inv_root, gain_in, upstream):
    weighted = upstream * gain_in
    inner_mean = jnp.mean(weighted * activation, axis=-1, keepdims=True)
    grad_in = inv_root * weighted - activation * (inv_root * inv_root * inv_root) * inner_mean
    return (grad_in, jnp.sum(upstream * activation * inv_root, axis=0))


def toeplitz_bias(row, rows):
    wide = jnp.broadcast_to(row, (rows, row.shape[1]))
    return pltpu.roll(wide, 0, 1, stride=1, stride_axis=0)[:, :rows]


def head_half(value, side, lanes):
    keep = lanes < HEAD if side == 0 else lanes >= HEAD
    return jnp.where(keep, value, jnp.zeros_like(value))


def masked_scores(query, key, length_ref, bias_ref, head):
    scores = product_right(query, key)
    if bias_ref is None:
        return scores
    rows, columns = scores.shape
    scores = scores + toeplitz_bias(bias_ref[pl.ds(head, 1), :], rows)
    at_row = lax.broadcasted_iota(jnp.int32, (rows, columns), 0)
    at_column = lax.broadcasted_iota(jnp.int32, (rows, columns), 1)
    allowed = (at_column <= at_row) & (at_column < length_ref[0])
    return jnp.where(allowed, scores, MASKED)


def softmax_rows(scores):
    exponent = jnp.exp(scores - jnp.max(scores, axis=-1, keepdims=True))
    return exponent / jnp.sum(exponent, axis=-1, keepdims=True)


def attention_forward_body(biased, *refs):
    if biased:
        length_ref, bias_ref, query_ref, key_ref, value_ref, out_ref = refs
    else:
        query_ref, key_ref, value_ref, out_ref = refs
        length_ref = bias_ref = None
    rows, width = query_ref.shape
    lanes = lax.broadcasted_iota(jnp.int32, (rows, PAIR), 1)

    def one_pair(pair, carry):
        columns = pl.ds(pl.multiple_of(pair * PAIR, PAIR), PAIR)
        query, key, value = query_ref[:, columns], key_ref[:, columns], value_ref[:, columns]
        mixed = []
        for side in range(2):
            scores = masked_scores(
                head_half(query, side, lanes), key, length_ref, bias_ref, 2 * pair + side
            )
            chance = softmax_rows(scores).astype(jnp.bfloat16)
            mixed.append(product_plain(chance, value))
        out_ref[:, columns] = jnp.where(lanes < HEAD, mixed[0], mixed[1]).astype(jnp.bfloat16)
        return carry

    lax.fori_loop(0, width // PAIR, one_pair, 0)


def attention_backward_body(biased, *refs):
    if biased:
        (
            length_ref,
            bias_ref,
            query_ref,
            key_ref,
            value_ref,
            grad_ref,
            dquery_ref,
            dkey_ref,
            dvalue_ref,
            diagonal_ref,
        ) = refs
    else:
        query_ref, key_ref, value_ref, grad_ref, dquery_ref, dkey_ref, dvalue_ref = refs
        length_ref = bias_ref = diagonal_ref = None
    rows, width = query_ref.shape
    lanes = lax.broadcasted_iota(jnp.int32, (rows, PAIR), 1)
    if biased:
        flip = (
            lax.broadcasted_iota(jnp.int32, (rows, rows), 0)
            + lax.broadcasted_iota(jnp.int32, (rows, rows), 1)
            == rows - 1
        ).astype(jnp.bfloat16)

    def one_pair(pair, carry):
        columns = pl.ds(pl.multiple_of(pair * PAIR, PAIR), PAIR)
        query, key, value = query_ref[:, columns], key_ref[:, columns], value_ref[:, columns]
        grad = grad_ref[:, columns]
        dquery, dkey, dvalue = [], [], []
        for side in range(2):
            head = 2 * pair + side
            scores = masked_scores(
                head_half(query, side, lanes), key, length_ref, bias_ref, head
            )
            chance = softmax_rows(scores)
            chance_grad = product_right(head_half(grad, side, lanes), value)
            delta = jnp.sum(chance * chance_grad, axis=-1, keepdims=True)
            score_grad = (chance * (chance_grad - delta)).astype(jnp.bfloat16)
            dquery.append(product_plain(score_grad, key))
            dkey.append(product_left(score_grad, query))
            dvalue.append(product_left(chance.astype(jnp.bfloat16), grad))
            if biased:
                flipped = product_plain(flip, score_grad)
                wide = jnp.concatenate([flipped, jnp.zeros_like(flipped)], axis=1)
                skewed = pltpu.roll(wide, rows + 1, 1, stride=1, stride_axis=0)
                diagonal_ref[pl.ds(head, 1), :] = jnp.sum(skewed, axis=0, keepdims=True)
        left = lanes < HEAD
        dquery_ref[:, columns] = jnp.where(left, dquery[0], dquery[1]).astype(jnp.bfloat16)
        dkey_ref[:, columns] = jnp.where(left, dkey[0], dkey[1]).astype(jnp.bfloat16)
        dvalue_ref[:, columns] = jnp.where(left, dvalue[0], dvalue[1]).astype(jnp.bfloat16)
        return carry

    lax.fori_loop(0, width // PAIR, one_pair, 0)


def vmem():
    return pl.BlockSpec(memory_space=pltpu.VMEM)


def smem():
    return pl.BlockSpec(memory_space=pltpu.SMEM)


def attention_forward(query, key, value, length=None, bias=None):
    biased = bias is not None
    extra = (length, bias) if biased else ()
    specs = [smem(), vmem()] if biased else []
    return pl.pallas_call(
        functools.partial(attention_forward_body, biased),
        out_shape=jax.ShapeDtypeStruct(query.shape, jnp.bfloat16),
        in_specs=specs + [vmem()] * 3,
        out_specs=vmem(),
        compiler_params=pltpu.CompilerParams(vmem_limit_bytes=32 << 20),
    )(*extra, query, key, value)


def attention_backward(query, key, value, grad, length=None, bias=None):
    biased = bias is not None
    extra = (length, bias) if biased else ()
    specs = [smem(), vmem()] if biased else []
    out_shape = [jax.ShapeDtypeStruct(query.shape, jnp.bfloat16)] * 3
    if biased:
        out_shape = out_shape + [jax.ShapeDtypeStruct(bias.shape, jnp.float32)]
    return pl.pallas_call(
        functools.partial(attention_backward_body, biased),
        out_shape=out_shape,
        in_specs=specs + [vmem()] * 4,
        out_specs=[vmem()] * len(out_shape),
        compiler_params=pltpu.CompilerParams(vmem_limit_bytes=32 << 20),
    )(*extra, query, key, value, grad)


def gelu_product(gate_pre, lift_pre):
    return jax.nn.gelu(gate_pre, approximate=True) * lift_pre


def pair_total(partial_value):
    mine = partial_value.astype(jnp.bfloat16)
    return mine.astype(jnp.float32) + swap_tensor(mine).astype(jnp.float32)


def deal(value, order, devices):
    rows, width = value.shape
    first = lax.all_to_all(
        value.reshape(devices, rows // devices, width), "dp", split_axis=0, concat_axis=0, tiled=True
    )
    second = lax.all_to_all(
        jnp.take(first, order, axis=0), "dp", split_axis=0, concat_axis=0, tiled=True
    )
    return second.reshape(rows, width)


def on_device(
    tokens,
    encoder_states,
    cotangent,
    lengths,
    deal_order,
    bucket_index,
    rel_table,
    gain_self,
    self_query,
    self_key,
    self_value,
    self_output,
    gain_cross,
    cross_query,
    cross_key,
    cross_value,
    cross_output,
    gain_feed,
    feed_gate,
    feed_value,
    feed_output,
):
    devices = lax.axis_size("dp")
    myself = lax.axis_index("dp")
    core = lax.axis_index("tensor")
    length_all, model_width = tokens.shape
    block = model_width // devices
    buckets, head_count = rel_table.shape
    inner = self_query.shape[1]
    feed = feed_gate.shape[1]
    masks = exchange_masks(devices)
    order_a, order_b, order_z = masks["a"], masks["b"], masks["z"]

    numbers = jnp.arange(devices, dtype=jnp.int32)
    owner_of = jnp.sum(
        jnp.where(deal_order[:, None] == numbers[None, :], numbers[:, None], 0), axis=0
    )
    my_length = jnp.sum(jnp.where(numbers == myself, lengths, 0))
    length_ref = my_length.reshape(1)

    def gathered(parts, order):
        whole = gather_rows(jnp.concatenate(parts, axis=1), order, devices)
        return reorder_blocks(whole, order, order_a)

    low_qk = gathered((self_query, self_key), order_a)
    low_vo = gathered((self_value, self_output), order_b)
    cross_kv = gathered((cross_key, cross_value), order_a)
    cross_qo = gathered((cross_query, cross_output), order_b)
    gate_weight = gathered((feed_gate,), order_a)
    lift_weight = gathered((feed_value,), order_b)
    down_weight = gathered((feed_output,), order_z)
    query_weight, key_weight = low_qk[:, :inner], low_qk[:, inner:]
    value_weight, output_weight = low_vo[:, :inner], low_vo[:, inner:]
    cross_key_weight, cross_value_weight = cross_kv[:, :inner], cross_kv[:, inner:]
    cross_query_weight, cross_output_weight = cross_qo[:, :inner], cross_qo[:, inner:]

    offsets = jnp.asarray(np.array(block_offsets(order_a), np.int32))
    source_column = (
        ((myself ^ offsets) * block)[:, None] + jnp.arange(block, dtype=jnp.int32)[None, :]
    ).reshape(-1)
    columns = jnp.arange(model_width, dtype=jnp.int32)
    permute = (columns[:, None] == source_column[None, :]).astype(jnp.bfloat16)
    gains = jnp.dot(
        jnp.stack([gain_self, gain_cross, gain_feed]), permute.astype(jnp.float32), precision=HIGHEST
    )
    gain_self, gain_cross, gain_feed = gains[0], gains[1], gains[2]

    half = length_all // 2
    memory_half = deal(
        lax.dynamic_slice_in_dim(encoder_states, core * half, half, axis=0), deal_order, devices
    )
    memory = jnp.concatenate([memory_half, swap_tensor(memory_half)], axis=0)
    memory = product_plain(memory, permute).astype(jnp.bfloat16)

    positions = jnp.arange(length_all, dtype=jnp.int32)
    valid_rows = (positions < my_length).astype(jnp.float32)[:, None]
    skewed_bucket = jnp.concatenate(
        [
            bucket_index[:1],
            jnp.full((length_all,), -1, jnp.int32),
            bucket_index[::-1][: length_all - 1],
        ]
    )
    onehot_bucket = (
        jnp.arange(buckets, dtype=jnp.int32)[:, None] == skewed_bucket[None, :]
    ).astype(jnp.float32)
    bias_rows = jnp.dot(rel_table.T, onehot_bucket, precision=HIGHEST)

    masked_input = product_plain(tokens, permute) * valid_rows
    grad_three = product_plain(cotangent, permute) * valid_rows

    normed_self, root_self = norm_forward(masked_input, gain_self)
    normed_self_low = normed_self.astype(jnp.bfloat16)
    query_self = product_plain(normed_self_low, query_weight).astype(jnp.bfloat16)
    key_self = product_plain(normed_self_low, key_weight).astype(jnp.bfloat16)
    value_self = product_plain(normed_self_low, value_weight).astype(jnp.bfloat16)
    self_mixed_low = attention_forward(query_self, key_self, value_self, length_ref, bias_rows)
    hidden_one = masked_input + pair_total(product_right(self_mixed_low, output_weight))
    normed_cross, root_cross = norm_forward(hidden_one, gain_cross)
    normed_cross_low = normed_cross.astype(jnp.bfloat16)
    query_cross = product_plain(normed_cross_low, cross_query_weight).astype(jnp.bfloat16)
    key_cross = product_plain(memory, cross_key_weight).astype(jnp.bfloat16)
    value_cross = product_plain(memory, cross_value_weight).astype(jnp.bfloat16)
    cross_mixed_low = attention_forward(query_cross, key_cross, value_cross)
    hidden_two = hidden_one + pair_total(product_right(cross_mixed_low, cross_output_weight))
    normed_feed, root_feed = norm_forward(hidden_two, gain_feed)
    normed_feed_low = normed_feed.astype(jnp.bfloat16)
    gate_pre = product_plain(normed_feed_low, gate_weight)
    lift_pre = product_plain(normed_feed_low, lift_weight)
    hidden_low = gelu_product(gate_pre, lift_pre).astype(jnp.bfloat16)
    hidden_three = hidden_two + pair_total(product_right(hidden_low, down_weight))
    layer_result = (hidden_three * valid_rows).astype(jnp.bfloat16)
    layer_result = product_right(layer_result, permute).astype(jnp.bfloat16)

    def summed(grad, order):
        return reduce_rows(
            reorder_blocks(grad.astype(jnp.bfloat16), order_a, order), order, devices
        )

    branch_grad = grad_three.astype(jnp.bfloat16)
    hidden_grad = product_plain(branch_grad, down_weight).astype(jnp.bfloat16)
    gate_grad, lift_grad = jax.vjp(gelu_product, gate_pre, lift_pre)[1](
        hidden_grad.astype(jnp.float32)
    )
    gate_grad_low = gate_grad.astype(jnp.bfloat16)
    lift_grad_low = lift_grad.astype(jnp.bfloat16)
    down_sum = summed(product_left(branch_grad, hidden_low), order_z)
    gate_sum = summed(product_left(normed_feed_low, gate_grad_low), order_a)
    lift_sum = summed(product_left(normed_feed_low, lift_grad_low), order_b)
    feed_normed_grad = pair_total(
        product_right(gate_grad_low, gate_weight) + product_right(lift_grad_low, lift_weight)
    )
    back_feed, gain_feed_grad = norm_backward(hidden_two, root_feed, gain_feed, feed_normed_grad)
    grad_two = grad_three + back_feed
    branch_grad = grad_two.astype(jnp.bfloat16)
    mixed_grad = product_plain(branch_grad, cross_output_weight).astype(jnp.bfloat16)
    query_grad_low, key_grad_low, value_grad_low = attention_backward(
        query_cross, key_cross, value_cross, mixed_grad
    )
    kv_sum = summed(
        product_left(memory, jnp.concatenate([key_grad_low, value_grad_low], axis=1)), order_a
    )
    qo_sum = summed(
        jnp.concatenate(
            [
                product_left(normed_cross_low, query_grad_low),
                product_left(branch_grad, cross_mixed_low),
            ],
            axis=1,
        ),
        order_b,
    )
    encoder_partial = (
        product_right(key_grad_low, cross_key_weight)
        + product_right(value_grad_low, cross_value_weight)
    ).astype(jnp.bfloat16)
    encoder_half = (
        encoder_partial[:half].astype(jnp.float32)
        + swap_tensor(encoder_partial[half:]).astype(jnp.float32)
    ).astype(jnp.bfloat16)
    encoder_half = product_right(encoder_half, permute).astype(jnp.bfloat16)
    encoder_grad = deal(encoder_half, owner_of, devices)
    cross_normed_grad = pair_total(product_right(query_grad_low, cross_query_weight))
    back_cross, gain_cross_grad = norm_backward(
        hidden_one, root_cross, gain_cross, cross_normed_grad
    )
    grad_one = grad_two + back_cross
    branch_grad = grad_one.astype(jnp.bfloat16)
    mixed_grad = product_plain(branch_grad, output_weight).astype(jnp.bfloat16)
    query_grad_low, key_grad_low, value_grad_low, diagonal = attention_backward(
        query_self, key_self, value_self, mixed_grad, length_ref, bias_rows
    )
    table_grad = lax.dot_general(
        onehot_bucket, diagonal, (((1,), (1,)), ((), ())), precision=HIGHEST
    )
    low_qk_sum = summed(
        product_left(normed_self_low, jnp.concatenate([query_grad_low, key_grad_low], axis=1)),
        order_a,
    )
    low_vo_sum = summed(
        jnp.concatenate(
            [
                product_left(normed_self_low, value_grad_low),
                product_left(branch_grad, self_mixed_low),
            ],
            axis=1,
        ),
        order_b,
    )
    self_normed_grad = pair_total(
        product_right(query_grad_low, query_weight)
        + product_right(key_grad_low, key_weight)
        + product_right(value_grad_low, value_weight)
    )
    back_self, gain_self_grad = norm_backward(masked_input, root_self, gain_self, self_normed_grad)
    input_grad = ((grad_one + back_self) * valid_rows).astype(jnp.bfloat16)
    input_grad = product_right(input_grad, permute).astype(jnp.bfloat16)

    gain_grads = lax.dot_general(
        jnp.stack([gain_self_grad, gain_cross_grad, gain_feed_grad]),
        permute.astype(jnp.float32),
        (((1,), (1,)), ((), ())),
        precision=HIGHEST,
    )
    small = total_small(
        jnp.concatenate([gain_grads.reshape(-1), table_grad.reshape(-1)]).reshape(-1, 128), devices
    ).reshape(-1)
    gain_sums = small[: 3 * model_width].reshape(3, model_width)
    table_sum = small[3 * model_width :].reshape(buckets, head_count)
    return (
        layer_result,
        input_grad,
        encoder_grad,
        table_sum,
        gain_sums[0],
        low_qk_sum[:, :inner],
        low_qk_sum[:, inner:],
        low_vo_sum[:, :inner],
        low_vo_sum[:, inner:],
        gain_sums[1],
        qo_sum[:, :inner],
        kv_sum[:, :inner],
        kv_sum[:, inner:],
        qo_sum[:, inner:],
        gain_sums[2],
        gate_sum,
        lift_sum,
        down_sum,
    )


def solution(mesh):
    in_specs = (
        P("dp", None),
        P("dp", None),
        P("dp", None),
        P(),
        P(),
        P(),
        P(None, "tensor"),
        P(),
        P("dp", "tensor"),
        P("dp", "tensor"),
        P("dp", "tensor"),
        P("dp", "tensor"),
        P(),
        P("dp", "tensor"),
        P("dp", "tensor"),
        P("dp", "tensor"),
        P("dp", "tensor"),
        P(),
        P("dp", "tensor"),
        P("dp", "tensor"),
        P("dp", "tensor"),
    )
    out_specs = (
        P("dp", None),
        P("dp", None),
        P(("dp", "tensor"), None),
        P(None, "tensor"),
        P(),
        P("dp", "tensor"),
        P("dp", "tensor"),
        P("dp", "tensor"),
        P("dp", "tensor"),
        P(),
        P("dp", "tensor"),
        P("dp", "tensor"),
        P("dp", "tensor"),
        P("dp", "tensor"),
        P(),
        P("dp", "tensor"),
        P("dp", "tensor"),
        P("dp", "tensor"),
    )
    return jax.shard_map(
        on_device, mesh=mesh, in_specs=in_specs, out_specs=out_specs, check_vma=False
    )
```

```python
import functools

import jax
import jax.numpy as jnp
import numpy as np
from jax import lax
from jax.experimental import pallas as pl
from jax.experimental.pallas import tpu as pltpu
from jax.sharding import PartitionSpec as P

EPSILON = 1e-06
MASKED = -1e30
HIGHEST = lax.Precision.HIGHEST
HEAD = 64
PAIR = 2 * HEAD
LOW = jnp.bfloat16
FULL = jnp.float32


def upper_masks(devices):
    if devices == 16:
        return [12, 4]
    return [1 << bit for bit in range(devices.bit_length() - 2, 1, -1)]


def block_offsets(masks):
    offsets = [0]
    for mask in masks:
        offsets = offsets + [offset ^ mask for offset in offsets]
    return offsets


def swap_dp(value, mask, devices):
    return lax.ppermute(value, "dp", [(one, one ^ mask) for one in range(devices)])


def swap_tensor(value):
    return lax.ppermute(value, "tensor", [(0, 1), (1, 0)])


def total_small(value, devices):
    mask = 1
    while mask < devices:
        value = value + swap_dp(value, mask, devices)
        mask = 2 * mask
    return value


def product_plain(left, right):
    return jnp.dot(left, right, preferred_element_type=FULL)


def product_right(left, right):
    return lax.dot_general(left, right, (((1,), (1,)), ((), ())), preferred_element_type=FULL)


def product_left(left, right):
    return lax.dot_general(left, right, (((0,), (0,)), ((), ())), preferred_element_type=FULL)


def quarter(ref, number):
    width = ref.shape[1] // 4
    return ref[:, number * width : (number + 1) * width]


def project_in(value_ref, pieces, first, width):
    total = None
    for number, piece in enumerate(pieces):
        part = product_plain(quarter(value_ref, number), piece[:, first : first + width])
        total = part if total is None else total + part
    return total


def inverse_root(value):
    return lax.rsqrt(jnp.mean(value * value, axis=-1, keepdims=True) + EPSILON)


def norm_backward(value, gain, upstream):
    root = inverse_root(value)
    weighted = upstream * gain
    inner_mean = jnp.mean(weighted * value, axis=-1, keepdims=True)
    grad = root * weighted - value * (root * root * root) * inner_mean
    return grad, jnp.sum(upstream * value * root, axis=0, keepdims=True)


def both(mine_ref, other_ref):
    return mine_ref[...].astype(FULL) + other_ref[...].astype(FULL)


def valid_column(length_ref, rows):
    return (lax.broadcasted_iota(jnp.int32, (rows, 1), 0) < length_ref[0]).astype(FULL)


def toeplitz_bias(row, rows):
    wide = jnp.broadcast_to(row, (rows, row.shape[1]))
    return pltpu.roll(wide, 0, 1, stride=1, stride_axis=0)[:, :rows]


def head_half(value, side, lanes):
    keep = lanes < HEAD if side == 0 else lanes >= HEAD
    return jnp.where(keep, value, jnp.zeros_like(value))


def masked_scores(query, key, length_ref, bias_ref, head):
    scores = product_right(query, key)
    if bias_ref is None:
        return scores
    rows, columns = scores.shape
    scores = scores + toeplitz_bias(bias_ref[pl.ds(head, 1), :], rows)
    at_row = lax.broadcasted_iota(jnp.int32, (rows, columns), 0)
    at_column = lax.broadcasted_iota(jnp.int32, (rows, columns), 1)
    allowed = (at_column <= at_row) & (at_column < length_ref[0])
    return jnp.where(allowed, scores, MASKED)


def softmax_rows(scores):
    exponent = jnp.exp(scores - jnp.max(scores, axis=-1, keepdims=True))
    return exponent / jnp.sum(exponent, axis=-1, keepdims=True)


def attention_forward(query_ref, key_ref, value_ref, out_ref, length_ref=None, bias_ref=None):
    rows, width = query_ref.shape
    lanes = lax.broadcasted_iota(jnp.int32, (rows, PAIR), 1)

    def one_pair(pair, carry):
        columns = pl.ds(pl.multiple_of(pair * PAIR, PAIR), PAIR)
        query, key, value = query_ref[:, columns], key_ref[:, columns], value_ref[:, columns]
        mixed = []
        for side in range(2):
            scores = masked_scores(
                head_half(query, side, lanes), key, length_ref, bias_ref, 2 * pair + side
            )
            mixed.append(product_plain(softmax_rows(scores).astype(LOW), value))
        out_ref[:, columns] = jnp.where(lanes < HEAD, mixed[0], mixed[1]).astype(LOW)
        return carry

    lax.fori_loop(0, width // PAIR, one_pair, 0)


def attention_backward(
    query_ref,
    key_ref,
    value_ref,
    grad_ref,
    dquery_ref,
    dkey_ref,
    dvalue_ref,
    length_ref=None,
    bias_ref=None,
    diagonal_ref=None,
):
    rows, width = query_ref.shape
    lanes = lax.broadcasted_iota(jnp.int32, (rows, PAIR), 1)
    if bias_ref is not None:
        flip = (
            lax.broadcasted_iota(jnp.int32, (rows, rows), 0)
            + lax.broadcasted_iota(jnp.int32, (rows, rows), 1)
            == rows - 1
        ).astype(LOW)

    def one_pair(pair, carry):
        columns = pl.ds(pl.multiple_of(pair * PAIR, PAIR), PAIR)
        query, key, value = query_ref[:, columns], key_ref[:, columns], value_ref[:, columns]
        grad = grad_ref[:, columns]
        dquery, dkey, dvalue = [], [], []
        for side in range(2):
            head = 2 * pair + side
            scores = masked_scores(head_half(query, side, lanes), key, length_ref, bias_ref, head)
            chance = softmax_rows(scores)
            chance_grad = product_right(head_half(grad, side, lanes), value)
            delta = jnp.sum(chance * chance_grad, axis=-1, keepdims=True)
            score_grad = (chance * (chance_grad - delta)).astype(LOW)
            dquery.append(product_plain(score_grad, key))
            dkey.append(product_left(score_grad, query))
            dvalue.append(product_left(chance.astype(LOW), grad))
            if bias_ref is not None:
                flipped = product_plain(flip, score_grad)
                wide = jnp.concatenate([flipped, jnp.zeros_like(flipped)], axis=1)
                skewed = pltpu.roll(wide, rows + 1, 1, stride=1, stride_axis=0)
                diagonal_ref[pl.ds(head, 1), :] = jnp.sum(skewed, axis=0, keepdims=True)
        left = lanes < HEAD
        dquery_ref[:, columns] = jnp.where(left, dquery[0], dquery[1]).astype(LOW)
        dkey_ref[:, columns] = jnp.where(left, dkey[0], dkey[1]).astype(LOW)
        dvalue_ref[:, columns] = jnp.where(left, dvalue[0], dvalue[1]).astype(LOW)
        return carry

    lax.fori_loop(0, width // PAIR, one_pair, 0)


def low_shape(*shape):
    return jax.ShapeDtypeStruct(shape, LOW)


def full_shape(*shape):
    return jax.ShapeDtypeStruct(shape, FULL)


def call(body, out_shape, scalars, arrays, scratch=(), flops=0):
    vmem = pl.BlockSpec(memory_space=pltpu.VMEM)
    smem = pl.BlockSpec(memory_space=pltpu.SMEM)
    moved = sum(
        one.size * one.dtype.itemsize for one in list(arrays) + list(out_shape)
    )
    return pl.pallas_call(
        body,
        out_shape=list(out_shape),
        in_specs=[smem] * len(scalars) + [vmem] * len(arrays),
        out_specs=[vmem] * len(out_shape),
        scratch_shapes=list(scratch),
        cost_estimate=pl.CostEstimate(
            flops=int(flops), transcendentals=0, bytes_accessed=int(moved)
        ),
        compiler_params=pltpu.CompilerParams(vmem_limit_bytes=44 << 20),
    )(*scalars, *arrays)


def prepare_body(
    length_ref,
    tokens_ref,
    cotangent_ref,
    gains_ref,
    source_ref,
    permute_ref,
    input_ref,
    grad_ref,
    gains_out_ref,
    normed_ref,
):
    rows, width = tokens_ref.shape
    at_row = lax.broadcasted_iota(jnp.int32, (width, width), 0)
    permute_ref[...] = (at_row == source_ref[...]).astype(FULL).astype(LOW)
    permute = permute_ref[...]
    valid = valid_column(length_ref, rows)
    masked = product_plain(tokens_ref[...], permute) * valid
    input_ref[...] = masked.astype(LOW)
    grad_ref[...] = (product_plain(cotangent_ref[...], permute) * valid).astype(LOW)
    gains = gains_ref[...]
    high = gains.astype(LOW)
    middle = (gains - high.astype(FULL)).astype(LOW)
    low = (gains - high.astype(FULL) - middle.astype(FULL)).astype(LOW)
    gains_out_ref[...] = (
        product_plain(high, permute) + product_plain(middle, permute)
    ) + product_plain(low, permute)
    normed_ref[...] = (masked * inverse_root(masked) * gains_out_ref[0:1, :]).astype(LOW)


def self_forward_body(
    length_ref, bias_ref, normed_ref, *refs
):
    qk, vo = refs[:4], refs[4:8]
    query_ref, key_ref, value_ref, mixed_ref, partial_ref = refs[8:]
    inner = query_ref.shape[1]
    query_ref[...] = project_in(normed_ref, qk, 0, inner).astype(LOW)
    key_ref[...] = project_in(normed_ref, qk, inner, inner).astype(LOW)
    value_ref[...] = project_in(normed_ref, vo, 0, inner).astype(LOW)
    attention_forward(query_ref, key_ref, value_ref, mixed_ref, length_ref, bias_ref)
    width = partial_ref.shape[1] // 4
    for number in range(4):
        partial_ref[:, number * width : (number + 1) * width] = product_right(
            mixed_ref[...], vo[number][:, inner:]
        ).astype(LOW)


def memory_body(half_ref, other_ref, permute_ref, *refs):
    kv = refs[:4]
    memory_ref, key_ref, value_ref = refs[4:]
    inner = key_ref.shape[1]
    half = half_ref.shape[0]
    memory_ref[:half, :] = product_plain(half_ref[...], permute_ref[...]).astype(LOW)
    memory_ref[half:, :] = product_plain(other_ref[...], permute_ref[...]).astype(LOW)
    key_ref[...] = project_in(memory_ref, kv, 0, inner).astype(LOW)
    value_ref[...] = project_in(memory_ref, kv, inner, inner).astype(LOW)


def cross_forward_body(input_ref, mine_ref, other_ref, gains_ref, key_ref, value_ref, *refs):
    qo = refs[:4]
    hidden_ref, normed_ref, query_ref, mixed_ref, partial_ref = refs[4:]
    inner = query_ref.shape[1]
    hidden = input_ref[...].astype(FULL) + both(mine_ref, other_ref)
    hidden_ref[...] = hidden
    normed_ref[...] = (hidden * inverse_root(hidden) * gains_ref[1:2, :]).astype(LOW)
    query_ref[...] = project_in(normed_ref, qo, 0, inner).astype(LOW)
    attention_forward(query_ref, key_ref, value_ref, mixed_ref)
    width = partial_ref.shape[1] // 4
    for number in range(4):
        partial_ref[:, number * width : (number + 1) * width] = product_right(
            mixed_ref[...], qo[number][:, inner:]
        ).astype(LOW)


GELU_SCALE = float(np.sqrt(2.0 / np.pi))
GELU_CUBE = 0.044715


def feed_body(transposed, hidden_in_ref, mine_ref, other_ref, gains_ref, grad_ref, *refs):
    gate_w, lift_w, down_w = refs[:4], refs[4:8], refs[8:12]
    hidden_ref, partial_ref, dnormed_ref = refs[12:15]
    dgate_w, dlift_w, ddown_w = refs[15:19], refs[19:23], refs[23:27]
    normed_ref, normed_t_ref, grad_t_ref, down_ref, total_ref, dtotal_ref = refs[27:]
    rows, model = hidden_ref.shape
    width = model // 4
    block = width // 4
    feed = gate_w[0].shape[1]
    hidden = hidden_in_ref[...] + both(mine_ref, other_ref)
    hidden_ref[...] = hidden
    normed_ref[...] = (hidden * inverse_root(hidden) * gains_ref[2:3, :]).astype(LOW)
    normed_t_ref[...] = normed_ref[...].T
    grad_t_ref[...] = grad_ref[...].T
    for number in range(4):
        if transposed:
            for other in range(4):
                place = number * width + other * block
                down_ref[place : place + block, :] = down_w[other][
                    number * block : (number + 1) * block, :
                ]
        else:
            down_ref[number * width : (number + 1) * width, :] = down_w[number][...]
    first = 0
    while first < feed:
        last = min(first + 512, feed)
        gate = project_in(normed_ref, gate_w, first, last - first)
        lift = project_in(normed_ref, lift_w, first, last - first)
        squared = gate * gate
        curve = jnp.tanh(GELU_SCALE * (gate + GELU_CUBE * squared * gate))
        half_up = 0.5 * (1.0 + curve)
        activated = gate * half_up
        product = (activated * lift).astype(LOW)
        down = down_ref[:, first:last]
        forward = product_right(product, down)
        dproduct = product_plain(grad_ref[...], down).astype(LOW).astype(FULL)
        slope = half_up + 0.5 * gate * (1.0 - curve * curve) * (
            GELU_SCALE * (1.0 + 3.0 * GELU_CUBE * squared)
        )
        dgate = (dproduct * lift * slope).astype(LOW)
        dlift = (dproduct * activated).astype(LOW)
        for number in range(4):
            part = slice(number * width, (number + 1) * width)
            dgate_w[number][:, first:last] = product_plain(normed_t_ref[part, :], dgate).astype(
                LOW
            )
            dlift_w[number][:, first:last] = product_plain(normed_t_ref[part, :], dlift).astype(
                LOW
            )
            ddown = product_plain(grad_t_ref[part, :], product).astype(LOW)
            if transposed:
                for other in range(4):
                    ddown_w[other][number * block : (number + 1) * block, first:last] = ddown[
                        other * block : (other + 1) * block, :
                    ]
            else:
                ddown_w[number][:, first:last] = ddown
            back = product_right(dgate, gate_w[number][:, first:last]) + product_right(
                dlift, lift_w[number][:, first:last]
            )
            if first == 0:
                dtotal_ref[:, part] = back
            else:
                dtotal_ref[:, part] += back
        if first == 0:
            total_ref[...] = forward
        else:
            total_ref[...] += forward
        first = last
    partial_ref[...] = total_ref[...].astype(LOW)
    dnormed_ref[...] = dtotal_ref[...].astype(LOW)


def cross_backward_body(
    hidden_ref,
    mine_ref,
    other_ref,
    gains_ref,
    grad_ref,
    normed_ref,
    memory_ref,
    query_ref,
    key_ref,
    value_ref,
    mixed_ref,
    *refs,
):
    kv, qo = refs[:4], refs[4:8]
    grad_out_ref, dgain_ref, dnormed_ref, keep_ref, away_ref = refs[8:13]
    dkv, dqo = refs[13:17], refs[17:21]
    low_ref, transposed_ref, dmixed_ref, dquery_ref, dkey_ref, dvalue_ref = refs[21:]
    rows, model = hidden_ref.shape
    width = model // 4
    inner = query_ref.shape[1]
    half = rows // 2
    back, dgain_ref[...] = norm_backward(
        hidden_ref[...], gains_ref[2:3, :], both(mine_ref, other_ref)
    )
    grad = grad_ref[...].astype(FULL) + back
    grad_out_ref[...] = grad
    low_ref[...] = grad.astype(LOW)
    dmixed_ref[...] = project_in(low_ref, qo_columns(qo, inner), 0, inner).astype(LOW)
    attention_backward(
        query_ref, key_ref, value_ref, dmixed_ref, dquery_ref, dkey_ref, dvalue_ref
    )
    for number in range(4):
        part = slice(number * width, (number + 1) * width)
        dnormed_ref[:, part] = product_right(dquery_ref[...], qo[number][:, :inner]).astype(LOW)
        partial = (
            product_right(dkey_ref[...], kv[number][:, :inner])
            + product_right(dvalue_ref[...], kv[number][:, inner:])
        ).astype(LOW)
        keep_ref[:, part] = partial[:half]
        away_ref[:, part] = partial[half:]
    transposed_ref[...] = memory_ref[...].T
    for number in range(4):
        part = slice(number * width, (number + 1) * width)
        dkv[number][:, :inner] = product_plain(transposed_ref[part, :], dkey_ref[...]).astype(LOW)
        dkv[number][:, inner:] = product_plain(transposed_ref[part, :], dvalue_ref[...]).astype(
            LOW
        )
    transposed_ref[...] = normed_ref[...].T
    for number in range(4):
        part = slice(number * width, (number + 1) * width)
        dqo[number][:, :inner] = product_plain(transposed_ref[part, :], dquery_ref[...]).astype(
            LOW
        )
    transposed_ref[...] = low_ref[...].T
    for number in range(4):
        part = slice(number * width, (number + 1) * width)
        dqo[number][:, inner:] = product_plain(transposed_ref[part, :], mixed_ref[...]).astype(LOW)


def qo_columns(pieces, first):
    return [piece.at[:, first:] for piece in pieces]


def self_backward_body(
    length_ref,
    bias_ref,
    hidden_ref,
    mine_ref,
    other_ref,
    gains_ref,
    grad_ref,
    normed_ref,
    query_ref,
    key_ref,
    value_ref,
    mixed_ref,
    *refs,
):
    qk, vo = refs[:4], refs[4:8]
    grad_out_ref, dgain_ref, dnormed_ref, diagonal_ref = refs[8:12]
    dqk, dvo = refs[12:16], refs[16:20]
    low_ref, transposed_ref, dmixed_ref, dquery_ref, dkey_ref, dvalue_ref = refs[20:]
    rows, model = hidden_ref.shape
    width = model // 4
    inner = query_ref.shape[1]
    back, dgain_ref[...] = norm_backward(
        hidden_ref[...], gains_ref[1:2, :], both(mine_ref, other_ref)
    )
    grad = grad_ref[...] + back
    grad_out_ref[...] = grad
    low_ref[...] = grad.astype(LOW)
    dmixed_ref[...] = project_in(low_ref, qo_columns(vo, inner), 0, inner).astype(LOW)
    attention_backward(
        query_ref,
        key_ref,
        value_ref,
        dmixed_ref,
        dquery_ref,
        dkey_ref,
        dvalue_ref,
        length_ref,
        bias_ref,
        diagonal_ref,
    )
    for number in range(4):
        part = slice(number * width, (number + 1) * width)
        dnormed_ref[:, part] = (
            product_right(dquery_ref[...], qk[number][:, :inner])
            + product_right(dkey_ref[...], qk[number][:, inner:])
            + product_right(dvalue_ref[...], vo[number][:, :inner])
        ).astype(LOW)
    transposed_ref[...] = normed_ref[...].T
    for number in range(4):
        part = slice(number * width, (number + 1) * width)
        dqk[number][:, :inner] = product_plain(transposed_ref[part, :], dquery_ref[...]).astype(
            LOW
        )
        dqk[number][:, inner:] = product_plain(transposed_ref[part, :], dkey_ref[...]).astype(LOW)
        dvo[number][:, :inner] = product_plain(transposed_ref[part, :], dvalue_ref[...]).astype(
            LOW
        )
    transposed_ref[...] = low_ref[...].T
    for number in range(4):
        part = slice(number * width, (number + 1) * width)
        dvo[number][:, inner:] = product_plain(transposed_ref[part, :], mixed_ref[...]).astype(LOW)


def finish_body(
    length_ref,
    permute_ref,
    input_ref,
    mine_ref,
    other_ref,
    gains_ref,
    grad_ref,
    dgain_cross_ref,
    dgain_feed_ref,
    onehot_ref,
    diagonal_ref,
    out_ref,
    dgains_ref,
    table_ref,
):
    rows = input_ref.shape[0]
    permute = permute_ref[...]
    back, dgain = norm_backward(
        input_ref[...].astype(FULL), gains_ref[0:1, :], both(mine_ref, other_ref)
    )
    total = ((grad_ref[...] + back) * valid_column(length_ref, rows)).astype(LOW)
    out_ref[...] = product_right(total, permute).astype(LOW)
    dgains = jnp.concatenate([dgain, dgain_cross_ref[...], dgain_feed_ref[...]], axis=0)
    high = dgains.astype(LOW)
    middle = (dgains - high.astype(FULL)).astype(LOW)
    low = (dgains - high.astype(FULL) - middle.astype(FULL)).astype(LOW)
    dgains_ref[...] = (
        product_right(high, permute) + product_right(middle, permute)
    ) + product_right(low, permute)
    table_ref[...] = lax.dot_general(
        onehot_ref[...],
        diagonal_ref[...],
        (((1,), (1,)), ((), ())),
        precision=HIGHEST,
        preferred_element_type=FULL,
    )


def output_body(length_ref, permute_ref, hidden_ref, mine_ref, other_ref, out_ref):
    rows = hidden_ref.shape[0]
    total = (hidden_ref[...] + both(mine_ref, other_ref)) * valid_column(length_ref, rows)
    out_ref[...] = product_right(total.astype(LOW), permute_ref[...]).astype(LOW)


def encoder_body(permute_ref, mine_ref, other_ref, out_ref):
    total = both(mine_ref, other_ref).astype(LOW)
    out_ref[...] = product_right(total, permute_ref[...]).astype(LOW)


def fold_body(count, *refs):
    terms, outs = refs[: 3 * count], refs[3 * count :]
    first = 0
    block = terms[0].shape[0] // 4
    for number in range(count):
        own, one, two = terms[3 * number : 3 * number + 3]
        last = first + own.shape[1]
        for place in range(4):
            rows = slice(place * block, (place + 1) * block)
            total = (
                own[rows, :].astype(FULL) + one[rows, :].astype(FULL) + two[rows, :].astype(FULL)
            )
            outs[place][:, first:last] = total.astype(outs[place].dtype)
        first = last


def fold_quarter(groups):
    count = len(groups)
    rows = groups[0][0].shape[0] // 4
    width = sum(group[0].shape[1] for group in groups)
    out_shape = [
        full_shape(rows, width),
        full_shape(rows, width),
        low_shape(rows, width),
        low_shape(rows, width),
    ]
    return call(
        functools.partial(fold_body, count),
        out_shape,
        (),
        [one for group in groups for one in group],
    )


def stack_body(count, *refs):
    parts, outs = refs[:4], refs[4:]
    block = parts[0].shape[0]
    first = 0
    for number in range(count):
        last = first + outs[number].shape[1]
        for place in range(4):
            outs[number][place * block : (place + 1) * block, :] = parts[place][:, first:last]
        first = last


def stack_quarter(parts, widths):
    rows = 4 * parts[0].shape[0]
    return call(
        functools.partial(stack_body, len(widths)),
        [low_shape(rows, width) for width in widths],
        (),
        parts,
    )


def gather_upper(value, widths, devices):
    masks = upper_masks(devices)
    if len(masks) == 2:
        one = swap_dp(value, masks[0], devices)
        two = swap_dp(value, masks[1], devices)
        three = swap_dp(one, masks[1], devices)
        return stack_quarter([value, one, two, three], widths)
    for mask in masks:
        value = jnp.concatenate([value, swap_dp(value, mask, devices)], axis=0)
    parts, first = [], 0
    for width in widths:
        parts.append(value[:, first : first + width])
        first += width
    return parts


def gather_lower(first, masks, devices):
    pair = {1: swap_dp(first, 1, devices), 2: swap_dp(first, 2, devices)}
    last = swap_dp(pair[masks[0]], masks[1], devices)
    return [first, pair[1], pair[2], last]


def gather_group(parts, devices):
    value = jnp.concatenate(parts[0] + parts[1], axis=1)
    widths = [sum(one.shape[1] for one in part) for part in parts]
    left, right = gather_upper(value, widths, devices)
    return gather_lower(left, (1, 2), devices), gather_lower(right, (2, 1), devices)


def reduce_lower(pieces, masks, devices):
    first, x_part, y_part, last = pieces
    parts = {1: x_part, 2: y_part}
    came = swap_dp(last, masks[1], devices)
    through = (parts[masks[0]].astype(FULL) + came.astype(FULL)).astype(LOW)
    return [
        first,
        swap_dp(parts[masks[1]], masks[1], devices),
        swap_dp(through, masks[0], devices),
    ]


def reduce_upper(groups, devices):
    masks = upper_masks(devices)
    if len(masks) == 2:
        own, one, two, three = fold_quarter(groups)
        one = (one + swap_dp(three, masks[1], devices).astype(FULL)).astype(LOW)
        two = swap_dp(two, masks[1], devices)
        return own + two.astype(FULL) + swap_dp(one, masks[0], devices).astype(FULL)
    value = jnp.concatenate(
        [sum(one.astype(FULL) for one in group) for group in groups], axis=1
    )
    for mask in masks[::-1]:
        half = value.shape[0] // 2
        away = swap_dp(value[half:].astype(LOW), mask, devices)
        value = value[:half] + away.astype(FULL)
    return value


def gather_across(value, devices):
    masks = upper_masks(devices)
    x_part, y_part = swap_dp(value, 1, devices), swap_dp(value, 2, devices)
    last = swap_dp(x_part, 2, devices)
    (first,) = stack_quarter([value, x_part, y_part, last], [value.shape[1]])
    one, two = swap_dp(first, masks[0], devices), swap_dp(first, masks[1], devices)
    return [first, one, two, swap_dp(one, masks[1], devices)]


def reduce_across(pieces, devices):
    masks = upper_masks(devices)
    first, one, two, last = pieces
    one = (one.astype(FULL) + swap_dp(last, masks[1], devices).astype(FULL)).astype(LOW)
    group = [first, swap_dp(two, masks[1], devices), swap_dp(one, masks[0], devices)]
    own, x_part, y_part, last = fold_quarter([group])
    x_part = (x_part + swap_dp(last, 2, devices).astype(FULL)).astype(LOW)
    return (
        own
        + swap_dp(y_part, 2, devices).astype(FULL)
        + swap_dp(x_part, 1, devices).astype(FULL)
    )


def deal(value, order, devices):
    rows, width = value.shape
    first = lax.all_to_all(
        value.reshape(devices, rows // devices, width), "dp", split_axis=0, concat_axis=0, tiled=True
    )
    second = lax.all_to_all(
        jnp.take(first, order, axis=0), "dp", split_axis=0, concat_axis=0, tiled=True
    )
    return second.reshape(rows, width)


def on_device(
    tokens,
    encoder_states,
    cotangent,
    lengths,
    deal_order,
    bucket_index,
    rel_table,
    gain_self,
    self_query,
    self_key,
    self_value,
    self_output,
    gain_cross,
    cross_query,
    cross_key,
    cross_value,
    cross_output,
    gain_feed,
    feed_gate,
    feed_value,
    feed_output,
):
    devices = lax.axis_size("dp")
    myself = lax.axis_index("dp")
    core = lax.axis_index("tensor")
    rows, model = tokens.shape
    block = model // devices
    buckets, heads = rel_table.shape
    inner = self_query.shape[1]
    feed = feed_gate.shape[1]
    across = devices == 16

    numbers = jnp.arange(devices, dtype=jnp.int32)
    owner_of = jnp.sum(
        jnp.where(deal_order[:, None] == numbers[None, :], numbers[:, None], 0), axis=0
    )
    length = jnp.sum(jnp.where(numbers == myself, lengths, 0)).reshape(1)

    qk, vo = gather_group(([self_query, self_key], [self_value, self_output]), devices)
    kv, qo = gather_group(([cross_key, cross_value], [cross_query, cross_output]), devices)
    if across:
        down = gather_across(feed_output, devices)
        gate, lift = gather_group(([feed_gate], [feed_value]), devices)
    else:
        gate, lift = gather_group(([feed_gate], [feed_value]), devices)
        (down,) = gather_upper(feed_output, [feed], devices)
        down = gather_lower(down, (1, 2), devices)

    offsets = jnp.asarray(np.array(block_offsets(upper_masks(devices) + [1, 2]), np.int32))
    source = (
        ((myself ^ offsets) * block)[:, None] + jnp.arange(block, dtype=jnp.int32)[None, :]
    ).reshape(1, -1)
    permute, masked_input, grad_three, gains, normed_self = call(
        prepare_body,
        [
            low_shape(model, model),
            low_shape(rows, model),
            low_shape(rows, model),
            full_shape(3, model),
            low_shape(rows, model),
        ],
        (length,),
        (tokens, cotangent, jnp.stack([gain_self, gain_cross, gain_feed]), source),
        flops=4 * rows * model * model,
    )

    half = rows // 2
    memory_half = deal(
        lax.dynamic_slice_in_dim(encoder_states, core * half, half, axis=0), deal_order, devices
    )
    memory_other = swap_tensor(memory_half)

    skewed_bucket = jnp.concatenate(
        [bucket_index[:1], jnp.full((rows,), -1, jnp.int32), bucket_index[::-1][: rows - 1]]
    )
    onehot = (jnp.arange(buckets, dtype=jnp.int32)[:, None] == skewed_bucket[None, :]).astype(FULL)
    bias_rows = jnp.dot(rel_table.T, onehot, precision=HIGHEST)

    unit = 2 * rows * model * inner
    query_self, key_self, value_self, mixed_self, partial = call(
        self_forward_body,
        [low_shape(rows, inner)] * 4 + [low_shape(rows, model)],
        (length,),
        (bias_rows, normed_self, *qk, *vo),
        flops=5 * unit,
    )
    memory, key_cross, value_cross = call(
        memory_body,
        [low_shape(rows, model)] + [low_shape(rows, inner)] * 2,
        (),
        (memory_half, memory_other, permute, *kv),
        flops=4 * unit,
    )
    hidden_one, normed_cross, query_cross, mixed_cross, partial = call(
        cross_forward_body,
        [full_shape(rows, model), low_shape(rows, model)]
        + [low_shape(rows, inner)] * 2
        + [low_shape(rows, model)],
        (),
        (masked_input, partial, swap_tensor(partial), gains, key_cross, value_cross, *qo),
        flops=3 * unit,
    )
    quarter_rows = model // 4
    feed_grads = [low_shape(quarter_rows, feed)] * 12
    outs = call(
        functools.partial(feed_body, across),
        [full_shape(rows, model), low_shape(rows, model), low_shape(rows, model)] + feed_grads,
        (),
        (hidden_one, partial, swap_tensor(partial), gains, grad_three, *gate, *lift, *down),
        scratch=[
            pltpu.VMEM((rows, model), LOW),
            pltpu.VMEM((model, rows), LOW),
            pltpu.VMEM((model, rows), LOW),
            pltpu.VMEM((model, feed), LOW),
            pltpu.VMEM((rows, model), FULL),
            pltpu.VMEM((rows, model), FULL),
        ],
        flops=18 * rows * model * feed,
    )
    hidden_two, partial, dpartial = outs[:3]
    dgate, dlift, ddown = outs[3:7], outs[7:11], outs[11:15]
    (layer_result,) = call(
        output_body,
        [low_shape(rows, model)],
        (length,),
        (permute, hidden_two, partial, swap_tensor(partial)),
        flops=2 * unit,
    )

    attention_scratch = [
        pltpu.VMEM((rows, model), LOW),
        pltpu.VMEM((model, rows), LOW),
    ] + [pltpu.VMEM((rows, inner), LOW)] * 4
    outs = call(
        cross_backward_body,
        [
            full_shape(rows, model),
            full_shape(1, model),
            low_shape(rows, model),
            low_shape(half, model),
            low_shape(half, model),
        ]
        + [low_shape(quarter_rows, 2 * inner)] * 8,
        (),
        (
            hidden_two,
            dpartial,
            swap_tensor(dpartial),
            gains,
            grad_three,
            normed_cross,
            memory,
            query_cross,
            key_cross,
            value_cross,
            mixed_cross,
            *kv,
            *qo,
        ),
        scratch=attention_scratch,
        flops=9 * unit,
    )
    grad_two, dgain_feed, dpartial, keep, away = outs[:5]
    dkv, dqo = outs[5:9], outs[9:13]
    (encoder_half,) = call(
        encoder_body,
        [low_shape(half, model)],
        (),
        (permute, keep, swap_tensor(away)),
        flops=unit,
    )
    encoder_grad = deal(encoder_half, owner_of, devices)

    outs = call(
        self_backward_body,
        [
            full_shape(rows, model),
            full_shape(1, model),
            low_shape(rows, model),
            full_shape(heads, 2 * rows),
        ]
        + [low_shape(quarter_rows, 2 * inner)] * 8,
        (length,),
        (
            bias_rows,
            hidden_one,
            dpartial,
            swap_tensor(dpartial),
            gains,
            grad_two,
            normed_self,
            query_self,
            key_self,
            value_self,
            mixed_self,
            *qk,
            *vo,
        ),
        scratch=attention_scratch,
        flops=10 * unit,
    )
    grad_one, dgain_cross, dpartial, diagonal = outs[:4]
    dqk, dvo = outs[4:8], outs[8:12]
    input_grad, dgains, dtable = call(
        finish_body,
        [low_shape(rows, model), full_shape(3, model), full_shape(buckets, heads)],
        (length,),
        (
            permute,
            masked_input,
            dpartial,
            swap_tensor(dpartial),
            gains,
            grad_one,
            dgain_cross,
            dgain_feed,
            onehot,
            diagonal,
        ),
        flops=2 * unit,
    )

    gate_terms = reduce_lower(dgate, (1, 2), devices)
    lift_terms = reduce_lower(dlift, (2, 1), devices)
    if across:
        feed_sums = reduce_upper([gate_terms, lift_terms], devices)
        down_sum = reduce_across(ddown, devices)
    else:
        down_terms = reduce_lower(ddown, (1, 2), devices)
        feed_sums = reduce_upper([gate_terms, lift_terms], devices)
        down_sum = reduce_upper([down_terms], devices)
    cross_sums = reduce_upper(
        [reduce_lower(dkv, (1, 2), devices), reduce_lower(dqo, (2, 1), devices)], devices
    )
    self_sums = reduce_upper(
        [reduce_lower(dqk, (1, 2), devices), reduce_lower(dvo, (2, 1), devices)], devices
    )
    small = total_small(
        jnp.concatenate([dgains.reshape(-1), dtable.reshape(-1)]).reshape(-1, 128), devices
    ).reshape(-1)
    gain_sums = small[: 3 * model].reshape(3, model)
    table_sum = small[3 * model :].reshape(buckets, heads)

    def column(value, number, width):
        return value[:, number * width : (number + 1) * width]

    return (
        layer_result,
        input_grad,
        encoder_grad,
        table_sum,
        gain_sums[0],
        column(self_sums, 0, inner),
        column(self_sums, 1, inner),
        column(self_sums, 2, inner),
        column(self_sums, 3, inner),
        gain_sums[1],
        column(cross_sums, 2, inner),
        column(cross_sums, 0, inner),
        column(cross_sums, 1, inner),
        column(cross_sums, 3, inner),
        gain_sums[2],
        column(feed_sums, 0, feed),
        column(feed_sums, 1, feed),
        down_sum,
    )


def solution(mesh):
    in_specs = (
        P("dp", None),
        P("dp", None),
        P("dp", None),
        P(),
        P(),
        P(),
        P(None, "tensor"),
        P(),
        P("dp", "tensor"),
        P("dp", "tensor"),
        P("dp", "tensor"),
        P("dp", "tensor"),
        P(),
        P("dp", "tensor"),
        P("dp", "tensor"),
        P("dp", "tensor"),
        P("dp", "tensor"),
        P(),
        P("dp", "tensor"),
        P("dp", "tensor"),
        P("dp", "tensor"),
    )
    out_specs = (
        P("dp", None),
        P("dp", None),
        P(("dp", "tensor"), None),
        P(None, "tensor"),
        P(),
        P("dp", "tensor"),
        P("dp", "tensor"),
        P("dp", "tensor"),
        P("dp", "tensor"),
        P(),
        P("dp", "tensor"),
        P("dp", "tensor"),
        P("dp", "tensor"),
        P("dp", "tensor"),
        P(),
        P("dp", "tensor"),
        P("dp", "tensor"),
        P("dp", "tensor"),
    )
    return jax.shard_map(
        on_device, mesh=mesh, in_specs=in_specs, out_specs=out_specs, check_vma=False
    )
```

```python
import functools

import jax
import jax.numpy as jnp
import numpy as np
from jax import lax
from jax.experimental import pallas as pl
from jax.experimental.pallas import tpu as pltpu
from jax.sharding import PartitionSpec as P

EPSILON = 1e-06
MASKED = -1e30
HIGHEST = lax.Precision.HIGHEST
HEAD = 64
PAIR = 2 * HEAD
LOW = jnp.bfloat16
FULL = jnp.float32


def upper_masks(devices):
    if devices == 16:
        return [12, 4]
    return [1 << bit for bit in range(devices.bit_length() - 2, 1, -1)]


def block_offsets(masks):
    offsets = [0]
    for mask in masks:
        offsets = offsets + [offset ^ mask for offset in offsets]
    return offsets


def swap_dp(value, mask, devices):
    return lax.ppermute(value, "dp", [(one, one ^ mask) for one in range(devices)])


def swap_tensor(value):
    return lax.ppermute(value, "tensor", [(0, 1), (1, 0)])


def total_small(value, devices):
    mask = 1
    while mask < devices:
        value = value + swap_dp(value, mask, devices)
        mask = 2 * mask
    return value


def product_plain(left, right):
    return jnp.dot(left, right, preferred_element_type=FULL)


def product_right(left, right):
    return lax.dot_general(left, right, (((1,), (1,)), ((), ())), preferred_element_type=FULL)


def product_left(left, right):
    return lax.dot_general(left, right, (((0,), (0,)), ((), ())), preferred_element_type=FULL)


def quarter(ref, number):
    width = ref.shape[1] // 4
    return ref[:, number * width : (number + 1) * width]


def sides(refs):
    own, x_part, y_part, left, right = refs
    rows = left.shape[0]
    return (
        [own.at[:rows], x_part.at[:rows], y_part.at[:rows], left],
        [own.at[rows:], x_part.at[rows:], y_part.at[rows:], right],
    )


def after(value, *earlier):
    return lax.optimization_barrier((value, *earlier))[0]


def project_in(value_ref, pieces, first, width):
    total = None
    for number, piece in enumerate(pieces):
        part = product_plain(quarter(value_ref, number), piece[:, first : first + width])
        total = part if total is None else total + part
    return total


def inverse_root(value):
    return lax.rsqrt(jnp.mean(value * value, axis=-1, keepdims=True) + EPSILON)


def norm_backward(value, gain, upstream):
    root = inverse_root(value)
    weighted = upstream * gain
    inner_mean = jnp.mean(weighted * value, axis=-1, keepdims=True)
    grad = root * weighted - value * (root * root * root) * inner_mean
    return grad, jnp.sum(upstream * value * root, axis=0, keepdims=True)


def both(mine_ref, other_ref):
    return mine_ref[...].astype(FULL) + other_ref[...].astype(FULL)


def valid_column(length_ref, rows):
    return (lax.broadcasted_iota(jnp.int32, (rows, 1), 0) < length_ref[0]).astype(FULL)


def toeplitz_bias(row, rows):
    wide = jnp.broadcast_to(row, (rows, row.shape[1]))
    return pltpu.roll(wide, 0, 1, stride=1, stride_axis=0)[:, :rows]


def head_half(value, side, lanes):
    keep = lanes < HEAD if side == 0 else lanes >= HEAD
    return jnp.where(keep, value, jnp.zeros_like(value))


def masked_scores(query, key, length_ref, bias_ref, head):
    scores = product_right(query, key)
    if bias_ref is None:
        return scores
    rows, columns = scores.shape
    scores = scores + toeplitz_bias(bias_ref[pl.ds(head, 1), :], rows)
    at_row = lax.broadcasted_iota(jnp.int32, (rows, columns), 0)
    at_column = lax.broadcasted_iota(jnp.int32, (rows, columns), 1)
    allowed = (at_column <= at_row) & (at_column < length_ref[0])
    return jnp.where(allowed, scores, MASKED)


def softmax_rows(scores):
    exponent = jnp.exp(scores - jnp.max(scores, axis=-1, keepdims=True))
    return exponent / jnp.sum(exponent, axis=-1, keepdims=True)


def attention_forward(query_ref, key_ref, value_ref, out_ref, length_ref=None, bias_ref=None):
    rows, width = query_ref.shape
    lanes = lax.broadcasted_iota(jnp.int32, (rows, PAIR), 1)

    def one_pair(pair, carry):
        columns = pl.ds(pl.multiple_of(pair * PAIR, PAIR), PAIR)
        query, key, value = query_ref[:, columns], key_ref[:, columns], value_ref[:, columns]
        mixed = []
        for side in range(2):
            scores = masked_scores(
                head_half(query, side, lanes), key, length_ref, bias_ref, 2 * pair + side
            )
            mixed.append(product_plain(softmax_rows(scores).astype(LOW), value))
        out_ref[:, columns] = jnp.where(lanes < HEAD, mixed[0], mixed[1]).astype(LOW)
        return carry

    lax.fori_loop(0, width // PAIR, one_pair, 0)


def attention_backward(
    query_ref,
    key_ref,
    value_ref,
    grad_ref,
    dquery_ref,
    dkey_ref,
    dvalue_ref,
    length_ref=None,
    bias_ref=None,
    diagonal_ref=None,
):
    rows, width = query_ref.shape
    lanes = lax.broadcasted_iota(jnp.int32, (rows, PAIR), 1)
    if bias_ref is not None:
        flip = (
            lax.broadcasted_iota(jnp.int32, (rows, rows), 0)
            + lax.broadcasted_iota(jnp.int32, (rows, rows), 1)
            == rows - 1
        ).astype(LOW)

    def one_pair(pair, carry):
        columns = pl.ds(pl.multiple_of(pair * PAIR, PAIR), PAIR)
        query, key, value = query_ref[:, columns], key_ref[:, columns], value_ref[:, columns]
        grad = grad_ref[:, columns]
        dquery, dkey, dvalue = [], [], []
        for side in range(2):
            head = 2 * pair + side
            scores = masked_scores(head_half(query, side, lanes), key, length_ref, bias_ref, head)
            chance = softmax_rows(scores)
            chance_grad = product_right(head_half(grad, side, lanes), value)
            delta = jnp.sum(chance * chance_grad, axis=-1, keepdims=True)
            score_grad = (chance * (chance_grad - delta)).astype(LOW)
            dquery.append(product_plain(score_grad, key))
            dkey.append(product_left(score_grad, query))
            dvalue.append(product_left(chance.astype(LOW), grad))
            if bias_ref is not None:
                flipped = product_plain(flip, score_grad)
                wide = jnp.concatenate([flipped, jnp.zeros_like(flipped)], axis=1)
                skewed = pltpu.roll(wide, rows + 1, 1, stride=1, stride_axis=0)
                diagonal_ref[pl.ds(head, 1), :] = jnp.sum(skewed, axis=0, keepdims=True)
        left = lanes < HEAD
        dquery_ref[:, columns] = jnp.where(left, dquery[0], dquery[1]).astype(LOW)
        dkey_ref[:, columns] = jnp.where(left, dkey[0], dkey[1]).astype(LOW)
        dvalue_ref[:, columns] = jnp.where(left, dvalue[0], dvalue[1]).astype(LOW)
        return carry

    lax.fori_loop(0, width // PAIR, one_pair, 0)


def low_shape(*shape):
    return jax.ShapeDtypeStruct(shape, LOW)


def full_shape(*shape):
    return jax.ShapeDtypeStruct(shape, FULL)


def call(body, out_shape, scalars, arrays, scratch=(), flops=0):
    vmem = pl.BlockSpec(memory_space=pltpu.VMEM)
    smem = pl.BlockSpec(memory_space=pltpu.SMEM)
    return pl.pallas_call(
        body,
        out_shape=list(out_shape),
        in_specs=[smem] * len(scalars) + [vmem] * len(arrays),
        out_specs=[vmem] * len(out_shape),
        scratch_shapes=list(scratch),
        name=getattr(body, "func", body).__name__,
        cost_estimate=pl.CostEstimate(
            flops=int(flops * 1), transcendentals=0, bytes_accessed=1024
        ),
        compiler_params=pltpu.CompilerParams(vmem_limit_bytes=44 << 20),
    )(*scalars, *arrays)


def prepare_body(
    length_ref,
    tokens_ref,
    cotangent_ref,
    gains_ref,
    source_ref,
    permute_ref,
    input_ref,
    grad_ref,
    gains_out_ref,
    normed_ref,
):
    rows, width = tokens_ref.shape
    at_row = lax.broadcasted_iota(jnp.int32, (width, width), 0)
    permute_ref[...] = (at_row == source_ref[...]).astype(FULL).astype(LOW)
    permute = permute_ref[...]
    valid = valid_column(length_ref, rows)
    masked = product_plain(tokens_ref[...], permute) * valid
    input_ref[...] = masked.astype(LOW)
    grad_ref[...] = (product_plain(cotangent_ref[...], permute) * valid).astype(LOW)
    gains = gains_ref[...]
    high = gains.astype(LOW)
    middle = (gains - high.astype(FULL)).astype(LOW)
    low = (gains - high.astype(FULL) - middle.astype(FULL)).astype(LOW)
    gains_out_ref[...] = (
        product_plain(high, permute) + product_plain(middle, permute)
    ) + product_plain(low, permute)
    normed_ref[...] = (masked * inverse_root(masked) * gains_out_ref[0:1, :]).astype(LOW)


def self_forward_body(
    length_ref, bias_ref, normed_ref, *refs
):
    qk, vo = sides(refs[:5])
    query_ref, key_ref, value_ref, mixed_ref, partial_ref = refs[5:]
    inner = query_ref.shape[1]
    query_ref[...] = project_in(normed_ref, qk, 0, inner).astype(LOW)
    key_ref[...] = project_in(normed_ref, qk, inner, inner).astype(LOW)
    value_ref[...] = project_in(normed_ref, vo, 0, inner).astype(LOW)
    attention_forward(query_ref, key_ref, value_ref, mixed_ref, length_ref, bias_ref)
    width = partial_ref.shape[1] // 4
    for number in range(4):
        partial_ref[:, number * width : (number + 1) * width] = product_right(
            mixed_ref[...], vo[number][:, inner:]
        ).astype(LOW)


def memory_body(half_ref, other_ref, permute_ref, *refs):
    kv, _ = sides(refs[:5])
    memory_ref, key_ref, value_ref = refs[5:]
    inner = key_ref.shape[1]
    half = half_ref.shape[0]
    memory_ref[:half, :] = product_plain(half_ref[...], permute_ref[...]).astype(LOW)
    memory_ref[half:, :] = product_plain(other_ref[...], permute_ref[...]).astype(LOW)
    key_ref[...] = project_in(memory_ref, kv, 0, inner).astype(LOW)
    value_ref[...] = project_in(memory_ref, kv, inner, inner).astype(LOW)


def cross_forward_body(input_ref, mine_ref, other_ref, gains_ref, key_ref, value_ref, *refs):
    _, qo = sides(refs[:5])
    hidden_ref, normed_ref, query_ref, mixed_ref, partial_ref = refs[5:]
    inner = query_ref.shape[1]
    hidden = input_ref[...].astype(FULL) + both(mine_ref, other_ref)
    hidden_ref[...] = hidden
    normed_ref[...] = (hidden * inverse_root(hidden) * gains_ref[1:2, :]).astype(LOW)
    query_ref[...] = project_in(normed_ref, qo, 0, inner).astype(LOW)
    attention_forward(query_ref, key_ref, value_ref, mixed_ref)
    width = partial_ref.shape[1] // 4
    for number in range(4):
        partial_ref[:, number * width : (number + 1) * width] = product_right(
            mixed_ref[...], qo[number][:, inner:]
        ).astype(LOW)


GELU_SCALE = float(np.sqrt(2.0 / np.pi))
GELU_CUBE = 0.044715


def feed_body(transposed, hidden_in_ref, mine_ref, other_ref, gains_ref, grad_ref, *refs):
    gate_w, lift_w = sides(refs[:5])
    down_w = refs[5:9]
    hidden_ref, partial_ref, dnormed_ref = refs[9:12]
    dgate_w, dlift_w = sides(refs[12:17])
    ddown_w = refs[17:21]
    normed_ref, normed_t_ref, grad_t_ref, down_ref, total_ref, dtotal_ref = refs[21:]
    rows, model = hidden_ref.shape
    width = model // 4
    block = width // 4
    feed = gate_w[0].shape[1]
    hidden = hidden_in_ref[...] + both(mine_ref, other_ref)
    hidden_ref[...] = hidden
    normed_ref[...] = (hidden * inverse_root(hidden) * gains_ref[2:3, :]).astype(LOW)
    normed_t_ref[...] = normed_ref[...].T
    grad_t_ref[...] = grad_ref[...].T
    for number in range(4):
        if transposed:
            for other in range(4):
                place = number * width + other * block
                down_ref[place : place + block, :] = down_w[other][
                    number * block : (number + 1) * block, :
                ]
        else:
            down_ref[number * width : (number + 1) * width, :] = down_w[number][...]
    first = 0
    while first < feed:
        last = min(first + 512, feed)
        gate = project_in(normed_ref, gate_w, first, last - first)
        lift = project_in(normed_ref, lift_w, first, last - first)
        squared = gate * gate
        curve = jnp.tanh(GELU_SCALE * (gate + GELU_CUBE * squared * gate))
        half_up = 0.5 * (1.0 + curve)
        activated = gate * half_up
        product = (activated * lift).astype(LOW)
        down = down_ref[:, first:last]
        forward = product_right(product, down)
        dproduct = product_plain(grad_ref[...], down).astype(LOW).astype(FULL)
        slope = half_up + 0.5 * gate * (1.0 - curve * curve) * (
            GELU_SCALE * (1.0 + 3.0 * GELU_CUBE * squared)
        )
        dgate = (dproduct * lift * slope).astype(LOW)
        dlift = (dproduct * activated).astype(LOW)
        for number in range(4):
            part = slice(number * width, (number + 1) * width)
            dgate_w[number][:, first:last] = product_plain(normed_t_ref[part, :], dgate).astype(
                LOW
            )
            dlift_w[number][:, first:last] = product_plain(normed_t_ref[part, :], dlift).astype(
                LOW
            )
            ddown = product_plain(grad_t_ref[part, :], product).astype(LOW)
            if transposed:
                for other in range(4):
                    ddown_w[other][number * block : (number + 1) * block, first:last] = ddown[
                        other * block : (other + 1) * block, :
                    ]
            else:
                ddown_w[number][:, first:last] = ddown
            back = product_right(dgate, gate_w[number][:, first:last]) + product_right(
                dlift, lift_w[number][:, first:last]
            )
            if first == 0:
                dtotal_ref[:, part] = back
            else:
                dtotal_ref[:, part] += back
        if first == 0:
            total_ref[...] = forward
        else:
            total_ref[...] += forward
        first = last
    partial_ref[...] = total_ref[...].astype(LOW)
    dnormed_ref[...] = dtotal_ref[...].astype(LOW)


def cross_backward_body(
    hidden_ref,
    mine_ref,
    other_ref,
    gains_ref,
    grad_ref,
    normed_ref,
    memory_ref,
    query_ref,
    key_ref,
    value_ref,
    mixed_ref,
    *refs,
):
    kv, qo = sides(refs[:5])
    grad_out_ref, dgain_ref, dnormed_ref, keep_ref, away_ref = refs[5:10]
    dkv, dqo = sides(refs[10:15])
    low_ref, transposed_ref, dmixed_ref, dquery_ref, dkey_ref, dvalue_ref = refs[15:]
    rows, model = hidden_ref.shape
    width = model // 4
    inner = query_ref.shape[1]
    half = rows // 2
    back, dgain_ref[...] = norm_backward(
        hidden_ref[...], gains_ref[2:3, :], both(mine_ref, other_ref)
    )
    grad = grad_ref[...].astype(FULL) + back
    grad_out_ref[...] = grad
    low_ref[...] = grad.astype(LOW)
    dmixed_ref[...] = project_in(low_ref, qo, inner, inner).astype(LOW)
    attention_backward(
        query_ref, key_ref, value_ref, dmixed_ref, dquery_ref, dkey_ref, dvalue_ref
    )
    for number in range(4):
        part = slice(number * width, (number + 1) * width)
        dnormed_ref[:, part] = product_right(dquery_ref[...], qo[number][:, :inner]).astype(LOW)
        partial = (
            product_right(dkey_ref[...], kv[number][:, :inner])
            + product_right(dvalue_ref[...], kv[number][:, inner:])
        ).astype(LOW)
        keep_ref[:, part] = partial[:half]
        away_ref[:, part] = partial[half:]
    transposed_ref[...] = memory_ref[...].T
    for number in range(4):
        part = slice(number * width, (number + 1) * width)
        dkv[number][:, :inner] = product_plain(transposed_ref[part, :], dkey_ref[...]).astype(LOW)
        dkv[number][:, inner:] = product_plain(transposed_ref[part, :], dvalue_ref[...]).astype(
            LOW
        )
    transposed_ref[...] = normed_ref[...].T
    for number in range(4):
        part = slice(number * width, (number + 1) * width)
        dqo[number][:, :inner] = product_plain(transposed_ref[part, :], dquery_ref[...]).astype(
            LOW
        )
    transposed_ref[...] = low_ref[...].T
    for number in range(4):
        part = slice(number * width, (number + 1) * width)
        dqo[number][:, inner:] = product_plain(transposed_ref[part, :], mixed_ref[...]).astype(LOW)


def self_backward_body(
    length_ref,
    bias_ref,
    hidden_ref,
    mine_ref,
    other_ref,
    gains_ref,
    grad_ref,
    normed_ref,
    query_ref,
    key_ref,
    value_ref,
    mixed_ref,
    *refs,
):
    qk, vo = sides(refs[:5])
    grad_out_ref, dgain_ref, dnormed_ref, diagonal_ref = refs[5:9]
    dqk, dvo = sides(refs[9:14])
    low_ref, transposed_ref, dmixed_ref, dquery_ref, dkey_ref, dvalue_ref = refs[14:]
    rows, model = hidden_ref.shape
    width = model // 4
    inner = query_ref.shape[1]
    back, dgain_ref[...] = norm_backward(
        hidden_ref[...], gains_ref[1:2, :], both(mine_ref, other_ref)
    )
    grad = grad_ref[...] + back
    grad_out_ref[...] = grad
    low_ref[...] = grad.astype(LOW)
    dmixed_ref[...] = project_in(low_ref, vo, inner, inner).astype(LOW)
    attention_backward(
        query_ref,
        key_ref,
        value_ref,
        dmixed_ref,
        dquery_ref,
        dkey_ref,
        dvalue_ref,
        length_ref,
        bias_ref,
        diagonal_ref,
    )
    for number in range(4):
        part = slice(number * width, (number + 1) * width)
        dnormed_ref[:, part] = (
            product_right(dquery_ref[...], qk[number][:, :inner])
            + product_right(dkey_ref[...], qk[number][:, inner:])
            + product_right(dvalue_ref[...], vo[number][:, :inner])
        ).astype(LOW)
    transposed_ref[...] = normed_ref[...].T
    for number in range(4):
        part = slice(number * width, (number + 1) * width)
        dqk[number][:, :inner] = product_plain(transposed_ref[part, :], dquery_ref[...]).astype(
            LOW
        )
        dqk[number][:, inner:] = product_plain(transposed_ref[part, :], dkey_ref[...]).astype(LOW)
        dvo[number][:, :inner] = product_plain(transposed_ref[part, :], dvalue_ref[...]).astype(
            LOW
        )
    transposed_ref[...] = low_ref[...].T
    for number in range(4):
        part = slice(number * width, (number + 1) * width)
        dvo[number][:, inner:] = product_plain(transposed_ref[part, :], mixed_ref[...]).astype(LOW)


def finish_body(
    length_ref,
    permute_ref,
    input_ref,
    mine_ref,
    other_ref,
    gains_ref,
    grad_ref,
    dgain_cross_ref,
    dgain_feed_ref,
    onehot_ref,
    diagonal_ref,
    out_ref,
    dgains_ref,
    table_ref,
):
    rows = input_ref.shape[0]
    permute = permute_ref[...]
    back, dgain = norm_backward(
        input_ref[...].astype(FULL), gains_ref[0:1, :], both(mine_ref, other_ref)
    )
    total = ((grad_ref[...] + back) * valid_column(length_ref, rows)).astype(LOW)
    out_ref[...] = product_right(total, permute).astype(LOW)
    dgains = jnp.concatenate([dgain, dgain_cross_ref[...], dgain_feed_ref[...]], axis=0)
    high = dgains.astype(LOW)
    middle = (dgains - high.astype(FULL)).astype(LOW)
    low = (dgains - high.astype(FULL) - middle.astype(FULL)).astype(LOW)
    dgains_ref[...] = (
        product_right(high, permute) + product_right(middle, permute)
    ) + product_right(low, permute)
    table_ref[...] = lax.dot_general(
        onehot_ref[...],
        diagonal_ref[...],
        (((1,), (1,)), ((), ())),
        precision=HIGHEST,
        preferred_element_type=FULL,
    )


def output_body(length_ref, permute_ref, hidden_ref, mine_ref, other_ref, out_ref):
    rows = hidden_ref.shape[0]
    total = (hidden_ref[...] + both(mine_ref, other_ref)) * valid_column(length_ref, rows)
    out_ref[...] = product_right(total.astype(LOW), permute_ref[...]).astype(LOW)


def encoder_body(permute_ref, mine_ref, other_ref, out_ref):
    total = both(mine_ref, other_ref).astype(LOW)
    out_ref[...] = product_right(total, permute_ref[...]).astype(LOW)


def fold_body(*refs):
    own, one, two = refs[:3]
    outs = refs[3:]
    width = own.shape[1]
    sides_held = outs[0].shape[1] // width
    block = outs[0].shape[0]
    for side in range(sides_held):
        for place in range(4):
            first = (4 * side + place) * block
            rows = slice(first, first + block)
            total = (
                own[rows, :].astype(FULL) + one[rows, :].astype(FULL) + two[rows, :].astype(FULL)
            )
            outs[place][:, side * width : (side + 1) * width] = total.astype(outs[place].dtype)


def fold_quarter(terms, sides_held):
    rows = terms[0].shape[0] // (4 * sides_held)
    width = terms[0].shape[1] * sides_held
    kinds = [full_shape, full_shape, low_shape, low_shape]
    return call(fold_body, [kind(rows, width) for kind in kinds], (), terms)


def stack_body(*refs):
    parts, outs = refs[:4], refs[4:]
    block = parts[0].shape[0]
    first = 0
    for out in outs:
        width = out.shape[1]
        for side in range(out.shape[0] // (4 * block)):
            for place in range(4):
                row = (4 * side + place) * block
                out[row : row + block, :] = parts[place][:, first : first + width]
            first += width


def stack_quarter(parts, shapes):
    return call(stack_body, [low_shape(*shape) for shape in shapes], (), parts)


def merge_body(x_in, y_in, left, right, x_out, y_out):
    x_out[...] = (x_in[...].astype(FULL) + left[...].astype(FULL)).astype(LOW)
    y_out[...] = (y_in[...].astype(FULL) + right[...].astype(FULL)).astype(LOW)


def merge_quarters(x_part, y_part, left, right):
    rows, width = left.shape
    at = [
        pl.BlockSpec((rows, width), lambda one: (0, 0)),
        pl.BlockSpec((rows, width), lambda one: (1, 0)),
    ]
    whole = pl.BlockSpec((rows, width), lambda one: (0, 0))
    return pl.pallas_call(
        merge_body,
        out_shape=[low_shape(*x_part.shape), low_shape(*y_part.shape)],
        grid=(1,),
        in_specs=at + [whole, whole],
        out_specs=at,
        input_output_aliases={0: 0, 1: 1},
        name="merge_body",
        cost_estimate=pl.CostEstimate(flops=1024, transcendentals=0, bytes_accessed=1024),
    )(x_part, y_part, left, right)


def gather_upper(value, devices, wait=()):
    masks = upper_masks(devices)
    if wait:
        value = after(value, *wait)
    if len(masks) == 2:
        one = swap_dp(value, masks[0], devices)
        two = swap_dp(value, masks[1], devices)
        return [value, one, two, swap_dp(one, masks[1], devices)]
    for mask in masks:
        value = jnp.concatenate([value, swap_dp(value, mask, devices)], axis=0)
    return [value]


def stack_sides(blocks, widths):
    if len(blocks) == 4:
        rows = 4 * blocks[0].shape[0]
        return stack_quarter(blocks, [(2 * rows, width) for width in widths])
    groups, first = [], 0
    for width in widths:
        middle, last = first + width, first + 2 * width
        groups.append(
            jnp.concatenate([blocks[0][:, first:middle], blocks[0][:, middle:last]], axis=0)
        )
        first = last
    return groups


def gather_lower(first, devices, x_wait=(), y_wait=(), last_wait=()):
    rows = first.shape[0] // 2
    x_part = swap_dp(after(first, *x_wait) if x_wait else first, 1, devices)
    y_part = swap_dp(after(first, *y_wait) if y_wait else first, 2, devices)
    left, right = x_part[:rows], y_part[rows:]
    if last_wait:
        left, right = after(left, *last_wait), after(right, *last_wait)
    return [first, x_part, y_part, swap_dp(left, 2, devices), swap_dp(right, 1, devices)]


def reduce_last(pieces, devices, wait=()):
    left, right = pieces[3:]
    if wait:
        left, right = after(left, *wait), after(right, *wait)
    return [swap_dp(left, 2, devices), swap_dp(right, 1, devices)]


def reduce_lower(pieces, came, devices, wait=()):
    x_part, y_part = merge_quarters(*pieces[1:3], *came)
    if wait:
        x_part, y_part = after(x_part, *wait), after(y_part, *wait)
    return [pieces[0], swap_dp(x_part, 1, devices), swap_dp(y_part, 2, devices)]


def reduce_upper(terms, devices, wait=()):
    masks = upper_masks(devices)
    if len(masks) == 2:
        own, one, two, three = fold_quarter(terms, 2)
        if wait:
            two, three = after(two, *wait), after(three, *wait)
        one = (one + swap_dp(three, masks[1], devices).astype(FULL)).astype(LOW)
        two = swap_dp(two, masks[1], devices)
        return own + two.astype(FULL) + swap_dp(one, masks[0], devices).astype(FULL)
    value = terms[0].astype(FULL) + terms[1].astype(FULL) + terms[2].astype(FULL)
    rows = value.shape[0] // 2
    value = jnp.concatenate([value[:rows], value[rows:]], axis=1)
    for mask in masks[::-1]:
        half = value.shape[0] // 2
        away = swap_dp(value[half:].astype(LOW), mask, devices)
        value = value[:half] + away.astype(FULL)
    return value


def first_across(value, devices):
    x_part, y_part = swap_dp(value, 1, devices), swap_dp(value, 2, devices)
    return [value, x_part, y_part, swap_dp(x_part, 2, devices)]


def gather_across(blocks, devices, wait):
    masks = upper_masks(devices)
    rows, width = blocks[0].shape
    first = after(stack_quarter(blocks, [(4 * rows, width)])[0], *wait)
    one, two = swap_dp(first, masks[0], devices), swap_dp(first, masks[1], devices)
    return [first, one, two, swap_dp(one, masks[1], devices)]


def reduce_across_last(pieces, devices):
    mask = upper_masks(devices)[1]
    return [swap_dp(pieces[3], mask, devices), swap_dp(pieces[2], mask, devices)]


def reduce_across(pieces, came, devices):
    mask = upper_masks(devices)[0]
    one = (pieces[1].astype(FULL) + came[0].astype(FULL)).astype(LOW)
    return [pieces[0], came[1], swap_dp(one, mask, devices)]


def reduce_across_first(terms, devices):
    own, x_part, y_part, last = fold_quarter(terms, 1)
    x_part = (x_part + swap_dp(last, 2, devices).astype(FULL)).astype(LOW)
    return (
        own
        + swap_dp(y_part, 2, devices).astype(FULL)
        + swap_dp(x_part, 1, devices).astype(FULL)
    )


def deal(value, order, devices):
    rows, width = value.shape
    first = lax.all_to_all(
        value.reshape(devices, rows // devices, width), "dp", split_axis=0, concat_axis=0, tiled=True
    )
    second = lax.all_to_all(
        jnp.take(first, order, axis=0), "dp", split_axis=0, concat_axis=0, tiled=True
    )
    return second.reshape(rows, width)


def on_device(
    tokens,
    encoder_states,
    cotangent,
    lengths,
    deal_order,
    bucket_index,
    rel_table,
    gain_self,
    self_query,
    self_key,
    self_value,
    self_output,
    gain_cross,
    cross_query,
    cross_key,
    cross_value,
    cross_output,
    gain_feed,
    feed_gate,
    feed_value,
    feed_output,
):
    devices = lax.axis_size("dp")
    myself = lax.axis_index("dp")
    core = lax.axis_index("tensor")
    rows, model = tokens.shape
    block = model // devices
    buckets, heads = rel_table.shape
    inner = self_query.shape[1]
    feed = feed_gate.shape[1]
    across = devices == 16

    numbers = jnp.arange(devices, dtype=jnp.int32)
    owner_of = jnp.sum(
        jnp.where(deal_order[:, None] == numbers[None, :], numbers[:, None], 0), axis=0
    )
    length = jnp.sum(jnp.where(numbers == myself, lengths, 0)).reshape(1)

    self_own = jnp.concatenate([self_query, self_key, self_value, self_output], axis=1)
    cross_own = jnp.concatenate([cross_key, cross_value, cross_query, cross_output], axis=1)
    feed_own = jnp.concatenate([feed_gate, feed_value], axis=1)
    self_blocks = gather_upper(self_own, devices)
    if across:
        down_blocks = first_across(feed_output, devices)
        self_blocks[3] = after(self_blocks[3], *down_blocks[1:3])
    (self_first,) = stack_sides(self_blocks, [2 * inner])
    cross_blocks = gather_upper(cross_own, devices, self_blocks[1:3])
    self_w = gather_lower(self_first, devices)
    (cross_first,) = stack_sides(cross_blocks, [2 * inner])
    cross_w = gather_lower(cross_first, devices, self_w[1:2], self_w[2:3])
    feed_blocks = gather_upper(feed_own, devices, cross_blocks[1:3])
    (feed_first,) = stack_sides(feed_blocks, [feed])
    if across:
        down = gather_across(down_blocks, devices, feed_blocks[1:3])
    else:
        down = gather_upper(feed_output, devices)[0]
        width = feed // 2
        down = gather_lower(
            jnp.concatenate([down[:, :width], down[:, width:]], axis=0), devices
        )
        middle = down[0].shape[0] // 2
        down = [
            jnp.concatenate([one[:middle], one[middle:]], axis=1) for one in down[:3]
        ] + [jnp.concatenate(down[3:], axis=1)]

    offsets = jnp.asarray(np.array(block_offsets(upper_masks(devices) + [1, 2]), np.int32))
    source = (
        ((myself ^ offsets) * block)[:, None] + jnp.arange(block, dtype=jnp.int32)[None, :]
    ).reshape(1, -1)
    permute, masked_input, grad_three, gains, normed_self = call(
        prepare_body,
        [
            low_shape(model, model),
            low_shape(rows, model),
            low_shape(rows, model),
            full_shape(3, model),
            low_shape(rows, model),
        ],
        (length,),
        (tokens, cotangent, jnp.stack([gain_self, gain_cross, gain_feed]), source),
        flops=4 * rows * model * model,
    )

    half = rows // 2
    memory_half = deal(
        lax.dynamic_slice_in_dim(encoder_states, core * half, half, axis=0), deal_order, devices
    )
    memory_other = swap_tensor(memory_half)

    skewed_bucket = jnp.concatenate(
        [bucket_index[:1], jnp.full((rows,), -1, jnp.int32), bucket_index[::-1][: rows - 1]]
    )
    onehot = (jnp.arange(buckets, dtype=jnp.int32)[:, None] == skewed_bucket[None, :]).astype(FULL)
    bias_rows = jnp.dot(rel_table.T, onehot, precision=HIGHEST)

    unit = 2 * rows * model * inner
    query_self, key_self, value_self, mixed_self, self_partial = call(
        self_forward_body,
        [low_shape(rows, inner)] * 4 + [low_shape(rows, model)],
        (length,),
        (bias_rows, normed_self, *self_w),
        flops=5 * unit,
    )
    memory, key_cross, value_cross = call(
        memory_body,
        [low_shape(rows, model)] + [low_shape(rows, inner)] * 2,
        (),
        (memory_half, memory_other, permute, *cross_w),
        flops=4 * unit,
    )
    hidden_one, normed_cross, query_cross, mixed_cross, partial = call(
        cross_forward_body,
        [full_shape(rows, model), low_shape(rows, model)]
        + [low_shape(rows, inner)] * 2
        + [low_shape(rows, model)],
        (),
        (
            masked_input,
            self_partial,
            swap_tensor(self_partial),
            gains,
            key_cross,
            value_cross,
            *cross_w,
        ),
        flops=3 * unit,
    )
    quarter_rows = model // 4
    feed_w = gather_lower(
        feed_first,
        devices,
        (cross_w[1], self_partial),
        (cross_w[2], self_partial),
        (partial,),
    )

    def group_shapes(width):
        return [low_shape(2 * quarter_rows, width)] * 3 + [low_shape(quarter_rows, width)] * 2

    feed_grads = group_shapes(feed) + [low_shape(quarter_rows, feed)] * 4
    outs = call(
        functools.partial(feed_body, across),
        [full_shape(rows, model), low_shape(rows, model), low_shape(rows, model)] + feed_grads,
        (),
        (hidden_one, partial, swap_tensor(partial), gains, grad_three, *feed_w, *down),
        scratch=[
            pltpu.VMEM((rows, model), LOW),
            pltpu.VMEM((model, rows), LOW),
            pltpu.VMEM((model, rows), LOW),
            pltpu.VMEM((model, feed), LOW),
            pltpu.VMEM((rows, model), FULL),
            pltpu.VMEM((rows, model), FULL),
        ],
        flops=18 * rows * model * feed,
    )
    hidden_two, partial, dpartial = outs[:3]
    dfeed, ddown = outs[3:8], outs[8:12]
    feed_came = reduce_last(dfeed, devices)
    if across:
        down_came = reduce_across_last(ddown, devices)
    else:
        width = feed // 2
        ddown = [
            jnp.concatenate([one[:, :width], one[:, width:]], axis=0) for one in ddown[:3]
        ] + [ddown[3][:, :width], ddown[3][:, width:]]
        down_came = reduce_last(ddown, devices)
    (layer_result,) = call(
        output_body,
        [low_shape(rows, model)],
        (length,),
        (permute, hidden_two, partial, swap_tensor(partial)),
        flops=2 * unit,
    )

    attention_scratch = [
        pltpu.VMEM((rows, model), LOW),
        pltpu.VMEM((model, rows), LOW),
    ] + [pltpu.VMEM((rows, inner), LOW)] * 4
    outs = call(
        cross_backward_body,
        [
            full_shape(rows, model),
            full_shape(1, model),
            low_shape(rows, model),
            low_shape(half, model),
            low_shape(half, model),
        ]
        + group_shapes(2 * inner),
        (),
        (
            hidden_two,
            dpartial,
            swap_tensor(dpartial),
            gains,
            grad_three,
            normed_cross,
            memory,
            query_cross,
            key_cross,
            value_cross,
            mixed_cross,
            *cross_w,
        ),
        scratch=attention_scratch,
        flops=9 * unit,
    )
    grad_two, dgain_feed, dpartial, keep, away = outs[:5]
    dcross = outs[5:10]
    feed_terms = reduce_lower(
        dfeed, [after(one, dpartial) for one in feed_came], devices
    )
    cross_came = reduce_last(dcross, devices, down_came)
    cross_terms = reduce_lower(dcross, cross_came, devices, feed_terms[1:])
    (encoder_half,) = call(
        encoder_body,
        [low_shape(half, model)],
        (),
        (permute, keep, swap_tensor(away)),
        flops=unit,
    )
    encoder_grad = deal(encoder_half, owner_of, devices)

    outs = call(
        self_backward_body,
        [
            full_shape(rows, model),
            full_shape(1, model),
            low_shape(rows, model),
            full_shape(heads, 2 * rows),
        ]
        + group_shapes(2 * inner),
        (length,),
        (
            bias_rows,
            hidden_one,
            dpartial,
            swap_tensor(dpartial),
            gains,
            after(grad_two, *feed_came),
            normed_self,
            query_self,
            key_self,
            value_self,
            mixed_self,
            *self_w,
        ),
        scratch=attention_scratch,
        flops=10 * unit,
    )
    grad_one, dgain_cross, dpartial, diagonal = outs[:4]
    dself = outs[4:9]
    self_came = reduce_last(dself, devices, feed_terms[1:])
    self_terms = reduce_lower(dself, self_came, devices, cross_terms[1:])
    input_grad, dgains, dtable = call(
        finish_body,
        [low_shape(rows, model), full_shape(3, model), full_shape(buckets, heads)],
        (length,),
        (
            permute,
            masked_input,
            dpartial,
            swap_tensor(dpartial),
            gains,
            grad_one,
            dgain_cross,
            dgain_feed,
            onehot,
            diagonal,
        ),
        flops=2 * unit,
    )

    if across:
        down_terms = reduce_across(ddown, down_came, devices)
        feed_sums = reduce_upper(feed_terms, devices, down_terms[2:])
        down_sum = reduce_across_first(down_terms, devices)
    else:
        down_sum = reduce_upper(reduce_lower(ddown, down_came, devices), devices)
        feed_sums = reduce_upper(feed_terms, devices)
    cross_sums = reduce_upper(cross_terms, devices, (feed_sums,))
    self_sums = reduce_upper(self_terms, devices, (cross_sums,))
    small = total_small(
        jnp.concatenate([dgains.reshape(-1), dtable.reshape(-1)]).reshape(-1, 128), devices
    ).reshape(-1)
    gain_sums = small[: 3 * model].reshape(3, model)
    table_sum = small[3 * model :].reshape(buckets, heads)

    def column(value, number, width):
        return value[:, number * width : (number + 1) * width]

    return (
        layer_result,
        input_grad,
        encoder_grad,
        table_sum,
        gain_sums[0],
        column(self_sums, 0, inner),
        column(self_sums, 1, inner),
        column(self_sums, 2, inner),
        column(self_sums, 3, inner),
        gain_sums[1],
        column(cross_sums, 2, inner),
        column(cross_sums, 0, inner),
        column(cross_sums, 1, inner),
        column(cross_sums, 3, inner),
        gain_sums[2],
        column(feed_sums, 0, feed),
        column(feed_sums, 1, feed),
        down_sum,
    )


def solution(mesh):
    in_specs = (
        P("dp", None),
        P("dp", None),
        P("dp", None),
        P(),
        P(),
        P(),
        P(None, "tensor"),
        P(),
        P("dp", "tensor"),
        P("dp", "tensor"),
        P("dp", "tensor"),
        P("dp", "tensor"),
        P(),
        P("dp", "tensor"),
        P("dp", "tensor"),
        P("dp", "tensor"),
        P("dp", "tensor"),
        P(),
        P("dp", "tensor"),
        P("dp", "tensor"),
        P("dp", "tensor"),
    )
    out_specs = (
        P("dp", None),
        P("dp", None),
        P(("dp", "tensor"), None),
        P(None, "tensor"),
        P(),
        P("dp", "tensor"),
        P("dp", "tensor"),
        P("dp", "tensor"),
        P("dp", "tensor"),
        P(),
        P("dp", "tensor"),
        P("dp", "tensor"),
        P("dp", "tensor"),
        P("dp", "tensor"),
        P(),
        P("dp", "tensor"),
        P("dp", "tensor"),
        P("dp", "tensor"),
    )
    return jax.shard_map(
        on_device, mesh=mesh, in_specs=in_specs, out_specs=out_specs, check_vma=False
    )
```

```python
import functools

import jax
import jax.numpy as jnp
import numpy as np
from jax import lax
from jax.experimental import pallas as pl
from jax.experimental.pallas import tpu as pltpu
from jax.sharding import PartitionSpec as P

EPSILON = 1e-06
MASKED = -1e30
HIGHEST = lax.Precision.HIGHEST
HEAD = 64
PAIR = 2 * HEAD
LOW = jnp.bfloat16
FULL = jnp.float32


def upper_masks(devices):
    if devices == 16:
        return [12, 4]
    return [1 << bit for bit in range(devices.bit_length() - 2, 1, -1)]


def block_offsets(masks):
    offsets = [0]
    for mask in masks:
        offsets = offsets + [offset ^ mask for offset in offsets]
    return offsets


def swap_dp(value, mask, devices):
    return lax.ppermute(value, "dp", [(one, one ^ mask) for one in range(devices)])


def swap_tensor(value):
    return lax.ppermute(value, "tensor", [(0, 1), (1, 0)])


def total_small(value, devices):
    mask = 1
    while mask < devices:
        value = value + swap_dp(value, mask, devices)
        mask = 2 * mask
    return value


def product_plain(left, right):
    return jnp.dot(left, right, preferred_element_type=FULL)


def product_right(left, right):
    return lax.dot_general(left, right, (((1,), (1,)), ((), ())), preferred_element_type=FULL)


def product_left(left, right):
    return lax.dot_general(left, right, (((0,), (0,)), ((), ())), preferred_element_type=FULL)


def quarter(ref, number):
    width = ref.shape[1] // 4
    return ref[:, number * width : (number + 1) * width]


def sides(refs):
    own, x_part, y_part, left, right = refs
    rows = left.shape[0]
    return (
        [own.at[:rows], x_part.at[:rows], y_part.at[:rows], left],
        [own.at[rows:], x_part.at[rows:], y_part.at[rows:], right],
    )


def after(value, *earlier):
    return lax.optimization_barrier((value, *earlier))[0]


def project_in(value_ref, pieces, columns):
    total = None
    for number, piece in enumerate(pieces):
        part = product_plain(quarter(value_ref, number), piece[:, columns])
        total = part if total is None else total + part
    return total


def inverse_root(value):
    return lax.rsqrt(jnp.mean(value * value, axis=-1, keepdims=True) + EPSILON)


def norm_backward(value, gain, upstream):
    root = inverse_root(value)
    weighted = upstream * gain
    inner_mean = jnp.mean(weighted * value, axis=-1, keepdims=True)
    grad = root * weighted - value * (root * root * root) * inner_mean
    return grad, jnp.sum(upstream * value * root, axis=0, keepdims=True)


def both(mine_ref, other_ref):
    return mine_ref[...].astype(FULL) + other_ref[...].astype(FULL)


def valid_column(length_ref, rows):
    return (lax.broadcasted_iota(jnp.int32, (rows, 1), 0) < length_ref[0]).astype(FULL)


def toeplitz_bias(row, rows):
    wide = jnp.broadcast_to(row, (rows, row.shape[1]))
    return pltpu.roll(wide, 0, 1, stride=1, stride_axis=0)[:, :rows]


def head_half(value, side, lanes):
    keep = lanes < HEAD if side == 0 else lanes >= HEAD
    return jnp.where(keep, value, jnp.zeros_like(value))


def masked_scores(query, key, length_ref, bias_ref, head):
    scores = product_right(query, key)
    if bias_ref is None:
        return scores
    rows, columns = scores.shape
    scores = scores + toeplitz_bias(bias_ref[pl.ds(head, 1), :], rows)
    at_row = lax.broadcasted_iota(jnp.int32, (rows, columns), 0)
    at_column = lax.broadcasted_iota(jnp.int32, (rows, columns), 1)
    allowed = (at_column <= at_row) & (at_column < length_ref[0])
    return jnp.where(allowed, scores, MASKED)


def softmax_rows(scores):
    exponent = jnp.exp(scores - jnp.max(scores, axis=-1, keepdims=True))
    return exponent / jnp.sum(exponent, axis=-1, keepdims=True)


def attention_forward(query_ref, key_ref, value_ref, out_ref, length_ref=None, bias_ref=None):
    rows, width = query_ref.shape
    lanes = lax.broadcasted_iota(jnp.int32, (rows, PAIR), 1)

    def one_pair(pair, carry):
        columns = pl.ds(pl.multiple_of(pair * PAIR, PAIR), PAIR)
        query, key, value = query_ref[:, columns], key_ref[:, columns], value_ref[:, columns]
        mixed = []
        for side in range(2):
            scores = masked_scores(
                head_half(query, side, lanes), key, length_ref, bias_ref, 2 * pair + side
            )
            mixed.append(product_plain(softmax_rows(scores).astype(LOW), value))
        out_ref[:, columns] = jnp.where(lanes < HEAD, mixed[0], mixed[1]).astype(LOW)
        return carry

    lax.fori_loop(0, width // PAIR, one_pair, 0)


def attention_backward(
    query_ref,
    key_ref,
    value_ref,
    grad_ref,
    dquery_ref,
    dkey_ref,
    dvalue_ref,
    length_ref=None,
    bias_ref=None,
    diagonal_ref=None,
):
    rows, width = query_ref.shape
    lanes = lax.broadcasted_iota(jnp.int32, (rows, PAIR), 1)
    if bias_ref is not None:
        flip = (
            lax.broadcasted_iota(jnp.int32, (rows, rows), 0)
            + lax.broadcasted_iota(jnp.int32, (rows, rows), 1)
            == rows - 1
        ).astype(LOW)

    def one_pair(pair, carry):
        columns = pl.ds(pl.multiple_of(pair * PAIR, PAIR), PAIR)
        query, key, value = query_ref[:, columns], key_ref[:, columns], value_ref[:, columns]
        grad = grad_ref[:, columns]
        dquery, dkey, dvalue = [], [], []
        for side in range(2):
            head = 2 * pair + side
            scores = masked_scores(head_half(query, side, lanes), key, length_ref, bias_ref, head)
            chance = softmax_rows(scores)
            chance_grad = product_right(head_half(grad, side, lanes), value)
            delta = jnp.sum(chance * chance_grad, axis=-1, keepdims=True)
            score_grad = (chance * (chance_grad - delta)).astype(LOW)
            dquery.append(product_plain(score_grad, key))
            dkey.append(product_left(score_grad, query))
            dvalue.append(product_left(chance.astype(LOW), grad))
            if bias_ref is not None:
                flipped = product_plain(flip, score_grad)
                wide = jnp.concatenate([flipped, jnp.zeros_like(flipped)], axis=1)
                skewed = pltpu.roll(wide, rows + 1, 1, stride=1, stride_axis=0)
                diagonal_ref[pl.ds(head, 1), :] = jnp.sum(skewed, axis=0, keepdims=True)
        left = lanes < HEAD
        dquery_ref[:, columns] = jnp.where(left, dquery[0], dquery[1]).astype(LOW)
        dkey_ref[:, columns] = jnp.where(left, dkey[0], dkey[1]).astype(LOW)
        dvalue_ref[:, columns] = jnp.where(left, dvalue[0], dvalue[1]).astype(LOW)
        return carry

    lax.fori_loop(0, width // PAIR, one_pair, 0)


def low_shape(*shape):
    return jax.ShapeDtypeStruct(shape, LOW)


def full_shape(*shape):
    return jax.ShapeDtypeStruct(shape, FULL)


def call(body, out_shape, scalars, arrays, scratch=(), flops=0):
    vmem = pl.BlockSpec(memory_space=pltpu.VMEM)
    smem = pl.BlockSpec(memory_space=pltpu.SMEM)
    return pl.pallas_call(
        body,
        out_shape=list(out_shape),
        in_specs=[smem] * len(scalars) + [vmem] * len(arrays),
        out_specs=[vmem] * len(out_shape),
        scratch_shapes=list(scratch),
        name=getattr(body, "func", body).__name__,
        cost_estimate=pl.CostEstimate(
            flops=int(flops * 1), transcendentals=0, bytes_accessed=1024
        ),
        compiler_params=pltpu.CompilerParams(vmem_limit_bytes=44 << 20),
    )(*scalars, *arrays)


def prepare_body(
    length_ref,
    tokens_ref,
    cotangent_ref,
    gains_ref,
    source_ref,
    permute_ref,
    input_ref,
    grad_ref,
    gains_out_ref,
    normed_ref,
):
    rows, width = tokens_ref.shape
    at_row = lax.broadcasted_iota(jnp.int32, (width, width), 0)
    permute_ref[...] = (at_row == source_ref[...]).astype(FULL).astype(LOW)
    permute = permute_ref[...]
    valid = valid_column(length_ref, rows)
    masked = product_plain(tokens_ref[...], permute) * valid
    input_ref[...] = masked.astype(LOW)
    grad_ref[...] = (product_plain(cotangent_ref[...], permute) * valid).astype(LOW)
    gains = gains_ref[...]
    high = gains.astype(LOW)
    middle = (gains - high.astype(FULL)).astype(LOW)
    low = (gains - high.astype(FULL) - middle.astype(FULL)).astype(LOW)
    gains_out_ref[...] = (
        product_plain(high, permute) + product_plain(middle, permute)
    ) + product_plain(low, permute)
    normed_ref[...] = (masked * inverse_root(masked) * gains_out_ref[0:1, :]).astype(LOW)


def self_forward_body(
    length_ref, bias_ref, normed_ref, *refs
):
    qk, vo = sides(refs[:5])
    query_ref, key_ref, value_ref, mixed_ref, partial_ref = refs[5:]
    inner = query_ref.shape[1]
    query_ref[...] = project_in(normed_ref, qk, slice(0, inner)).astype(LOW)
    key_ref[...] = project_in(normed_ref, qk, slice(inner, 2 * inner)).astype(LOW)
    value_ref[...] = project_in(normed_ref, vo, slice(0, inner)).astype(LOW)
    attention_forward(query_ref, key_ref, value_ref, mixed_ref, length_ref, bias_ref)
    width = partial_ref.shape[1] // 4
    for number in range(4):
        partial_ref[:, number * width : (number + 1) * width] = product_right(
            mixed_ref[...], vo[number][:, inner:]
        ).astype(LOW)


def memory_body(half_ref, other_ref, permute_ref, *refs):
    kv, _ = sides(refs[:5])
    memory_ref, key_ref, value_ref = refs[5:]
    inner = key_ref.shape[1]
    half = half_ref.shape[0]
    memory_ref[:half, :] = product_plain(half_ref[...], permute_ref[...]).astype(LOW)
    memory_ref[half:, :] = product_plain(other_ref[...], permute_ref[...]).astype(LOW)
    key_ref[...] = project_in(memory_ref, kv, slice(0, inner)).astype(LOW)
    value_ref[...] = project_in(memory_ref, kv, slice(inner, 2 * inner)).astype(LOW)


def cross_forward_body(input_ref, mine_ref, other_ref, gains_ref, key_ref, value_ref, *refs):
    _, qo = sides(refs[:5])
    hidden_ref, normed_ref, query_ref, mixed_ref, partial_ref = refs[5:]
    inner = query_ref.shape[1]
    hidden = input_ref[...].astype(FULL) + both(mine_ref, other_ref)
    hidden_ref[...] = hidden
    normed_ref[...] = (hidden * inverse_root(hidden) * gains_ref[1:2, :]).astype(LOW)
    query_ref[...] = project_in(normed_ref, qo, slice(0, inner)).astype(LOW)
    attention_forward(query_ref, key_ref, value_ref, mixed_ref)
    width = partial_ref.shape[1] // 4
    for number in range(4):
        partial_ref[:, number * width : (number + 1) * width] = product_right(
            mixed_ref[...], qo[number][:, inner:]
        ).astype(LOW)


GELU_SCALE = float(np.sqrt(2.0 / np.pi))
GELU_CUBE = 0.044715
CHUNK = 256


def feed_body(transposed, hidden_in_ref, mine_ref, other_ref, gains_ref, grad_ref, *refs):
    gate_w, lift_w = sides(refs[:5])
    down_w = refs[5:9]
    hidden_ref, partial_ref, dnormed_ref = refs[9:12]
    dgate_w, dlift_w = sides(refs[12:17])
    ddown_w = refs[17:21]
    normed_ref, normed_t_ref, grad_t_ref, down_ref, total_ref, dtotal_ref = refs[21:]
    rows, model = hidden_ref.shape
    width = model // 4
    block = width // 4
    feed = gate_w[0].shape[1]
    hidden = hidden_in_ref[...] + both(mine_ref, other_ref)
    hidden_ref[...] = hidden
    normed_ref[...] = (hidden * inverse_root(hidden) * gains_ref[2:3, :]).astype(LOW)
    normed_t_ref[...] = normed_ref[...].T
    grad_t_ref[...] = grad_ref[...].T
    for number in range(4):
        if transposed:
            for other in range(4):
                place = number * width + other * block
                down_ref[place : place + block, :] = down_w[other][
                    number * block : (number + 1) * block, :
                ]
        else:
            down_ref[number * width : (number + 1) * width, :] = down_w[number][...]
    total_ref[...] = jnp.zeros_like(total_ref)
    dtotal_ref[...] = jnp.zeros_like(dtotal_ref)

    def some_columns(columns):
        gate = project_in(normed_ref, gate_w, columns)
        lift = project_in(normed_ref, lift_w, columns)
        squared = gate * gate
        curve = jnp.tanh(GELU_SCALE * (gate + GELU_CUBE * squared * gate))
        half_up = 0.5 * (1.0 + curve)
        activated = gate * half_up
        product = (activated * lift).astype(LOW)
        down = down_ref[:, columns]
        dproduct = product_plain(grad_ref[...], down).astype(LOW).astype(FULL)
        slope = half_up + 0.5 * gate * (1.0 - curve * curve) * (
            GELU_SCALE * (1.0 + 3.0 * GELU_CUBE * squared)
        )
        dgate = (dproduct * lift * slope).astype(LOW)
        dlift = (dproduct * activated).astype(LOW)
        total_ref[...] += product_right(product, down)
        for number in range(4):
            part = slice(number * width, (number + 1) * width)
            normed_t = normed_t_ref[part, :]
            dgate_w[number][:, columns] = product_plain(normed_t, dgate).astype(LOW)
            dlift_w[number][:, columns] = product_plain(normed_t, dlift).astype(LOW)
            ddown = product_plain(grad_t_ref[part, :], product).astype(LOW)
            if transposed:
                for other in range(4):
                    ddown_w[other][number * block : (number + 1) * block, columns] = ddown[
                        other * block : (other + 1) * block, :
                    ]
            else:
                ddown_w[number][:, columns] = ddown
            dtotal_ref[:, part] += product_right(
                dgate, gate_w[number][:, columns]
            ) + product_right(dlift, lift_w[number][:, columns])

    def one_chunk(chunk, carry):
        some_columns(pl.ds(pl.multiple_of(chunk * CHUNK, CHUNK), CHUNK))
        return carry

    whole = feed // CHUNK
    lax.fori_loop(0, whole, one_chunk, 0)
    if feed % CHUNK:
        some_columns(pl.ds(whole * CHUNK, feed % CHUNK))
    partial_ref[...] = total_ref[...].astype(LOW)
    dnormed_ref[...] = dtotal_ref[...].astype(LOW)


def cross_backward_body(
    hidden_ref,
    mine_ref,
    other_ref,
    gains_ref,
    grad_ref,
    normed_ref,
    memory_ref,
    query_ref,
    key_ref,
    value_ref,
    mixed_ref,
    *refs,
):
    kv, qo = sides(refs[:5])
    grad_out_ref, dgain_ref, dnormed_ref, keep_ref, away_ref = refs[5:10]
    dkv, dqo = sides(refs[10:15])
    low_ref, transposed_ref, dmixed_ref, dquery_ref, dkey_ref, dvalue_ref = refs[15:]
    rows, model = hidden_ref.shape
    width = model // 4
    inner = query_ref.shape[1]
    half = rows // 2
    back, dgain_ref[...] = norm_backward(
        hidden_ref[...], gains_ref[2:3, :], both(mine_ref, other_ref)
    )
    grad = grad_ref[...].astype(FULL) + back
    grad_out_ref[...] = grad
    low_ref[...] = grad.astype(LOW)
    dmixed_ref[...] = project_in(low_ref, qo, slice(inner, 2 * inner)).astype(LOW)
    attention_backward(
        query_ref, key_ref, value_ref, dmixed_ref, dquery_ref, dkey_ref, dvalue_ref
    )
    for number in range(4):
        part = slice(number * width, (number + 1) * width)
        dnormed_ref[:, part] = product_right(dquery_ref[...], qo[number][:, :inner]).astype(LOW)
        partial = (
            product_right(dkey_ref[...], kv[number][:, :inner])
            + product_right(dvalue_ref[...], kv[number][:, inner:])
        ).astype(LOW)
        keep_ref[:, part] = partial[:half]
        away_ref[:, part] = partial[half:]
    transposed_ref[...] = memory_ref[...].T
    for number in range(4):
        part = slice(number * width, (number + 1) * width)
        dkv[number][:, :inner] = product_plain(transposed_ref[part, :], dkey_ref[...]).astype(LOW)
        dkv[number][:, inner:] = product_plain(transposed_ref[part, :], dvalue_ref[...]).astype(
            LOW
        )
    transposed_ref[...] = normed_ref[...].T
    for number in range(4):
        part = slice(number * width, (number + 1) * width)
        dqo[number][:, :inner] = product_plain(transposed_ref[part, :], dquery_ref[...]).astype(
            LOW
        )
    transposed_ref[...] = low_ref[...].T
    for number in range(4):
        part = slice(number * width, (number + 1) * width)
        dqo[number][:, inner:] = product_plain(transposed_ref[part, :], mixed_ref[...]).astype(LOW)


def self_backward_body(
    length_ref,
    bias_ref,
    hidden_ref,
    mine_ref,
    other_ref,
    gains_ref,
    grad_ref,
    normed_ref,
    query_ref,
    key_ref,
    value_ref,
    mixed_ref,
    *refs,
):
    qk, vo = sides(refs[:5])
    grad_out_ref, dgain_ref, dnormed_ref, diagonal_ref = refs[5:9]
    dqk, dvo = sides(refs[9:14])
    low_ref, transposed_ref, dmixed_ref, dquery_ref, dkey_ref, dvalue_ref = refs[14:]
    rows, model = hidden_ref.shape
    width = model // 4
    inner = query_ref.shape[1]
    back, dgain_ref[...] = norm_backward(
        hidden_ref[...], gains_ref[1:2, :], both(mine_ref, other_ref)
    )
    grad = grad_ref[...] + back
    grad_out_ref[...] = grad
    low_ref[...] = grad.astype(LOW)
    dmixed_ref[...] = project_in(low_ref, vo, slice(inner, 2 * inner)).astype(LOW)
    attention_backward(
        query_ref,
        key_ref,
        value_ref,
        dmixed_ref,
        dquery_ref,
        dkey_ref,
        dvalue_ref,
        length_ref,
        bias_ref,
        diagonal_ref,
    )
    for number in range(4):
        part = slice(number * width, (number + 1) * width)
        dnormed_ref[:, part] = (
            product_right(dquery_ref[...], qk[number][:, :inner])
            + product_right(dkey_ref[...], qk[number][:, inner:])
            + product_right(dvalue_ref[...], vo[number][:, :inner])
        ).astype(LOW)
    transposed_ref[...] = normed_ref[...].T
    for number in range(4):
        part = slice(number * width, (number + 1) * width)
        dqk[number][:, :inner] = product_plain(transposed_ref[part, :], dquery_ref[...]).astype(
            LOW
        )
        dqk[number][:, inner:] = product_plain(transposed_ref[part, :], dkey_ref[...]).astype(LOW)
        dvo[number][:, :inner] = product_plain(transposed_ref[part, :], dvalue_ref[...]).astype(
            LOW
        )
    transposed_ref[...] = low_ref[...].T
    for number in range(4):
        part = slice(number * width, (number + 1) * width)
        dvo[number][:, inner:] = product_plain(transposed_ref[part, :], mixed_ref[...]).astype(LOW)


def finish_body(
    length_ref,
    permute_ref,
    input_ref,
    mine_ref,
    other_ref,
    gains_ref,
    grad_ref,
    dgain_cross_ref,
    dgain_feed_ref,
    onehot_ref,
    diagonal_ref,
    out_ref,
    dgains_ref,
    table_ref,
):
    rows = input_ref.shape[0]
    permute = permute_ref[...]
    back, dgain = norm_backward(
        input_ref[...].astype(FULL), gains_ref[0:1, :], both(mine_ref, other_ref)
    )
    total = ((grad_ref[...] + back) * valid_column(length_ref, rows)).astype(LOW)
    out_ref[...] = product_right(total, permute).astype(LOW)
    dgains = jnp.concatenate([dgain, dgain_cross_ref[...], dgain_feed_ref[...]], axis=0)
    high = dgains.astype(LOW)
    middle = (dgains - high.astype(FULL)).astype(LOW)
    low = (dgains - high.astype(FULL) - middle.astype(FULL)).astype(LOW)
    dgains_ref[...] = (
        product_right(high, permute) + product_right(middle, permute)
    ) + product_right(low, permute)
    table_ref[...] = lax.dot_general(
        onehot_ref[...],
        diagonal_ref[...],
        (((1,), (1,)), ((), ())),
        precision=HIGHEST,
        preferred_element_type=FULL,
    )


def output_body(length_ref, permute_ref, hidden_ref, mine_ref, other_ref, out_ref):
    rows = hidden_ref.shape[0]
    total = (hidden_ref[...] + both(mine_ref, other_ref)) * valid_column(length_ref, rows)
    out_ref[...] = product_right(total.astype(LOW), permute_ref[...]).astype(LOW)


def encoder_body(permute_ref, mine_ref, other_ref, out_ref):
    total = both(mine_ref, other_ref).astype(LOW)
    out_ref[...] = product_right(total, permute_ref[...]).astype(LOW)


def fold_body(*refs):
    own, one, two = refs[:3]
    outs = refs[3:]
    width = own.shape[1]
    sides_held = outs[0].shape[1] // width
    block = outs[0].shape[0]
    for side in range(sides_held):
        for place in range(4):
            first = (4 * side + place) * block
            rows = slice(first, first + block)
            total = (
                own[rows, :].astype(FULL) + one[rows, :].astype(FULL) + two[rows, :].astype(FULL)
            )
            outs[place][:, side * width : (side + 1) * width] = total.astype(outs[place].dtype)


def fold_quarter(terms, sides_held):
    rows = terms[0].shape[0] // (4 * sides_held)
    width = terms[0].shape[1] * sides_held
    kinds = [full_shape, full_shape, low_shape, low_shape]
    return call(fold_body, [kind(rows, width) for kind in kinds], (), terms)


def stack_body(*refs):
    parts, outs = refs[:4], refs[4:]
    block = parts[0].shape[0]
    first = 0
    for out in outs:
        width = out.shape[1]
        for side in range(out.shape[0] // (4 * block)):
            for place in range(4):
                row = (4 * side + place) * block
                out[row : row + block, :] = parts[place][:, first : first + width]
            first += width


def stack_quarter(parts, shapes):
    return call(stack_body, [low_shape(*shape) for shape in shapes], (), parts)


def merge_body(x_in, y_in, left, right, x_out, y_out):
    x_out[...] = (x_in[...].astype(FULL) + left[...].astype(FULL)).astype(LOW)
    y_out[...] = (y_in[...].astype(FULL) + right[...].astype(FULL)).astype(LOW)


def merge_quarters(x_part, y_part, left, right):
    rows, width = left.shape
    at = [
        pl.BlockSpec((rows, width), lambda one: (0, 0)),
        pl.BlockSpec((rows, width), lambda one: (1, 0)),
    ]
    whole = pl.BlockSpec((rows, width), lambda one: (0, 0))
    return pl.pallas_call(
        merge_body,
        out_shape=[low_shape(*x_part.shape), low_shape(*y_part.shape)],
        grid=(1,),
        in_specs=at + [whole, whole],
        out_specs=at,
        input_output_aliases={0: 0, 1: 1},
        name="merge_body",
        cost_estimate=pl.CostEstimate(flops=1024, transcendentals=0, bytes_accessed=1024),
    )(x_part, y_part, left, right)


def gather_upper(value, devices, wait=()):
    masks = upper_masks(devices)
    if wait:
        value = after(value, *wait)
    if len(masks) == 2:
        one = swap_dp(value, masks[0], devices)
        two = swap_dp(value, masks[1], devices)
        return [value, one, two, swap_dp(one, masks[1], devices)]
    for mask in masks:
        value = jnp.concatenate([value, swap_dp(value, mask, devices)], axis=0)
    return [value]


def stack_sides(blocks, widths):
    if len(blocks) == 4:
        rows = 4 * blocks[0].shape[0]
        return stack_quarter(blocks, [(2 * rows, width) for width in widths])
    groups, first = [], 0
    for width in widths:
        middle, last = first + width, first + 2 * width
        groups.append(
            jnp.concatenate([blocks[0][:, first:middle], blocks[0][:, middle:last]], axis=0)
        )
        first = last
    return groups


def gather_lower(first, devices, x_wait=(), y_wait=(), last_wait=()):
    rows = first.shape[0] // 2
    x_part = swap_dp(after(first, *x_wait) if x_wait else first, 1, devices)
    y_part = swap_dp(after(first, *y_wait) if y_wait else first, 2, devices)
    left, right = x_part[:rows], y_part[rows:]
    if last_wait:
        left, right = after(left, *last_wait), after(right, *last_wait)
    return [first, x_part, y_part, swap_dp(left, 2, devices), swap_dp(right, 1, devices)]


def reduce_last(pieces, devices, wait=()):
    left, right = pieces[3:]
    if wait:
        left, right = after(left, *wait), after(right, *wait)
    return [swap_dp(left, 2, devices), swap_dp(right, 1, devices)]


def reduce_lower(pieces, came, devices, wait=()):
    x_part, y_part = merge_quarters(*pieces[1:3], *came)
    if wait:
        x_part, y_part = after(x_part, *wait), after(y_part, *wait)
    return [pieces[0], swap_dp(x_part, 1, devices), swap_dp(y_part, 2, devices)]


def reduce_upper(terms, devices, wait=()):
    masks = upper_masks(devices)
    if len(masks) == 2:
        own, one, two, three = fold_quarter(terms, 2)
        if wait:
            two, three = after(two, *wait), after(three, *wait)
        one = (one + swap_dp(three, masks[1], devices).astype(FULL)).astype(LOW)
        two = swap_dp(two, masks[1], devices)
        return own + two.astype(FULL) + swap_dp(one, masks[0], devices).astype(FULL)
    value = terms[0].astype(FULL) + terms[1].astype(FULL) + terms[2].astype(FULL)
    rows = value.shape[0] // 2
    value = jnp.concatenate([value[:rows], value[rows:]], axis=1)
    for mask in masks[::-1]:
        half = value.shape[0] // 2
        away = swap_dp(value[half:].astype(LOW), mask, devices)
        value = value[:half] + away.astype(FULL)
    return value


def first_across(value, devices):
    x_part, y_part = swap_dp(value, 1, devices), swap_dp(value, 2, devices)
    return [value, x_part, y_part, swap_dp(x_part, 2, devices)]


def gather_across(blocks, devices, wait):
    masks = upper_masks(devices)
    rows, width = blocks[0].shape
    first = after(stack_quarter(blocks, [(4 * rows, width)])[0], *wait)
    one, two = swap_dp(first, masks[0], devices), swap_dp(first, masks[1], devices)
    return [first, one, two, swap_dp(one, masks[1], devices)]


def reduce_across_last(pieces, devices):
    mask = upper_masks(devices)[1]
    return [swap_dp(pieces[3], mask, devices), swap_dp(pieces[2], mask, devices)]


def reduce_across(pieces, came, devices):
    mask = upper_masks(devices)[0]
    one = (pieces[1].astype(FULL) + came[0].astype(FULL)).astype(LOW)
    return [pieces[0], came[1], swap_dp(one, mask, devices)]


def reduce_across_first(terms, devices):
    own, x_part, y_part, last = fold_quarter(terms, 1)
    x_part = (x_part + swap_dp(last, 2, devices).astype(FULL)).astype(LOW)
    return (
        own
        + swap_dp(y_part, 2, devices).astype(FULL)
        + swap_dp(x_part, 1, devices).astype(FULL)
    )


def deal(value, order, devices):
    rows, width = value.shape
    first = lax.all_to_all(
        value.reshape(devices, rows // devices, width), "dp", split_axis=0, concat_axis=0, tiled=True
    )
    second = lax.all_to_all(
        jnp.take(first, order, axis=0), "dp", split_axis=0, concat_axis=0, tiled=True
    )
    return second.reshape(rows, width)


def on_device(
    tokens,
    encoder_states,
    cotangent,
    lengths,
    deal_order,
    bucket_index,
    rel_table,
    gain_self,
    self_query,
    self_key,
    self_value,
    self_output,
    gain_cross,
    cross_query,
    cross_key,
    cross_value,
    cross_output,
    gain_feed,
    feed_gate,
    feed_value,
    feed_output,
):
    devices = lax.axis_size("dp")
    myself = lax.axis_index("dp")
    core = lax.axis_index("tensor")
    rows, model = tokens.shape
    block = model // devices
    buckets, heads = rel_table.shape
    inner = self_query.shape[1]
    feed = feed_gate.shape[1]
    across = devices == 16

    numbers = jnp.arange(devices, dtype=jnp.int32)
    owner_of = jnp.sum(
        jnp.where(deal_order[:, None] == numbers[None, :], numbers[:, None], 0), axis=0
    )
    length = jnp.sum(jnp.where(numbers == myself, lengths, 0)).reshape(1)

    self_own = jnp.concatenate([self_query, self_key, self_value, self_output], axis=1)
    cross_own = jnp.concatenate([cross_key, cross_value, cross_query, cross_output], axis=1)
    feed_own = jnp.concatenate([feed_gate, feed_value], axis=1)
    self_blocks = gather_upper(self_own, devices)
    if across:
        down_blocks = first_across(feed_output, devices)
        self_blocks[3] = after(self_blocks[3], *down_blocks[1:3])
    (self_first,) = stack_sides(self_blocks, [2 * inner])
    cross_blocks = gather_upper(cross_own, devices, self_blocks[1:3])
    self_w = gather_lower(self_first, devices)
    (cross_first,) = stack_sides(cross_blocks, [2 * inner])
    cross_w = gather_lower(cross_first, devices, self_w[1:2], self_w[2:3])
    feed_blocks = gather_upper(feed_own, devices, cross_blocks[1:3])
    (feed_first,) = stack_sides(feed_blocks, [feed])
    if across:
        down = gather_across(down_blocks, devices, feed_blocks[1:3])
    else:
        down = gather_upper(feed_output, devices)[0]
        width = feed // 2
        down = gather_lower(
            jnp.concatenate([down[:, :width], down[:, width:]], axis=0), devices
        )
        middle = down[0].shape[0] // 2
        down = [
            jnp.concatenate([one[:middle], one[middle:]], axis=1) for one in down[:3]
        ] + [jnp.concatenate(down[3:], axis=1)]

    offsets = jnp.asarray(np.array(block_offsets(upper_masks(devices) + [1, 2]), np.int32))
    source = (
        ((myself ^ offsets) * block)[:, None] + jnp.arange(block, dtype=jnp.int32)[None, :]
    ).reshape(1, -1)
    permute, masked_input, grad_three, gains, normed_self = call(
        prepare_body,
        [
            low_shape(model, model),
            low_shape(rows, model),
            low_shape(rows, model),
            full_shape(3, model),
            low_shape(rows, model),
        ],
        (length,),
        (tokens, cotangent, jnp.stack([gain_self, gain_cross, gain_feed]), source),
        flops=4 * rows * model * model,
    )

    half = rows // 2
    memory_half = deal(
        lax.dynamic_slice_in_dim(encoder_states, core * half, half, axis=0), deal_order, devices
    )
    memory_other = swap_tensor(memory_half)

    skewed_bucket = jnp.concatenate(
        [bucket_index[:1], jnp.full((rows,), -1, jnp.int32), bucket_index[::-1][: rows - 1]]
    )
    onehot = (jnp.arange(buckets, dtype=jnp.int32)[:, None] == skewed_bucket[None, :]).astype(FULL)
    bias_rows = jnp.dot(rel_table.T, onehot, precision=HIGHEST)

    unit = 2 * rows * model * inner
    query_self, key_self, value_self, mixed_self, self_partial = call(
        self_forward_body,
        [low_shape(rows, inner)] * 4 + [low_shape(rows, model)],
        (length,),
        (bias_rows, normed_self, *self_w),
        flops=5 * unit,
    )
    memory, key_cross, value_cross = call(
        memory_body,
        [low_shape(rows, model)] + [low_shape(rows, inner)] * 2,
        (),
        (memory_half, memory_other, permute, *cross_w),
        flops=4 * unit,
    )
    hidden_one, normed_cross, query_cross, mixed_cross, partial = call(
        cross_forward_body,
        [full_shape(rows, model), low_shape(rows, model)]
        + [low_shape(rows, inner)] * 2
        + [low_shape(rows, model)],
        (),
        (
            masked_input,
            self_partial,
            swap_tensor(self_partial),
            gains,
            key_cross,
            value_cross,
            *cross_w,
        ),
        flops=3 * unit,
    )
    quarter_rows = model // 4
    feed_w = gather_lower(
        feed_first,
        devices,
        (cross_w[1], self_partial),
        (cross_w[2], self_partial),
        (partial,),
    )

    def group_shapes(width):
        return [low_shape(2 * quarter_rows, width)] * 3 + [low_shape(quarter_rows, width)] * 2

    feed_grads = group_shapes(feed) + [low_shape(quarter_rows, feed)] * 4
    outs = call(
        functools.partial(feed_body, across),
        [full_shape(rows, model), low_shape(rows, model), low_shape(rows, model)] + feed_grads,
        (),
        (hidden_one, partial, swap_tensor(partial), gains, grad_three, *feed_w, *down),
        scratch=[
            pltpu.VMEM((rows, model), LOW),
            pltpu.VMEM((model, rows), LOW),
            pltpu.VMEM((model, rows), LOW),
            pltpu.VMEM((model, feed), LOW),
            pltpu.VMEM((rows, model), FULL),
            pltpu.VMEM((rows, model), FULL),
        ],
        flops=18 * rows * model * feed,
    )
    hidden_two, partial, dpartial = outs[:3]
    dfeed, ddown = outs[3:8], outs[8:12]
    feed_came = reduce_last(dfeed, devices)
    if across:
        down_came = reduce_across_last(ddown, devices)
    else:
        width = feed // 2
        ddown = [
            jnp.concatenate([one[:, :width], one[:, width:]], axis=0) for one in ddown[:3]
        ] + [ddown[3][:, :width], ddown[3][:, width:]]
        down_came = reduce_last(ddown, devices)
    (layer_result,) = call(
        output_body,
        [low_shape(rows, model)],
        (length,),
        (permute, hidden_two, partial, swap_tensor(partial)),
        flops=2 * unit,
    )

    attention_scratch = [
        pltpu.VMEM((rows, model), LOW),
        pltpu.VMEM((model, rows), LOW),
    ] + [pltpu.VMEM((rows, inner), LOW)] * 4
    outs = call(
        cross_backward_body,
        [
            full_shape(rows, model),
            full_shape(1, model),
            low_shape(rows, model),
            low_shape(half, model),
            low_shape(half, model),
        ]
        + group_shapes(2 * inner),
        (),
        (
            hidden_two,
            dpartial,
            swap_tensor(dpartial),
            gains,
            grad_three,
            normed_cross,
            memory,
            query_cross,
            key_cross,
            value_cross,
            mixed_cross,
            *cross_w,
        ),
        scratch=attention_scratch,
        flops=9 * unit,
    )
    grad_two, dgain_feed, dpartial, keep, away = outs[:5]
    dcross = outs[5:10]
    feed_terms = reduce_lower(
        dfeed, [after(one, dpartial) for one in feed_came], devices
    )
    cross_came = reduce_last(dcross, devices, down_came[:1])
    cross_terms = reduce_lower(dcross, cross_came, devices, feed_terms[1:])
    (encoder_half,) = call(
        encoder_body,
        [low_shape(half, model)],
        (),
        (permute, keep, swap_tensor(away)),
        flops=unit,
    )
    encoder_grad = deal(encoder_half, owner_of, devices)

    outs = call(
        self_backward_body,
        [
            full_shape(rows, model),
            full_shape(1, model),
            low_shape(rows, model),
            full_shape(heads, 2 * rows),
        ]
        + group_shapes(2 * inner),
        (length,),
        (
            bias_rows,
            hidden_one,
            dpartial,
            swap_tensor(dpartial),
            gains,
            after(grad_two, *feed_came),
            normed_self,
            query_self,
            key_self,
            value_self,
            mixed_self,
            *self_w,
        ),
        scratch=attention_scratch,
        flops=10 * unit,
    )
    grad_one, dgain_cross, dpartial, diagonal = outs[:4]
    dself = outs[4:9]
    self_came = reduce_last(dself, devices, feed_terms[1:])
    self_terms = reduce_lower(dself, self_came, devices, cross_terms[1:])
    input_grad, dgains, dtable = call(
        finish_body,
        [low_shape(rows, model), full_shape(3, model), full_shape(buckets, heads)],
        (length,),
        (
            permute,
            masked_input,
            dpartial,
            swap_tensor(dpartial),
            gains,
            grad_one,
            dgain_cross,
            dgain_feed,
            onehot,
            diagonal,
        ),
        flops=2 * unit,
    )

    if across:
        down_terms = reduce_across(ddown, down_came, devices)
        feed_sums = reduce_upper(feed_terms, devices, down_terms[2:])
        down_sum = reduce_across_first(down_terms, devices)
    else:
        down_sum = reduce_upper(reduce_lower(ddown, down_came, devices), devices)
        feed_sums = reduce_upper(feed_terms, devices)
    cross_sums = reduce_upper(cross_terms, devices, (feed_sums,))
    self_sums = reduce_upper(self_terms, devices, (cross_sums,))
    small = total_small(
        jnp.concatenate([dgains.reshape(-1), dtable.reshape(-1)]).reshape(-1, 128), devices
    ).reshape(-1)
    gain_sums = small[: 3 * model].reshape(3, model)
    table_sum = small[3 * model :].reshape(buckets, heads)

    def column(value, number, width):
        return value[:, number * width : (number + 1) * width]

    return (
        layer_result,
        input_grad,
        encoder_grad,
        table_sum,
        gain_sums[0],
        column(self_sums, 0, inner),
        column(self_sums, 1, inner),
        column(self_sums, 2, inner),
        column(self_sums, 3, inner),
        gain_sums[1],
        column(cross_sums, 2, inner),
        column(cross_sums, 0, inner),
        column(cross_sums, 1, inner),
        column(cross_sums, 3, inner),
        gain_sums[2],
        column(feed_sums, 0, feed),
        column(feed_sums, 1, feed),
        down_sum,
    )


def solution(mesh):
    in_specs = (
        P("dp", None),
        P("dp", None),
        P("dp", None),
        P(),
        P(),
        P(),
        P(None, "tensor"),
        P(),
        P("dp", "tensor"),
        P("dp", "tensor"),
        P("dp", "tensor"),
        P("dp", "tensor"),
        P(),
        P("dp", "tensor"),
        P("dp", "tensor"),
        P("dp", "tensor"),
        P("dp", "tensor"),
        P(),
        P("dp", "tensor"),
        P("dp", "tensor"),
        P("dp", "tensor"),
    )
    out_specs = (
        P("dp", None),
        P("dp", None),
        P(("dp", "tensor"), None),
        P(None, "tensor"),
        P(),
        P("dp", "tensor"),
        P("dp", "tensor"),
        P("dp", "tensor"),
        P("dp", "tensor"),
        P(),
        P("dp", "tensor"),
        P("dp", "tensor"),
        P("dp", "tensor"),
        P("dp", "tensor"),
        P(),
        P("dp", "tensor"),
        P("dp", "tensor"),
        P("dp", "tensor"),
    )
    return jax.shard_map(
        on_device, mesh=mesh, in_specs=in_specs, out_specs=out_specs, check_vma=False
    )
```

```python
import functools

import jax
import jax.numpy as jnp
import numpy as np
from jax import lax
from jax.experimental import pallas as pl
from jax.experimental.pallas import tpu as pltpu
from jax.sharding import PartitionSpec as P

EPSILON = 1e-06
MASKED = -1e30
HIGHEST = lax.Precision.HIGHEST
HEAD = 64
PAIR = 2 * HEAD
LOW = jnp.bfloat16
FULL = jnp.float32


def upper_masks(devices):
    if devices == 16:
        return [12, 4]
    return [1 << bit for bit in range(devices.bit_length() - 2, 1, -1)]


def block_offsets(masks):
    offsets = [0]
    for mask in masks:
        offsets = offsets + [offset ^ mask for offset in offsets]
    return offsets


def swap_dp(value, mask, devices):
    return lax.ppermute(value, "dp", [(one, one ^ mask) for one in range(devices)])


def swap_tensor(value):
    return lax.ppermute(value, "tensor", [(0, 1), (1, 0)])


def total_small(value, devices):
    mask = 1
    while mask < devices:
        value = value + swap_dp(value, mask, devices)
        mask = 2 * mask
    return value


def product_plain(left, right):
    return jnp.dot(left, right, preferred_element_type=FULL)


def product_right(left, right):
    return lax.dot_general(left, right, (((1,), (1,)), ((), ())), preferred_element_type=FULL)


def product_left(left, right):
    return lax.dot_general(left, right, (((0,), (0,)), ((), ())), preferred_element_type=FULL)


def quarter(ref, number):
    width = ref.shape[1] // 4
    return ref[:, number * width : (number + 1) * width]


def sides(refs):
    own, x_part, y_part, left, right = refs
    rows = left.shape[0]
    return (
        [own.at[:rows], x_part.at[:rows], y_part.at[:rows], left],
        [own.at[rows:], x_part.at[rows:], y_part.at[rows:], right],
    )


def after(value, *earlier):
    return lax.optimization_barrier((value, *earlier))[0]


def project_in(value_ref, pieces, columns):
    total = None
    for number, piece in enumerate(pieces):
        part = product_plain(quarter(value_ref, number), piece[:, columns])
        total = part if total is None else total + part
    return total


def inverse_root(value):
    return lax.rsqrt(jnp.mean(value * value, axis=-1, keepdims=True) + EPSILON)


def norm_backward(value, gain, upstream):
    root = inverse_root(value)
    weighted = upstream * gain
    inner_mean = jnp.mean(weighted * value, axis=-1, keepdims=True)
    grad = root * weighted - value * (root * root * root) * inner_mean
    return grad, jnp.sum(upstream * value * root, axis=0, keepdims=True)


def both(mine_ref, other_ref):
    return mine_ref[...].astype(FULL) + other_ref[...].astype(FULL)


def valid_column(length_ref, rows):
    return (lax.broadcasted_iota(jnp.int32, (rows, 1), 0) < length_ref[0]).astype(FULL)


def toeplitz_bias(row, rows):
    wide = jnp.broadcast_to(row, (rows, row.shape[1]))
    return pltpu.roll(wide, 0, 1, stride=1, stride_axis=0)[:, :rows]


def head_half(value, side, lanes):
    keep = lanes < HEAD if side == 0 else lanes >= HEAD
    return jnp.where(keep, value, jnp.zeros_like(value))


def masked_scores(query, key, length_ref, bias_ref, head):
    scores = product_right(query, key)
    if bias_ref is None:
        return scores
    rows, columns = scores.shape
    scores = scores + toeplitz_bias(bias_ref[pl.ds(head, 1), :], rows)
    at_row = lax.broadcasted_iota(jnp.int32, (rows, columns), 0)
    at_column = lax.broadcasted_iota(jnp.int32, (rows, columns), 1)
    allowed = (at_column <= at_row) & (at_column < length_ref[0])
    return jnp.where(allowed, scores, MASKED)


def softmax_rows(scores):
    exponent = jnp.exp(scores - jnp.max(scores, axis=-1, keepdims=True))
    return exponent / jnp.sum(exponent, axis=-1, keepdims=True)


def attention_forward(query_ref, key_ref, value_ref, out_ref, length_ref=None, bias_ref=None):
    rows, width = query_ref.shape
    lanes = lax.broadcasted_iota(jnp.int32, (rows, PAIR), 1)

    def one_pair(pair, carry):
        columns = pl.ds(pl.multiple_of(pair * PAIR, PAIR), PAIR)
        query, key, value = query_ref[:, columns], key_ref[:, columns], value_ref[:, columns]
        mixed = []
        for side in range(2):
            scores = masked_scores(
                head_half(query, side, lanes), key, length_ref, bias_ref, 2 * pair + side
            )
            mixed.append(product_plain(softmax_rows(scores).astype(LOW), value))
        out_ref[:, columns] = jnp.where(lanes < HEAD, mixed[0], mixed[1]).astype(LOW)
        return carry

    lax.fori_loop(0, width // PAIR, one_pair, 0)


def attention_backward(
    query_ref,
    key_ref,
    value_ref,
    grad_ref,
    dquery_ref,
    dkey_ref,
    dvalue_ref,
    length_ref=None,
    bias_ref=None,
    diagonal_ref=None,
):
    rows, width = query_ref.shape
    lanes = lax.broadcasted_iota(jnp.int32, (rows, PAIR), 1)
    if bias_ref is not None:
        flip = (
            lax.broadcasted_iota(jnp.int32, (rows, rows), 0)
            + lax.broadcasted_iota(jnp.int32, (rows, rows), 1)
            == rows - 1
        ).astype(LOW)

    def one_pair(pair, carry):
        columns = pl.ds(pl.multiple_of(pair * PAIR, PAIR), PAIR)
        query, key, value = query_ref[:, columns], key_ref[:, columns], value_ref[:, columns]
        grad = grad_ref[:, columns]
        dquery, dkey, dvalue = [], [], []
        for side in range(2):
            head = 2 * pair + side
            scores = masked_scores(head_half(query, side, lanes), key, length_ref, bias_ref, head)
            chance = softmax_rows(scores)
            chance_grad = product_right(head_half(grad, side, lanes), value)
            delta = jnp.sum(chance * chance_grad, axis=-1, keepdims=True)
            score_grad = (chance * (chance_grad - delta)).astype(LOW)
            dquery.append(product_plain(score_grad, key))
            dkey.append(product_left(score_grad, query))
            dvalue.append(product_left(chance.astype(LOW), grad))
            if bias_ref is not None:
                flipped = product_plain(flip, score_grad)
                wide = jnp.concatenate([flipped, jnp.zeros_like(flipped)], axis=1)
                skewed = pltpu.roll(wide, rows + 1, 1, stride=1, stride_axis=0)
                diagonal_ref[pl.ds(head, 1), :] = jnp.sum(skewed, axis=0, keepdims=True)
        left = lanes < HEAD
        dquery_ref[:, columns] = jnp.where(left, dquery[0], dquery[1]).astype(LOW)
        dkey_ref[:, columns] = jnp.where(left, dkey[0], dkey[1]).astype(LOW)
        dvalue_ref[:, columns] = jnp.where(left, dvalue[0], dvalue[1]).astype(LOW)
        return carry

    lax.fori_loop(0, width // PAIR, one_pair, 0)


def low_shape(*shape):
    return jax.ShapeDtypeStruct(shape, LOW)


def full_shape(*shape):
    return jax.ShapeDtypeStruct(shape, FULL)


def call(body, out_shape, scalars, arrays, scratch=(), flops=0, sent=()):
    vmem = pl.BlockSpec(memory_space=pltpu.VMEM)
    smem = pl.BlockSpec(memory_space=pltpu.SMEM)
    return pl.pallas_call(
        body,
        out_shape=list(out_shape),
        in_specs=[smem] * len(scalars) + [vmem] * len(arrays),
        out_specs=[
            pl.BlockSpec(one.shape, lambda step: (0, 0), pipeline_mode=pl.Buffered(1))
            if number in sent
            else vmem
            for number, one in enumerate(out_shape)
        ],
        grid=(1,) if sent else (),
        scratch_shapes=list(scratch),
        name=getattr(body, "func", body).__name__,
        cost_estimate=pl.CostEstimate(
            flops=int(flops * 1), transcendentals=0, bytes_accessed=1024
        ),
        compiler_params=pltpu.CompilerParams(vmem_limit_bytes=44 << 20),
    )(*scalars, *arrays)


def prepare_body(
    length_ref,
    tokens_ref,
    cotangent_ref,
    gains_ref,
    source_ref,
    permute_ref,
    input_ref,
    grad_ref,
    gains_out_ref,
    normed_ref,
):
    rows, width = tokens_ref.shape
    at_row = lax.broadcasted_iota(jnp.int32, (width, width), 0)
    permute_ref[...] = (at_row == source_ref[...]).astype(FULL).astype(LOW)
    permute = permute_ref[...]
    valid = valid_column(length_ref, rows)
    masked = product_plain(tokens_ref[...], permute) * valid
    input_ref[...] = masked.astype(LOW)
    grad_ref[...] = (product_plain(cotangent_ref[...], permute) * valid).astype(LOW)
    gains = gains_ref[...]
    high = gains.astype(LOW)
    middle = (gains - high.astype(FULL)).astype(LOW)
    low = (gains - high.astype(FULL) - middle.astype(FULL)).astype(LOW)
    gains_out_ref[...] = (
        product_plain(high, permute) + product_plain(middle, permute)
    ) + product_plain(low, permute)
    normed_ref[...] = (masked * inverse_root(masked) * gains_out_ref[0:1, :]).astype(LOW)


def self_forward_body(
    length_ref, bias_ref, normed_ref, *refs
):
    qk, vo = sides(refs[:5])
    query_ref, key_ref, value_ref, mixed_ref, partial_ref = refs[5:]
    inner = query_ref.shape[1]
    query_ref[...] = project_in(normed_ref, qk, slice(0, inner)).astype(LOW)
    key_ref[...] = project_in(normed_ref, qk, slice(inner, 2 * inner)).astype(LOW)
    value_ref[...] = project_in(normed_ref, vo, slice(0, inner)).astype(LOW)
    attention_forward(query_ref, key_ref, value_ref, mixed_ref, length_ref, bias_ref)
    width = partial_ref.shape[1] // 4
    for number in range(4):
        partial_ref[:, number * width : (number + 1) * width] = product_right(
            mixed_ref[...], vo[number][:, inner:]
        ).astype(LOW)


def memory_body(half_ref, other_ref, permute_ref, *refs):
    kv, _ = sides(refs[:5])
    memory_ref, key_ref, value_ref = refs[5:]
    inner = key_ref.shape[1]
    half = half_ref.shape[0]
    memory_ref[:half, :] = product_plain(half_ref[...], permute_ref[...]).astype(LOW)
    memory_ref[half:, :] = product_plain(other_ref[...], permute_ref[...]).astype(LOW)
    key_ref[...] = project_in(memory_ref, kv, slice(0, inner)).astype(LOW)
    value_ref[...] = project_in(memory_ref, kv, slice(inner, 2 * inner)).astype(LOW)


def cross_forward_body(input_ref, mine_ref, other_ref, gains_ref, key_ref, value_ref, *refs):
    _, qo = sides(refs[:5])
    hidden_ref, normed_ref, query_ref, mixed_ref, partial_ref = refs[5:]
    inner = query_ref.shape[1]
    hidden = input_ref[...].astype(FULL) + both(mine_ref, other_ref)
    hidden_ref[...] = hidden
    normed_ref[...] = (hidden * inverse_root(hidden) * gains_ref[1:2, :]).astype(LOW)
    query_ref[...] = project_in(normed_ref, qo, slice(0, inner)).astype(LOW)
    attention_forward(query_ref, key_ref, value_ref, mixed_ref)
    width = partial_ref.shape[1] // 4
    for number in range(4):
        partial_ref[:, number * width : (number + 1) * width] = product_right(
            mixed_ref[...], qo[number][:, inner:]
        ).astype(LOW)


GELU_SCALE = float(np.sqrt(2.0 / np.pi))
GELU_CUBE = 0.044715
CHUNK = 256


def feed_body(transposed, hidden_in_ref, mine_ref, other_ref, gains_ref, grad_ref, *refs):
    gate_w, lift_w = sides(refs[:5])
    down_w = refs[5:9]
    hidden_ref, partial_ref, dnormed_ref = refs[9:12]
    dgate_w, dlift_w = sides(refs[12:17])
    ddown_w = refs[17:21]
    normed_ref, normed_t_ref, grad_t_ref, down_ref, total_ref, dtotal_ref = refs[21:]
    rows, model = hidden_ref.shape
    width = model // 4
    block = width // 4
    feed = gate_w[0].shape[1]
    hidden = hidden_in_ref[...] + both(mine_ref, other_ref)
    hidden_ref[...] = hidden
    normed_ref[...] = (hidden * inverse_root(hidden) * gains_ref[2:3, :]).astype(LOW)
    normed_t_ref[...] = normed_ref[...].T
    grad_t_ref[...] = grad_ref[...].T
    for number in range(4):
        if transposed:
            for other in range(4):
                place = number * width + other * block
                down_ref[place : place + block, :] = down_w[other][
                    number * block : (number + 1) * block, :
                ]
        else:
            down_ref[number * width : (number + 1) * width, :] = down_w[number][...]
    total_ref[...] = jnp.zeros_like(total_ref)
    dtotal_ref[...] = jnp.zeros_like(dtotal_ref)

    def some_columns(columns):
        gate = project_in(normed_ref, gate_w, columns)
        lift = project_in(normed_ref, lift_w, columns)
        squared = gate * gate
        curve = jnp.tanh(GELU_SCALE * (gate + GELU_CUBE * squared * gate))
        half_up = 0.5 * (1.0 + curve)
        activated = gate * half_up
        product = (activated * lift).astype(LOW)
        down = down_ref[:, columns]
        dproduct = product_plain(grad_ref[...], down).astype(LOW).astype(FULL)
        slope = half_up + 0.5 * gate * (1.0 - curve * curve) * (
            GELU_SCALE * (1.0 + 3.0 * GELU_CUBE * squared)
        )
        dgate = (dproduct * lift * slope).astype(LOW)
        dlift = (dproduct * activated).astype(LOW)
        total_ref[...] += product_right(product, down)
        for number in range(4):
            part = slice(number * width, (number + 1) * width)
            normed_t = normed_t_ref[part, :]
            dgate_w[number][:, columns] = product_plain(normed_t, dgate).astype(LOW)
            dlift_w[number][:, columns] = product_plain(normed_t, dlift).astype(LOW)
            ddown = product_plain(grad_t_ref[part, :], product).astype(LOW)
            if transposed:
                for other in range(4):
                    ddown_w[other][number * block : (number + 1) * block, columns] = ddown[
                        other * block : (other + 1) * block, :
                    ]
            else:
                ddown_w[number][:, columns] = ddown
            dtotal_ref[:, part] += product_right(
                dgate, gate_w[number][:, columns]
            ) + product_right(dlift, lift_w[number][:, columns])

    def one_chunk(chunk, carry):
        some_columns(pl.ds(pl.multiple_of(chunk * CHUNK, CHUNK), CHUNK))
        return carry

    whole = feed // CHUNK
    lax.fori_loop(0, whole, one_chunk, 0)
    if feed % CHUNK:
        some_columns(pl.ds(whole * CHUNK, feed % CHUNK))
    partial_ref[...] = total_ref[...].astype(LOW)
    dnormed_ref[...] = dtotal_ref[...].astype(LOW)


def cross_backward_body(
    hidden_ref,
    mine_ref,
    other_ref,
    gains_ref,
    grad_ref,
    normed_ref,
    memory_ref,
    query_ref,
    key_ref,
    value_ref,
    mixed_ref,
    *refs,
):
    kv, qo = sides(refs[:5])
    grad_out_ref, dgain_ref, dnormed_ref, keep_ref, away_ref = refs[5:10]
    dkv, dqo = sides(refs[10:15])
    low_ref, transposed_ref, dmixed_ref, dquery_ref, dkey_ref, dvalue_ref = refs[15:]
    rows, model = hidden_ref.shape
    width = model // 4
    inner = query_ref.shape[1]
    half = rows // 2
    back, dgain_ref[...] = norm_backward(
        hidden_ref[...], gains_ref[2:3, :], both(mine_ref, other_ref)
    )
    grad = grad_ref[...].astype(FULL) + back
    grad_out_ref[...] = grad
    low_ref[...] = grad.astype(LOW)
    dmixed_ref[...] = project_in(low_ref, qo, slice(inner, 2 * inner)).astype(LOW)
    attention_backward(
        query_ref, key_ref, value_ref, dmixed_ref, dquery_ref, dkey_ref, dvalue_ref
    )
    for number in range(4):
        part = slice(number * width, (number + 1) * width)
        dnormed_ref[:, part] = product_right(dquery_ref[...], qo[number][:, :inner]).astype(LOW)
        partial = (
            product_right(dkey_ref[...], kv[number][:, :inner])
            + product_right(dvalue_ref[...], kv[number][:, inner:])
        ).astype(LOW)
        keep_ref[:, part] = partial[:half]
        away_ref[:, part] = partial[half:]
    transposed_ref[...] = memory_ref[...].T
    for number in range(4):
        part = slice(number * width, (number + 1) * width)
        dkv[number][:, :inner] = product_plain(transposed_ref[part, :], dkey_ref[...]).astype(LOW)
        dkv[number][:, inner:] = product_plain(transposed_ref[part, :], dvalue_ref[...]).astype(
            LOW
        )
    transposed_ref[...] = normed_ref[...].T
    for number in range(4):
        part = slice(number * width, (number + 1) * width)
        dqo[number][:, :inner] = product_plain(transposed_ref[part, :], dquery_ref[...]).astype(
            LOW
        )
    transposed_ref[...] = low_ref[...].T
    for number in range(4):
        part = slice(number * width, (number + 1) * width)
        dqo[number][:, inner:] = product_plain(transposed_ref[part, :], mixed_ref[...]).astype(LOW)


def self_backward_body(
    length_ref,
    bias_ref,
    hidden_ref,
    mine_ref,
    other_ref,
    gains_ref,
    grad_ref,
    normed_ref,
    query_ref,
    key_ref,
    value_ref,
    mixed_ref,
    *refs,
):
    qk, vo = sides(refs[:5])
    grad_out_ref, dgain_ref, dnormed_ref, diagonal_ref = refs[5:9]
    dqk, dvo = sides(refs[9:14])
    low_ref, transposed_ref, dmixed_ref, dquery_ref, dkey_ref, dvalue_ref = refs[14:]
    rows, model = hidden_ref.shape
    width = model // 4
    inner = query_ref.shape[1]
    back, dgain_ref[...] = norm_backward(
        hidden_ref[...], gains_ref[1:2, :], both(mine_ref, other_ref)
    )
    grad = grad_ref[...] + back
    grad_out_ref[...] = grad
    low_ref[...] = grad.astype(LOW)
    dmixed_ref[...] = project_in(low_ref, vo, slice(inner, 2 * inner)).astype(LOW)
    attention_backward(
        query_ref,
        key_ref,
        value_ref,
        dmixed_ref,
        dquery_ref,
        dkey_ref,
        dvalue_ref,
        length_ref,
        bias_ref,
        diagonal_ref,
    )
    for number in range(4):
        part = slice(number * width, (number + 1) * width)
        dnormed_ref[:, part] = (
            product_right(dquery_ref[...], qk[number][:, :inner])
            + product_right(dkey_ref[...], qk[number][:, inner:])
            + product_right(dvalue_ref[...], vo[number][:, :inner])
        ).astype(LOW)
    transposed_ref[...] = normed_ref[...].T
    for number in range(4):
        part = slice(number * width, (number + 1) * width)
        dqk[number][:, :inner] = product_plain(transposed_ref[part, :], dquery_ref[...]).astype(
            LOW
        )
        dqk[number][:, inner:] = product_plain(transposed_ref[part, :], dkey_ref[...]).astype(LOW)
        dvo[number][:, :inner] = product_plain(transposed_ref[part, :], dvalue_ref[...]).astype(
            LOW
        )
    transposed_ref[...] = low_ref[...].T
    for number in range(4):
        part = slice(number * width, (number + 1) * width)
        dvo[number][:, inner:] = product_plain(transposed_ref[part, :], mixed_ref[...]).astype(LOW)


def finish_body(
    length_ref,
    permute_ref,
    input_ref,
    mine_ref,
    other_ref,
    gains_ref,
    grad_ref,
    dgain_cross_ref,
    dgain_feed_ref,
    onehot_ref,
    diagonal_ref,
    out_ref,
    dgains_ref,
    table_ref,
):
    rows = input_ref.shape[0]
    permute = permute_ref[...]
    back, dgain = norm_backward(
        input_ref[...].astype(FULL), gains_ref[0:1, :], both(mine_ref, other_ref)
    )
    total = ((grad_ref[...] + back) * valid_column(length_ref, rows)).astype(LOW)
    out_ref[...] = product_right(total, permute).astype(LOW)
    dgains = jnp.concatenate([dgain, dgain_cross_ref[...], dgain_feed_ref[...]], axis=0)
    high = dgains.astype(LOW)
    middle = (dgains - high.astype(FULL)).astype(LOW)
    low = (dgains - high.astype(FULL) - middle.astype(FULL)).astype(LOW)
    dgains_ref[...] = (
        product_right(high, permute) + product_right(middle, permute)
    ) + product_right(low, permute)
    table_ref[...] = lax.dot_general(
        onehot_ref[...],
        diagonal_ref[...],
        (((1,), (1,)), ((), ())),
        precision=HIGHEST,
        preferred_element_type=FULL,
    )


def output_body(length_ref, permute_ref, hidden_ref, mine_ref, other_ref, out_ref):
    rows = hidden_ref.shape[0]
    total = (hidden_ref[...] + both(mine_ref, other_ref)) * valid_column(length_ref, rows)
    out_ref[...] = product_right(total.astype(LOW), permute_ref[...]).astype(LOW)


def encoder_body(permute_ref, mine_ref, other_ref, out_ref):
    total = both(mine_ref, other_ref).astype(LOW)
    out_ref[...] = product_right(total, permute_ref[...]).astype(LOW)


def fold_body(*refs):
    own, one, two = refs[:3]
    outs = refs[3:]
    width = own.shape[1]
    sides_held = outs[0].shape[1] // width
    block = outs[0].shape[0]
    for side in range(sides_held):
        for place in range(4):
            first = (4 * side + place) * block
            rows = slice(first, first + block)
            total = (
                own[rows, :].astype(FULL) + one[rows, :].astype(FULL) + two[rows, :].astype(FULL)
            )
            outs[place][:, side * width : (side + 1) * width] = total.astype(outs[place].dtype)


def fold_quarter(terms, sides_held):
    rows = terms[0].shape[0] // (4 * sides_held)
    width = terms[0].shape[1] * sides_held
    kinds = [full_shape, full_shape, low_shape, low_shape]
    return call(fold_body, [kind(rows, width) for kind in kinds], (), terms, sent=(2, 3))


def stack_body(*refs):
    parts, outs = refs[:4], refs[4:]
    block = parts[0].shape[0]
    first = 0
    for out in outs:
        width = out.shape[1]
        for side in range(out.shape[0] // (4 * block)):
            for place in range(4):
                row = (4 * side + place) * block
                out[row : row + block, :] = parts[place][:, first : first + width]
            first += width


def stack_quarter(parts, shapes):
    return call(
        stack_body, [low_shape(*shape) for shape in shapes], (), parts, sent=range(len(shapes))
    )


def merge_body(x_in, y_in, left, right, x_out, y_out):
    x_out[...] = (x_in[...].astype(FULL) + left[...].astype(FULL)).astype(LOW)
    y_out[...] = (y_in[...].astype(FULL) + right[...].astype(FULL)).astype(LOW)


def merge_quarters(x_part, y_part, left, right):
    rows, width = left.shape
    at = [
        pl.BlockSpec((rows, width), lambda one: (0, 0)),
        pl.BlockSpec((rows, width), lambda one: (1, 0)),
    ]
    whole = pl.BlockSpec((rows, width), lambda one: (0, 0))
    return pl.pallas_call(
        merge_body,
        out_shape=[low_shape(*x_part.shape), low_shape(*y_part.shape)],
        grid=(1,),
        in_specs=at + [whole, whole],
        out_specs=at,
        input_output_aliases={0: 0, 1: 1},
        name="merge_body",
        cost_estimate=pl.CostEstimate(flops=1024, transcendentals=0, bytes_accessed=1024),
    )(x_part, y_part, left, right)


def gather_upper(value, devices, wait=()):
    masks = upper_masks(devices)
    if wait:
        value = after(value, *wait)
    if len(masks) == 2:
        one = swap_dp(value, masks[0], devices)
        two = swap_dp(value, masks[1], devices)
        return [value, one, two, swap_dp(after(one, two), masks[1], devices)]
    for mask in masks:
        value = jnp.concatenate([value, swap_dp(value, mask, devices)], axis=0)
    return [value]


def stack_sides(blocks, widths):
    if len(blocks) == 4:
        rows = 4 * blocks[0].shape[0]
        return stack_quarter(blocks, [(2 * rows, width) for width in widths])
    groups, first = [], 0
    for width in widths:
        middle, last = first + width, first + 2 * width
        groups.append(
            jnp.concatenate([blocks[0][:, first:middle], blocks[0][:, middle:last]], axis=0)
        )
        first = last
    return groups


def gather_lower(first, devices, x_wait=(), y_wait=(), last_wait=()):
    rows = first.shape[0] // 2
    x_part = swap_dp(after(first, *x_wait) if x_wait else first, 1, devices)
    y_part = swap_dp(after(first, *y_wait) if y_wait else first, 2, devices)
    left, right = x_part[:rows], y_part[rows:]
    if last_wait:
        left, right = after(left, *last_wait), after(right, *last_wait)
    return [first, x_part, y_part, swap_dp(left, 2, devices), swap_dp(right, 1, devices)]


def reduce_last(pieces, devices, wait=()):
    left, right = pieces[3:]
    if wait:
        left, right = after(left, *wait), after(right, *wait)
    return [swap_dp(left, 2, devices), swap_dp(right, 1, devices)]


def reduce_lower(pieces, came, devices, wait=()):
    merged = merge_quarters(*pieces[1:3], *came)
    x_part, y_part = merged
    if wait:
        x_part, y_part = after(x_part, *wait), after(y_part, *wait)
    return [pieces[0], swap_dp(x_part, 1, devices), swap_dp(y_part, 2, devices)], merged


def reduce_upper(terms, devices, wait=()):
    masks = upper_masks(devices)
    if len(masks) == 2:
        own, one, two, three = fold_quarter(terms, 2)
        if wait:
            two, three = after(two, *wait), after(three, *wait)
        one = (one + swap_dp(three, masks[1], devices).astype(FULL)).astype(LOW)
        two = swap_dp(two, masks[1], devices)
        return own + two.astype(FULL) + swap_dp(one, masks[0], devices).astype(FULL)
    value = terms[0].astype(FULL) + terms[1].astype(FULL) + terms[2].astype(FULL)
    rows = value.shape[0] // 2
    value = jnp.concatenate([value[:rows], value[rows:]], axis=1)
    for mask in masks[::-1]:
        half = value.shape[0] // 2
        away = swap_dp(value[half:].astype(LOW), mask, devices)
        value = value[:half] + away.astype(FULL)
    return value


def first_across(value, devices):
    x_part, y_part = swap_dp(value, 1, devices), swap_dp(value, 2, devices)
    return [value, x_part, y_part, swap_dp(x_part, 2, devices)]


def gather_across(blocks, devices, wait):
    masks = upper_masks(devices)
    rows, width = blocks[0].shape
    first = after(stack_quarter(blocks, [(4 * rows, width)])[0], *wait)
    one, two = swap_dp(first, masks[0], devices), swap_dp(first, masks[1], devices)
    return [first, one, two, swap_dp(one, masks[1], devices)]


def reduce_across_last(pieces, devices):
    mask = upper_masks(devices)[1]
    return [swap_dp(pieces[3], mask, devices), swap_dp(pieces[2], mask, devices)]


def reduce_across(pieces, came, devices):
    mask = upper_masks(devices)[0]
    one = (pieces[1].astype(FULL) + came[0].astype(FULL)).astype(LOW)
    return [pieces[0], came[1], swap_dp(one, mask, devices)]


def reduce_across_first(terms, devices):
    own, x_part, y_part, last = fold_quarter(terms, 1)
    x_part = (x_part + swap_dp(last, 2, devices).astype(FULL)).astype(LOW)
    return (
        own
        + swap_dp(y_part, 2, devices).astype(FULL)
        + swap_dp(x_part, 1, devices).astype(FULL)
    )


def deal(value, order, devices):
    rows, width = value.shape
    first = lax.all_to_all(
        value.reshape(devices, rows // devices, width), "dp", split_axis=0, concat_axis=0, tiled=True
    )
    second = lax.all_to_all(
        jnp.take(first, order, axis=0), "dp", split_axis=0, concat_axis=0, tiled=True
    )
    return second.reshape(rows, width)


def on_device(
    tokens,
    encoder_states,
    cotangent,
    lengths,
    deal_order,
    bucket_index,
    rel_table,
    gain_self,
    self_query,
    self_key,
    self_value,
    self_output,
    gain_cross,
    cross_query,
    cross_key,
    cross_value,
    cross_output,
    gain_feed,
    feed_gate,
    feed_value,
    feed_output,
):
    devices = lax.axis_size("dp")
    myself = lax.axis_index("dp")
    core = lax.axis_index("tensor")
    rows, model = tokens.shape
    block = model // devices
    buckets, heads = rel_table.shape
    inner = self_query.shape[1]
    feed = feed_gate.shape[1]
    across = devices == 16

    numbers = jnp.arange(devices, dtype=jnp.int32)
    owner_of = jnp.sum(
        jnp.where(deal_order[:, None] == numbers[None, :], numbers[:, None], 0), axis=0
    )
    length = jnp.sum(jnp.where(numbers == myself, lengths, 0)).reshape(1)

    self_own = jnp.concatenate([self_query, self_key, self_value, self_output], axis=1)
    cross_own = jnp.concatenate([cross_key, cross_value, cross_query, cross_output], axis=1)
    feed_own = jnp.concatenate([feed_gate, feed_value], axis=1)
    self_blocks = gather_upper(self_own, devices)
    if across:
        down_blocks = first_across(feed_output, devices)
        self_blocks[3] = after(self_blocks[3], *down_blocks[1:3])
    (self_first,) = stack_sides(self_blocks, [2 * inner])
    cross_blocks = gather_upper(cross_own, devices, self_blocks[1:3])
    self_w = gather_lower(self_first, devices)
    (cross_first,) = stack_sides(cross_blocks, [2 * inner])
    cross_w = gather_lower(cross_first, devices, self_w[1:3], self_w[1:3], self_w[3:])
    feed_blocks = gather_upper(feed_own, devices, cross_blocks[1:3])
    (feed_first,) = stack_sides(feed_blocks, [feed])
    if across:
        down = gather_across(down_blocks, devices, feed_blocks[1:3])
    else:
        down = gather_upper(feed_output, devices)[0]
        width = feed // 2
        down = gather_lower(
            jnp.concatenate([down[:, :width], down[:, width:]], axis=0), devices
        )
        middle = down[0].shape[0] // 2
        down = [
            jnp.concatenate([one[:middle], one[middle:]], axis=1) for one in down[:3]
        ] + [jnp.concatenate(down[3:], axis=1)]

    offsets = jnp.asarray(np.array(block_offsets(upper_masks(devices) + [1, 2]), np.int32))
    source = (
        ((myself ^ offsets) * block)[:, None] + jnp.arange(block, dtype=jnp.int32)[None, :]
    ).reshape(1, -1)
    permute, masked_input, grad_three, gains, normed_self = call(
        prepare_body,
        [
            low_shape(model, model),
            low_shape(rows, model),
            low_shape(rows, model),
            full_shape(3, model),
            low_shape(rows, model),
        ],
        (length,),
        (tokens, cotangent, jnp.stack([gain_self, gain_cross, gain_feed]), source),
        flops=4 * rows * model * model,
    )

    half = rows // 2
    memory_half = deal(
        lax.dynamic_slice_in_dim(encoder_states, core * half, half, axis=0), deal_order, devices
    )
    memory_other = swap_tensor(memory_half)

    skewed_bucket = jnp.concatenate(
        [bucket_index[:1], jnp.full((rows,), -1, jnp.int32), bucket_index[::-1][: rows - 1]]
    )
    onehot = (jnp.arange(buckets, dtype=jnp.int32)[:, None] == skewed_bucket[None, :]).astype(FULL)
    bias_rows = jnp.dot(rel_table.T, onehot, precision=HIGHEST)

    unit = 2 * rows * model * inner
    query_self, key_self, value_self, mixed_self, self_partial = call(
        self_forward_body,
        [low_shape(rows, inner)] * 4 + [low_shape(rows, model)],
        (length,),
        (bias_rows, normed_self, *self_w),
        flops=5 * unit,
    )
    memory, key_cross, value_cross = call(
        memory_body,
        [low_shape(rows, model)] + [low_shape(rows, inner)] * 2,
        (),
        (memory_half, memory_other, permute, *cross_w),
        flops=4 * unit,
    )
    hidden_one, normed_cross, query_cross, mixed_cross, partial = call(
        cross_forward_body,
        [full_shape(rows, model), low_shape(rows, model)]
        + [low_shape(rows, inner)] * 2
        + [low_shape(rows, model)],
        (),
        (
            masked_input,
            self_partial,
            swap_tensor(self_partial),
            gains,
            key_cross,
            value_cross,
            *cross_w,
        ),
        flops=3 * unit,
    )
    quarter_rows = model // 4
    feed_w = gather_lower(
        feed_first,
        devices,
        (cross_w[1], self_partial),
        (cross_w[2], self_partial),
        (partial,),
    )

    def group_shapes(width):
        return [low_shape(2 * quarter_rows, width)] * 3 + [low_shape(quarter_rows, width)] * 2

    feed_grads = group_shapes(feed) + [low_shape(quarter_rows, feed)] * 4
    outs = call(
        functools.partial(feed_body, across),
        [full_shape(rows, model), low_shape(rows, model), low_shape(rows, model)] + feed_grads,
        (),
        (hidden_one, partial, swap_tensor(partial), gains, grad_three, *feed_w, *down),
        scratch=[
            pltpu.VMEM((rows, model), LOW),
            pltpu.VMEM((model, rows), LOW),
            pltpu.VMEM((model, rows), LOW),
            pltpu.VMEM((model, feed), LOW),
            pltpu.VMEM((rows, model), FULL),
            pltpu.VMEM((rows, model), FULL),
        ],
        flops=18 * rows * model * feed,
        sent=range(3, 12),
    )
    hidden_two, partial, dpartial = outs[:3]
    dfeed, ddown = outs[3:8], outs[8:12]
    feed_came = reduce_last(dfeed, devices)
    if across:
        down_came = reduce_across_last(ddown, devices)
    else:
        width = feed // 2
        ddown = [
            jnp.concatenate([one[:, :width], one[:, width:]], axis=0) for one in ddown[:3]
        ] + [ddown[3][:, :width], ddown[3][:, width:]]
        down_came = reduce_last(ddown, devices)
    (layer_result,) = call(
        output_body,
        [low_shape(rows, model)],
        (length,),
        (permute, hidden_two, partial, swap_tensor(partial)),
        flops=2 * unit,
    )

    attention_scratch = [
        pltpu.VMEM((rows, model), LOW),
        pltpu.VMEM((model, rows), LOW),
    ] + [pltpu.VMEM((rows, inner), LOW)] * 4
    outs = call(
        cross_backward_body,
        [
            full_shape(rows, model),
            full_shape(1, model),
            low_shape(rows, model),
            low_shape(half, model),
            low_shape(half, model),
        ]
        + group_shapes(2 * inner),
        (),
        (
            hidden_two,
            dpartial,
            swap_tensor(dpartial),
            gains,
            grad_three,
            normed_cross,
            memory,
            query_cross,
            key_cross,
            value_cross,
            mixed_cross,
            *cross_w,
        ),
        scratch=attention_scratch,
        flops=9 * unit,
        sent=range(5, 10),
    )
    grad_two, dgain_feed, dpartial, keep, away = outs[:5]
    dcross = outs[5:10]
    feed_terms, feed_merged = reduce_lower(
        dfeed, [after(one, dpartial) for one in feed_came], devices
    )
    cross_came = reduce_last(dcross, devices, down_came[:1])
    cross_terms, cross_merged = reduce_lower(dcross, cross_came, devices, feed_terms[1:])
    (encoder_half,) = call(
        encoder_body,
        [low_shape(half, model)],
        (),
        (permute, keep, swap_tensor(away)),
        flops=unit,
    )
    encoder_grad = deal(encoder_half, owner_of, devices)

    outs = call(
        self_backward_body,
        [
            full_shape(rows, model),
            full_shape(1, model),
            low_shape(rows, model),
            full_shape(heads, 2 * rows),
        ]
        + group_shapes(2 * inner),
        (length,),
        (
            bias_rows,
            hidden_one,
            dpartial,
            swap_tensor(dpartial),
            gains,
            after(grad_two, *feed_came),
            normed_self,
            query_self,
            key_self,
            value_self,
            mixed_self,
            *self_w,
        ),
        scratch=attention_scratch,
        flops=10 * unit,
        sent=range(4, 9),
    )
    grad_one, dgain_cross, dpartial, diagonal = outs[:4]
    dself = outs[4:9]
    self_came = reduce_last(dself, devices, feed_terms[1:])
    self_terms, self_merged = reduce_lower(dself, self_came, devices, cross_terms[1:])
    input_grad, dgains, dtable = call(
        finish_body,
        [low_shape(rows, model), full_shape(3, model), full_shape(buckets, heads)],
        (length,),
        (
            permute,
            masked_input,
            dpartial,
            swap_tensor(dpartial),
            gains,
            grad_one,
            dgain_cross,
            dgain_feed,
            onehot,
            diagonal,
        ),
        flops=2 * unit,
    )

    if across:
        down_terms = reduce_across(ddown, down_came, devices)
        feed_sums = reduce_upper(feed_terms, devices, down_terms[2:])
        down_sum = reduce_across_first(down_terms, devices)
    else:
        down_sum = reduce_upper(reduce_lower(ddown, down_came, devices)[0], devices)
        feed_sums = reduce_upper(feed_terms, devices)
    cross_sums = reduce_upper(cross_terms, devices, (feed_sums,))
    self_sums = reduce_upper(self_terms, devices, (cross_sums,))
    small = total_small(
        jnp.concatenate([dgains.reshape(-1), dtable.reshape(-1)]).reshape(-1, 128), devices
    ).reshape(-1)
    gain_sums = small[: 3 * model].reshape(3, model)
    table_sum = small[3 * model :].reshape(buckets, heads)

    def column(value, number, width):
        return value[:, number * width : (number + 1) * width]

    return (
        layer_result,
        input_grad,
        encoder_grad,
        table_sum,
        gain_sums[0],
        column(self_sums, 0, inner),
        column(self_sums, 1, inner),
        column(self_sums, 2, inner),
        column(self_sums, 3, inner),
        gain_sums[1],
        column(cross_sums, 2, inner),
        column(cross_sums, 0, inner),
        column(cross_sums, 1, inner),
        column(cross_sums, 3, inner),
        gain_sums[2],
        column(feed_sums, 0, feed),
        column(feed_sums, 1, feed),
        down_sum,
    )


def solution(mesh):
    in_specs = (
        P("dp", None),
        P("dp", None),
        P("dp", None),
        P(),
        P(),
        P(),
        P(None, "tensor"),
        P(),
        P("dp", "tensor"),
        P("dp", "tensor"),
        P("dp", "tensor"),
        P("dp", "tensor"),
        P(),
        P("dp", "tensor"),
        P("dp", "tensor"),
        P("dp", "tensor"),
        P("dp", "tensor"),
        P(),
        P("dp", "tensor"),
        P("dp", "tensor"),
        P("dp", "tensor"),
    )
    out_specs = (
        P("dp", None),
        P("dp", None),
        P(("dp", "tensor"), None),
        P(None, "tensor"),
        P(),
        P("dp", "tensor"),
        P("dp", "tensor"),
        P("dp", "tensor"),
        P("dp", "tensor"),
        P(),
        P("dp", "tensor"),
        P("dp", "tensor"),
        P("dp", "tensor"),
        P("dp", "tensor"),
        P(),
        P("dp", "tensor"),
        P("dp", "tensor"),
        P("dp", "tensor"),
    )
    return jax.shard_map(
        on_device, mesh=mesh, in_specs=in_specs, out_specs=out_specs, check_vma=False
    )
```

```python
import functools

import jax
import jax.numpy as jnp
import numpy as np
from jax import lax
from jax.experimental import pallas as pl
from jax.experimental.pallas import tpu as pltpu
from jax.sharding import PartitionSpec as P

EPSILON = 1e-06
MASKED = -1e30
HIGHEST = lax.Precision.HIGHEST
HEAD = 64
PAIR = 2 * HEAD
LOW = jnp.bfloat16
FULL = jnp.float32


def upper_masks(devices):
    if devices == 16:
        return [12, 4]
    return [1 << bit for bit in range(devices.bit_length() - 2, 1, -1)]


def block_offsets(masks):
    offsets = [0]
    for mask in masks:
        offsets = offsets + [offset ^ mask for offset in offsets]
    return offsets


def swap_dp(value, mask, devices):
    return lax.ppermute(value, "dp", [(one, one ^ mask) for one in range(devices)])


def swap_tensor(value):
    return lax.ppermute(value, "tensor", [(0, 1), (1, 0)])


def total_small(value, devices):
    mask = 1
    while mask < devices:
        value = value + swap_dp(value, mask, devices)
        mask = 2 * mask
    return value


def product_plain(left, right):
    return jnp.dot(left, right, preferred_element_type=FULL)


def product_right(left, right):
    return lax.dot_general(left, right, (((1,), (1,)), ((), ())), preferred_element_type=FULL)


def product_left(left, right):
    return lax.dot_general(left, right, (((0,), (0,)), ((), ())), preferred_element_type=FULL)


def quarter(ref, number):
    width = ref.shape[1] // 4
    return ref[:, number * width : (number + 1) * width]


def sides(refs):
    own, x_part, y_part, left, right = refs
    rows = left.shape[0]
    return (
        [own.at[:rows], x_part.at[:rows], y_part.at[:rows], left],
        [own.at[rows:], x_part.at[rows:], y_part.at[rows:], right],
    )


def after(value, *earlier):
    return lax.optimization_barrier((value, *earlier))[0]


def project_in(value_ref, pieces, columns):
    total = None
    for number, piece in enumerate(pieces):
        part = product_plain(quarter(value_ref, number), piece[:, columns])
        total = part if total is None else total + part
    return total


def inverse_root(value):
    return lax.rsqrt(jnp.mean(value * value, axis=-1, keepdims=True) + EPSILON)


def norm_backward(value, gain, upstream):
    root = inverse_root(value)
    weighted = upstream * gain
    inner_mean = jnp.mean(weighted * value, axis=-1, keepdims=True)
    grad = root * weighted - value * (root * root * root) * inner_mean
    return grad, jnp.sum(upstream * value * root, axis=0, keepdims=True)


def both(mine_ref, other_ref):
    return mine_ref[...].astype(FULL) + other_ref[...].astype(FULL)


def valid_column(length_ref, rows):
    return (lax.broadcasted_iota(jnp.int32, (rows, 1), 0) < length_ref[0]).astype(FULL)


def toeplitz_bias(row, rows):
    wide = jnp.broadcast_to(row, (rows, row.shape[1]))
    return pltpu.roll(wide, 0, 1, stride=1, stride_axis=0)[:, :rows]


def head_half(value, side, lanes):
    keep = lanes < HEAD if side == 0 else lanes >= HEAD
    return jnp.where(keep, value, jnp.zeros_like(value))


def masked_scores(query, key, length_ref, bias_ref, head):
    scores = product_right(query, key)
    if bias_ref is None:
        return scores
    rows, columns = scores.shape
    scores = scores + toeplitz_bias(bias_ref[pl.ds(head, 1), :], rows)
    at_row = lax.broadcasted_iota(jnp.int32, (rows, columns), 0)
    at_column = lax.broadcasted_iota(jnp.int32, (rows, columns), 1)
    allowed = (at_column <= at_row) & (at_column < length_ref[0])
    return jnp.where(allowed, scores, MASKED)


def softmax_rows(scores):
    exponent = jnp.exp(scores - jnp.max(scores, axis=-1, keepdims=True))
    return exponent * (1.0 / jnp.sum(exponent, axis=-1, keepdims=True))


def attention_forward(query_ref, key_ref, value_ref, out_ref, length_ref=None, bias_ref=None):
    rows, width = query_ref.shape
    lanes = lax.broadcasted_iota(jnp.int32, (rows, PAIR), 1)

    def one_pair(pair, carry):
        columns = pl.ds(pl.multiple_of(pair * PAIR, PAIR), PAIR)
        query, key, value = query_ref[:, columns], key_ref[:, columns], value_ref[:, columns]
        mixed = []
        for side in range(2):
            scores = masked_scores(
                head_half(query, side, lanes), key, length_ref, bias_ref, 2 * pair + side
            )
            mixed.append(product_plain(softmax_rows(scores).astype(LOW), value))
        out_ref[:, columns] = jnp.where(lanes < HEAD, mixed[0], mixed[1]).astype(LOW)
        return carry

    lax.fori_loop(0, width // PAIR, one_pair, 0)


def attention_backward(
    query_ref,
    key_ref,
    value_ref,
    grad_ref,
    dquery_ref,
    dkey_ref,
    dvalue_ref,
    length_ref=None,
    bias_ref=None,
    diagonal_ref=None,
):
    rows, width = query_ref.shape
    lanes = lax.broadcasted_iota(jnp.int32, (rows, PAIR), 1)
    if bias_ref is not None:
        flip = (
            lax.broadcasted_iota(jnp.int32, (rows, rows), 0)
            + lax.broadcasted_iota(jnp.int32, (rows, rows), 1)
            == rows - 1
        ).astype(LOW)

    def one_pair(pair, carry):
        columns = pl.ds(pl.multiple_of(pair * PAIR, PAIR), PAIR)
        query, key, value = query_ref[:, columns], key_ref[:, columns], value_ref[:, columns]
        grad = grad_ref[:, columns]
        dquery, dkey, dvalue = [], [], []
        for side in range(2):
            head = 2 * pair + side
            scores = masked_scores(head_half(query, side, lanes), key, length_ref, bias_ref, head)
            chance = softmax_rows(scores)
            chance_grad = product_right(head_half(grad, side, lanes), value)
            delta = jnp.sum(chance * chance_grad, axis=-1, keepdims=True)
            score_grad = (chance * (chance_grad - delta)).astype(LOW)
            dquery.append(product_plain(score_grad, key))
            dkey.append(product_left(score_grad, query))
            dvalue.append(product_left(chance.astype(LOW), grad))
            if bias_ref is not None:
                flipped = product_plain(flip, score_grad)
                wide = jnp.concatenate([flipped, jnp.zeros_like(flipped)], axis=1)
                skewed = pltpu.roll(wide, rows + 1, 1, stride=1, stride_axis=0)
                diagonal_ref[pl.ds(head, 1), :] = jnp.sum(skewed, axis=0, keepdims=True)
        left = lanes < HEAD
        dquery_ref[:, columns] = jnp.where(left, dquery[0], dquery[1]).astype(LOW)
        dkey_ref[:, columns] = jnp.where(left, dkey[0], dkey[1]).astype(LOW)
        dvalue_ref[:, columns] = jnp.where(left, dvalue[0], dvalue[1]).astype(LOW)
        return carry

    lax.fori_loop(0, width // PAIR, one_pair, 0)


def low_shape(*shape):
    return jax.ShapeDtypeStruct(shape, LOW)


def full_shape(*shape):
    return jax.ShapeDtypeStruct(shape, FULL)


def call(body, out_shape, scalars, arrays, scratch=(), flops=0, sent=()):
    vmem = pl.BlockSpec(memory_space=pltpu.VMEM)
    smem = pl.BlockSpec(memory_space=pltpu.SMEM)
    return pl.pallas_call(
        body,
        out_shape=list(out_shape),
        in_specs=[smem] * len(scalars) + [vmem] * len(arrays),
        out_specs=[
            pl.BlockSpec(one.shape, lambda step: (0, 0), pipeline_mode=pl.Buffered(1))
            if number in sent
            else vmem
            for number, one in enumerate(out_shape)
        ],
        grid=(1,) if sent else (),
        scratch_shapes=list(scratch),
        name=getattr(body, "func", body).__name__,
        cost_estimate=pl.CostEstimate(
            flops=int(flops * 1), transcendentals=0, bytes_accessed=1024
        ),
        compiler_params=pltpu.CompilerParams(vmem_limit_bytes=44 << 20),
    )(*scalars, *arrays)


def prepare_body(
    length_ref,
    tokens_ref,
    cotangent_ref,
    gains_ref,
    source_ref,
    permute_ref,
    input_ref,
    grad_ref,
    gains_out_ref,
    normed_ref,
):
    rows, width = tokens_ref.shape
    at_row = lax.broadcasted_iota(jnp.int32, (width, width), 0)
    permute_ref[...] = (at_row == source_ref[...]).astype(FULL).astype(LOW)
    permute = permute_ref[...]
    valid = valid_column(length_ref, rows)
    masked = product_plain(tokens_ref[...], permute) * valid
    input_ref[...] = masked.astype(LOW)
    grad_ref[...] = (product_plain(cotangent_ref[...], permute) * valid).astype(LOW)
    gains = gains_ref[...]
    high = gains.astype(LOW)
    middle = (gains - high.astype(FULL)).astype(LOW)
    low = (gains - high.astype(FULL) - middle.astype(FULL)).astype(LOW)
    gains_out_ref[...] = (
        product_plain(high, permute) + product_plain(middle, permute)
    ) + product_plain(low, permute)
    normed_ref[...] = (masked * inverse_root(masked) * gains_out_ref[0:1, :]).astype(LOW)


def self_forward_body(
    length_ref, bias_ref, normed_ref, *refs
):
    qk, vo = sides(refs[:5])
    query_ref, key_ref, value_ref, mixed_ref, partial_ref = refs[5:]
    inner = query_ref.shape[1]
    query_ref[...] = project_in(normed_ref, qk, slice(0, inner)).astype(LOW)
    key_ref[...] = project_in(normed_ref, qk, slice(inner, 2 * inner)).astype(LOW)
    value_ref[...] = project_in(normed_ref, vo, slice(0, inner)).astype(LOW)
    attention_forward(query_ref, key_ref, value_ref, mixed_ref, length_ref, bias_ref)
    width = partial_ref.shape[1] // 4
    for number in range(4):
        partial_ref[:, number * width : (number + 1) * width] = product_right(
            mixed_ref[...], vo[number][:, inner:]
        ).astype(LOW)


def memory_body(half_ref, other_ref, permute_ref, *refs):
    kv, _ = sides(refs[:5])
    memory_ref, key_ref, value_ref = refs[5:]
    inner = key_ref.shape[1]
    half = half_ref.shape[0]
    memory_ref[:half, :] = product_plain(half_ref[...], permute_ref[...]).astype(LOW)
    memory_ref[half:, :] = product_plain(other_ref[...], permute_ref[...]).astype(LOW)
    key_ref[...] = project_in(memory_ref, kv, slice(0, inner)).astype(LOW)
    value_ref[...] = project_in(memory_ref, kv, slice(inner, 2 * inner)).astype(LOW)


def cross_forward_body(input_ref, mine_ref, other_ref, gains_ref, key_ref, value_ref, *refs):
    _, qo = sides(refs[:5])
    hidden_ref, normed_ref, query_ref, mixed_ref, partial_ref = refs[5:]
    inner = query_ref.shape[1]
    hidden = input_ref[...].astype(FULL) + both(mine_ref, other_ref)
    hidden_ref[...] = hidden
    normed_ref[...] = (hidden * inverse_root(hidden) * gains_ref[1:2, :]).astype(LOW)
    query_ref[...] = project_in(normed_ref, qo, slice(0, inner)).astype(LOW)
    attention_forward(query_ref, key_ref, value_ref, mixed_ref)
    width = partial_ref.shape[1] // 4
    for number in range(4):
        partial_ref[:, number * width : (number + 1) * width] = product_right(
            mixed_ref[...], qo[number][:, inner:]
        ).astype(LOW)


GELU_SCALE = float(np.sqrt(2.0 / np.pi))
GELU_CUBE = 0.044715
CHUNK = 256


def feed_body(transposed, hidden_in_ref, mine_ref, other_ref, gains_ref, grad_ref, *refs):
    gate_w, lift_w = sides(refs[:5])
    down_w = refs[5:9]
    hidden_ref, partial_ref, dnormed_ref = refs[9:12]
    dgate_w, dlift_w = sides(refs[12:17])
    ddown_w = refs[17:21]
    normed_ref, normed_t_ref, grad_t_ref, down_ref, total_ref, dtotal_ref = refs[21:]
    rows, model = hidden_ref.shape
    width = model // 4
    block = width // 4
    feed = gate_w[0].shape[1]
    hidden = hidden_in_ref[...] + both(mine_ref, other_ref)
    hidden_ref[...] = hidden
    normed_ref[...] = (hidden * inverse_root(hidden) * gains_ref[2:3, :]).astype(LOW)
    normed_t_ref[...] = normed_ref[...].T
    grad_t_ref[...] = grad_ref[...].T
    for number in range(4):
        if transposed:
            for other in range(4):
                place = number * width + other * block
                down_ref[place : place + block, :] = down_w[other][
                    number * block : (number + 1) * block, :
                ]
        else:
            down_ref[number * width : (number + 1) * width, :] = down_w[number][...]
    total_ref[...] = jnp.zeros_like(total_ref)
    dtotal_ref[...] = jnp.zeros_like(dtotal_ref)

    def some_columns(columns):
        gate = project_in(normed_ref, gate_w, columns)
        lift = project_in(normed_ref, lift_w, columns)
        squared = gate * gate
        curve = jnp.tanh(GELU_SCALE * (gate + GELU_CUBE * squared * gate))
        half_up = 0.5 * (1.0 + curve)
        activated = gate * half_up
        product = (activated * lift).astype(LOW)
        down = down_ref[:, columns]
        dproduct = product_plain(grad_ref[...], down).astype(LOW).astype(FULL)
        slope = half_up + 0.5 * gate * (1.0 - curve * curve) * (
            GELU_SCALE * (1.0 + 3.0 * GELU_CUBE * squared)
        )
        dgate = (dproduct * lift * slope).astype(LOW)
        dlift = (dproduct * activated).astype(LOW)
        total_ref[...] += product_right(product, down)
        for number in range(4):
            part = slice(number * width, (number + 1) * width)
            normed_t = normed_t_ref[part, :]
            dgate_w[number][:, columns] = product_plain(normed_t, dgate).astype(LOW)
            dlift_w[number][:, columns] = product_plain(normed_t, dlift).astype(LOW)
            ddown = product_plain(grad_t_ref[part, :], product).astype(LOW)
            if transposed:
                for other in range(4):
                    ddown_w[other][number * block : (number + 1) * block, columns] = ddown[
                        other * block : (other + 1) * block, :
                    ]
            else:
                ddown_w[number][:, columns] = ddown
            dtotal_ref[:, part] += product_right(
                dgate, gate_w[number][:, columns]
            ) + product_right(dlift, lift_w[number][:, columns])

    def one_chunk(chunk, carry):
        some_columns(pl.ds(pl.multiple_of(chunk * CHUNK, CHUNK), CHUNK))
        return carry

    whole = feed // CHUNK
    lax.fori_loop(0, whole, one_chunk, 0)
    if feed % CHUNK:
        some_columns(pl.ds(whole * CHUNK, feed % CHUNK))
    partial_ref[...] = total_ref[...].astype(LOW)
    dnormed_ref[...] = dtotal_ref[...].astype(LOW)


def cross_backward_body(
    hidden_ref,
    mine_ref,
    other_ref,
    gains_ref,
    grad_ref,
    normed_ref,
    memory_ref,
    query_ref,
    key_ref,
    value_ref,
    mixed_ref,
    *refs,
):
    kv, qo = sides(refs[:5])
    grad_out_ref, dgain_ref, dnormed_ref, keep_ref, away_ref = refs[5:10]
    dkv, dqo = sides(refs[10:15])
    low_ref, transposed_ref, dmixed_ref, dquery_ref, dkey_ref, dvalue_ref = refs[15:]
    rows, model = hidden_ref.shape
    width = model // 4
    inner = query_ref.shape[1]
    half = rows // 2
    back, dgain_ref[...] = norm_backward(
        hidden_ref[...], gains_ref[2:3, :], both(mine_ref, other_ref)
    )
    grad = grad_ref[...].astype(FULL) + back
    grad_out_ref[...] = grad
    low_ref[...] = grad.astype(LOW)
    dmixed_ref[...] = project_in(low_ref, qo, slice(inner, 2 * inner)).astype(LOW)
    attention_backward(
        query_ref, key_ref, value_ref, dmixed_ref, dquery_ref, dkey_ref, dvalue_ref
    )
    for number in range(4):
        part = slice(number * width, (number + 1) * width)
        dnormed_ref[:, part] = product_right(dquery_ref[...], qo[number][:, :inner]).astype(LOW)
        partial = (
            product_right(dkey_ref[...], kv[number][:, :inner])
            + product_right(dvalue_ref[...], kv[number][:, inner:])
        ).astype(LOW)
        keep_ref[:, part] = partial[:half]
        away_ref[:, part] = partial[half:]
    transposed_ref[...] = memory_ref[...].T
    for number in range(4):
        part = slice(number * width, (number + 1) * width)
        dkv[number][:, :inner] = product_plain(transposed_ref[part, :], dkey_ref[...]).astype(LOW)
        dkv[number][:, inner:] = product_plain(transposed_ref[part, :], dvalue_ref[...]).astype(
            LOW
        )
    transposed_ref[...] = normed_ref[...].T
    for number in range(4):
        part = slice(number * width, (number + 1) * width)
        dqo[number][:, :inner] = product_plain(transposed_ref[part, :], dquery_ref[...]).astype(
            LOW
        )
    transposed_ref[...] = low_ref[...].T
    for number in range(4):
        part = slice(number * width, (number + 1) * width)
        dqo[number][:, inner:] = product_plain(transposed_ref[part, :], mixed_ref[...]).astype(LOW)


def self_backward_body(
    length_ref,
    bias_ref,
    hidden_ref,
    mine_ref,
    other_ref,
    gains_ref,
    grad_ref,
    normed_ref,
    query_ref,
    key_ref,
    value_ref,
    mixed_ref,
    *refs,
):
    qk, vo = sides(refs[:5])
    grad_out_ref, dgain_ref, dnormed_ref, diagonal_ref = refs[5:9]
    dqk, dvo = sides(refs[9:14])
    low_ref, transposed_ref, dmixed_ref, dquery_ref, dkey_ref, dvalue_ref = refs[14:]
    rows, model = hidden_ref.shape
    width = model // 4
    inner = query_ref.shape[1]
    back, dgain_ref[...] = norm_backward(
        hidden_ref[...], gains_ref[1:2, :], both(mine_ref, other_ref)
    )
    grad = grad_ref[...] + back
    grad_out_ref[...] = grad
    low_ref[...] = grad.astype(LOW)
    dmixed_ref[...] = project_in(low_ref, vo, slice(inner, 2 * inner)).astype(LOW)
    attention_backward(
        query_ref,
        key_ref,
        value_ref,
        dmixed_ref,
        dquery_ref,
        dkey_ref,
        dvalue_ref,
        length_ref,
        bias_ref,
        diagonal_ref,
    )
    for number in range(4):
        part = slice(number * width, (number + 1) * width)
        dnormed_ref[:, part] = (
            product_right(dquery_ref[...], qk[number][:, :inner])
            + product_right(dkey_ref[...], qk[number][:, inner:])
            + product_right(dvalue_ref[...], vo[number][:, :inner])
        ).astype(LOW)
    transposed_ref[...] = normed_ref[...].T
    for number in range(4):
        part = slice(number * width, (number + 1) * width)
        dqk[number][:, :inner] = product_plain(transposed_ref[part, :], dquery_ref[...]).astype(
            LOW
        )
        dqk[number][:, inner:] = product_plain(transposed_ref[part, :], dkey_ref[...]).astype(LOW)
        dvo[number][:, :inner] = product_plain(transposed_ref[part, :], dvalue_ref[...]).astype(
            LOW
        )
    transposed_ref[...] = low_ref[...].T
    for number in range(4):
        part = slice(number * width, (number + 1) * width)
        dvo[number][:, inner:] = product_plain(transposed_ref[part, :], mixed_ref[...]).astype(LOW)


def finish_body(
    length_ref,
    permute_ref,
    input_ref,
    mine_ref,
    other_ref,
    gains_ref,
    grad_ref,
    dgain_cross_ref,
    dgain_feed_ref,
    onehot_ref,
    diagonal_ref,
    out_ref,
    dgains_ref,
    table_ref,
):
    rows = input_ref.shape[0]
    permute = permute_ref[...]
    back, dgain = norm_backward(
        input_ref[...].astype(FULL), gains_ref[0:1, :], both(mine_ref, other_ref)
    )
    total = ((grad_ref[...] + back) * valid_column(length_ref, rows)).astype(LOW)
    out_ref[...] = product_right(total, permute).astype(LOW)
    dgains = jnp.concatenate([dgain, dgain_cross_ref[...], dgain_feed_ref[...]], axis=0)
    high = dgains.astype(LOW)
    middle = (dgains - high.astype(FULL)).astype(LOW)
    low = (dgains - high.astype(FULL) - middle.astype(FULL)).astype(LOW)
    dgains_ref[...] = (
        product_right(high, permute) + product_right(middle, permute)
    ) + product_right(low, permute)
    table_ref[...] = lax.dot_general(
        onehot_ref[...],
        diagonal_ref[...],
        (((1,), (1,)), ((), ())),
        precision=HIGHEST,
        preferred_element_type=FULL,
    )


def output_body(length_ref, permute_ref, hidden_ref, mine_ref, other_ref, out_ref):
    rows = hidden_ref.shape[0]
    total = (hidden_ref[...] + both(mine_ref, other_ref)) * valid_column(length_ref, rows)
    out_ref[...] = product_right(total.astype(LOW), permute_ref[...]).astype(LOW)


def encoder_body(permute_ref, mine_ref, other_ref, out_ref):
    total = both(mine_ref, other_ref).astype(LOW)
    out_ref[...] = product_right(total, permute_ref[...]).astype(LOW)


def fold_body(*refs):
    own, one, two = refs[:3]
    outs = refs[3:]
    width = own.shape[1]
    sides_held = outs[0].shape[1] // width
    block = outs[0].shape[0]
    for side in range(sides_held):
        for place in range(4):
            first = (4 * side + place) * block
            rows = slice(first, first + block)
            total = (
                own[rows, :].astype(FULL) + one[rows, :].astype(FULL) + two[rows, :].astype(FULL)
            )
            outs[place][:, side * width : (side + 1) * width] = total.astype(outs[place].dtype)


def fold_quarter(terms, sides_held):
    rows = terms[0].shape[0] // (4 * sides_held)
    width = terms[0].shape[1] * sides_held
    kinds = [full_shape, full_shape, low_shape, low_shape]
    return call(fold_body, [kind(rows, width) for kind in kinds], (), terms, sent=(2, 3))


def stack_body(*refs):
    parts, outs = refs[:4], refs[4:]
    block = parts[0].shape[0]
    first = 0
    for out in outs:
        width = out.shape[1]
        for side in range(out.shape[0] // (4 * block)):
            for place in range(4):
                row = (4 * side + place) * block
                out[row : row + block, :] = parts[place][:, first : first + width]
            first += width


def stack_quarter(parts, shapes):
    return call(
        stack_body, [low_shape(*shape) for shape in shapes], (), parts, sent=range(len(shapes))
    )


def merge_body(x_in, y_in, left, right, x_out, y_out):
    x_out[...] = (x_in[...].astype(FULL) + left[...].astype(FULL)).astype(LOW)
    y_out[...] = (y_in[...].astype(FULL) + right[...].astype(FULL)).astype(LOW)


def merge_quarters(x_part, y_part, left, right):
    rows, width = left.shape
    steps = 2
    part = rows // steps
    first = pl.BlockSpec((part, width), lambda step: (step, 0))
    second = pl.BlockSpec((part, width), lambda step: (steps + step, 0))
    at = [first, second]
    return pl.pallas_call(
        merge_body,
        out_shape=[low_shape(*x_part.shape), low_shape(*y_part.shape)],
        grid=(steps,),
        in_specs=at + [first, first],
        out_specs=at,
        input_output_aliases={0: 0, 1: 1},
        name="merge_body",
        cost_estimate=pl.CostEstimate(flops=1024, transcendentals=0, bytes_accessed=1024),
    )(x_part, y_part, left, right)


def gather_upper(value, devices, wait=()):
    masks = upper_masks(devices)
    if wait:
        value = after(value, *wait)
    if len(masks) == 2:
        one = swap_dp(value, masks[0], devices)
        two = swap_dp(value, masks[1], devices)
        return [value, one, two, swap_dp(after(one, two), masks[1], devices)]
    for mask in masks:
        value = jnp.concatenate([value, swap_dp(value, mask, devices)], axis=0)
    return [value]


def stack_sides(blocks, widths):
    if len(blocks) == 4:
        rows = 4 * blocks[0].shape[0]
        return stack_quarter(blocks, [(2 * rows, width) for width in widths])
    groups, first = [], 0
    for width in widths:
        middle, last = first + width, first + 2 * width
        groups.append(
            jnp.concatenate([blocks[0][:, first:middle], blocks[0][:, middle:last]], axis=0)
        )
        first = last
    return groups


def gather_lower(first, devices, x_wait=(), y_wait=(), last_wait=()):
    rows = first.shape[0] // 2
    x_part = swap_dp(after(first, *x_wait) if x_wait else first, 1, devices)
    y_part = swap_dp(after(first, *y_wait) if y_wait else first, 2, devices)
    left, right = x_part[:rows], y_part[rows:]
    if last_wait:
        left, right = after(left, *last_wait), after(right, *last_wait)
    return [first, x_part, y_part, swap_dp(left, 2, devices), swap_dp(right, 1, devices)]


def reduce_last(pieces, devices, wait=()):
    left, right = pieces[3:]
    if wait:
        left, right = after(left, *wait), after(right, *wait)
    return [swap_dp(left, 2, devices), swap_dp(right, 1, devices)]


def reduce_lower(pieces, came, devices, wait=()):
    merged = merge_quarters(*pieces[1:3], *came)
    x_part, y_part = merged
    if wait:
        x_part, y_part = after(x_part, *wait), after(y_part, *wait)
    return [pieces[0], swap_dp(x_part, 1, devices), swap_dp(y_part, 2, devices)], merged


def reduce_upper(terms, devices, wait=()):
    masks = upper_masks(devices)
    if len(masks) == 2:
        own, one, two, three = fold_quarter(terms, 2)
        if wait:
            two, three = after(two, *wait), after(three, *wait)
        one = (one + swap_dp(three, masks[1], devices).astype(FULL)).astype(LOW)
        two = swap_dp(two, masks[1], devices)
        return own + two.astype(FULL) + swap_dp(one, masks[0], devices).astype(FULL)
    value = terms[0].astype(FULL) + terms[1].astype(FULL) + terms[2].astype(FULL)
    rows = value.shape[0] // 2
    value = jnp.concatenate([value[:rows], value[rows:]], axis=1)
    for mask in masks[::-1]:
        half = value.shape[0] // 2
        away = swap_dp(value[half:].astype(LOW), mask, devices)
        value = value[:half] + away.astype(FULL)
    return value


def first_across(value, devices):
    x_part, y_part = swap_dp(value, 1, devices), swap_dp(value, 2, devices)
    return [value, x_part, y_part, swap_dp(x_part, 2, devices)]


def gather_across(blocks, devices, wait):
    masks = upper_masks(devices)
    rows, width = blocks[0].shape
    first = after(stack_quarter(blocks, [(4 * rows, width)])[0], *wait)
    one, two = swap_dp(first, masks[0], devices), swap_dp(first, masks[1], devices)
    return [first, one, two, swap_dp(one, masks[1], devices)]


def reduce_across_last(pieces, devices):
    mask = upper_masks(devices)[1]
    return [swap_dp(pieces[3], mask, devices), swap_dp(pieces[2], mask, devices)]


def reduce_across(pieces, came, devices):
    mask = upper_masks(devices)[0]
    one = (pieces[1].astype(FULL) + came[0].astype(FULL)).astype(LOW)
    return [pieces[0], came[1], swap_dp(one, mask, devices)]


def reduce_across_first(terms, devices):
    own, x_part, y_part, last = fold_quarter(terms, 1)
    x_part = (x_part + swap_dp(last, 2, devices).astype(FULL)).astype(LOW)
    return (
        own
        + swap_dp(y_part, 2, devices).astype(FULL)
        + swap_dp(x_part, 1, devices).astype(FULL)
    )


def deal(value, order, devices):
    rows, width = value.shape
    first = lax.all_to_all(
        value.reshape(devices, rows // devices, width), "dp", split_axis=0, concat_axis=0, tiled=True
    )
    second = lax.all_to_all(
        jnp.take(first, order, axis=0), "dp", split_axis=0, concat_axis=0, tiled=True
    )
    return second.reshape(rows, width)


def on_device(
    tokens,
    encoder_states,
    cotangent,
    lengths,
    deal_order,
    bucket_index,
    rel_table,
    gain_self,
    self_query,
    self_key,
    self_value,
    self_output,
    gain_cross,
    cross_query,
    cross_key,
    cross_value,
    cross_output,
    gain_feed,
    feed_gate,
    feed_value,
    feed_output,
):
    devices = lax.axis_size("dp")
    myself = lax.axis_index("dp")
    core = lax.axis_index("tensor")
    rows, model = tokens.shape
    block = model // devices
    buckets, heads = rel_table.shape
    inner = self_query.shape[1]
    feed = feed_gate.shape[1]
    across = devices == 16

    numbers = jnp.arange(devices, dtype=jnp.int32)
    owner_of = jnp.sum(
        jnp.where(deal_order[:, None] == numbers[None, :], numbers[:, None], 0), axis=0
    )
    length = jnp.sum(jnp.where(numbers == myself, lengths, 0)).reshape(1)

    self_own = jnp.concatenate([self_query, self_key, self_value, self_output], axis=1)
    cross_own = jnp.concatenate([cross_key, cross_value, cross_query, cross_output], axis=1)
    feed_own = jnp.concatenate([feed_gate, feed_value], axis=1)
    self_blocks = gather_upper(self_own, devices)
    if across:
        down_blocks = first_across(feed_output, devices)
        self_blocks[3] = after(self_blocks[3], *down_blocks[1:3])
    (self_first,) = stack_sides(self_blocks, [2 * inner])
    cross_blocks = gather_upper(cross_own, devices, self_blocks[1:3])
    self_w = gather_lower(self_first, devices)
    (cross_first,) = stack_sides(cross_blocks, [2 * inner])
    cross_w = gather_lower(cross_first, devices, self_w[1:3], self_w[1:3], self_w[3:])
    feed_blocks = gather_upper(feed_own, devices, cross_blocks[1:3])
    (feed_first,) = stack_sides(feed_blocks, [feed])
    if across:
        down = gather_across(down_blocks, devices, feed_blocks[1:3])
    else:
        down = gather_upper(feed_output, devices)[0]
        width = feed // 2
        down = gather_lower(
            jnp.concatenate([down[:, :width], down[:, width:]], axis=0), devices
        )
        middle = down[0].shape[0] // 2
        down = [
            jnp.concatenate([one[:middle], one[middle:]], axis=1) for one in down[:3]
        ] + [jnp.concatenate(down[3:], axis=1)]

    offsets = jnp.asarray(np.array(block_offsets(upper_masks(devices) + [1, 2]), np.int32))
    source = (
        ((myself ^ offsets) * block)[:, None] + jnp.arange(block, dtype=jnp.int32)[None, :]
    ).reshape(1, -1)
    permute, masked_input, grad_three, gains, normed_self = call(
        prepare_body,
        [
            low_shape(model, model),
            low_shape(rows, model),
            low_shape(rows, model),
            full_shape(3, model),
            low_shape(rows, model),
        ],
        (length,),
        (tokens, cotangent, jnp.stack([gain_self, gain_cross, gain_feed]), source),
        flops=4 * rows * model * model,
    )

    half = rows // 2
    memory_half = deal(
        lax.dynamic_slice_in_dim(encoder_states, core * half, half, axis=0), deal_order, devices
    )
    memory_other = swap_tensor(memory_half)

    skewed_bucket = jnp.concatenate(
        [bucket_index[:1], jnp.full((rows,), -1, jnp.int32), bucket_index[::-1][: rows - 1]]
    )
    onehot = (jnp.arange(buckets, dtype=jnp.int32)[:, None] == skewed_bucket[None, :]).astype(FULL)
    bias_rows = jnp.dot(rel_table.T, onehot, precision=HIGHEST)

    unit = 2 * rows * model * inner
    query_self, key_self, value_self, mixed_self, self_partial = call(
        self_forward_body,
        [low_shape(rows, inner)] * 4 + [low_shape(rows, model)],
        (length,),
        (bias_rows, normed_self, *self_w),
        flops=5 * unit,
    )
    memory, key_cross, value_cross = call(
        memory_body,
        [low_shape(rows, model)] + [low_shape(rows, inner)] * 2,
        (),
        (memory_half, memory_other, permute, *cross_w),
        flops=4 * unit,
    )
    hidden_one, normed_cross, query_cross, mixed_cross, partial = call(
        cross_forward_body,
        [full_shape(rows, model), low_shape(rows, model)]
        + [low_shape(rows, inner)] * 2
        + [low_shape(rows, model)],
        (),
        (
            masked_input,
            self_partial,
            swap_tensor(self_partial),
            gains,
            key_cross,
            value_cross,
            *cross_w,
        ),
        flops=3 * unit,
    )
    quarter_rows = model // 4
    feed_w = gather_lower(
        feed_first,
        devices,
        (cross_w[1], self_partial),
        (cross_w[2], self_partial),
        (partial,),
    )

    def group_shapes(width):
        return [low_shape(2 * quarter_rows, width)] * 3 + [low_shape(quarter_rows, width)] * 2

    feed_grads = group_shapes(feed) + [low_shape(quarter_rows, feed)] * 4
    outs = call(
        functools.partial(feed_body, across),
        [full_shape(rows, model), low_shape(rows, model), low_shape(rows, model)] + feed_grads,
        (),
        (hidden_one, partial, swap_tensor(partial), gains, grad_three, *feed_w, *down),
        scratch=[
            pltpu.VMEM((rows, model), LOW),
            pltpu.VMEM((model, rows), LOW),
            pltpu.VMEM((model, rows), LOW),
            pltpu.VMEM((model, feed), LOW),
            pltpu.VMEM((rows, model), FULL),
            pltpu.VMEM((rows, model), FULL),
        ],
        flops=18 * rows * model * feed,
        sent=range(3, 12),
    )
    hidden_two, partial, dpartial = outs[:3]
    dfeed, ddown = outs[3:8], outs[8:12]
    feed_came = reduce_last(dfeed, devices)
    if across:
        down_came = reduce_across_last(ddown, devices)
    else:
        width = feed // 2
        ddown = [
            jnp.concatenate([one[:, :width], one[:, width:]], axis=0) for one in ddown[:3]
        ] + [ddown[3][:, :width], ddown[3][:, width:]]
        down_came = reduce_last(ddown, devices)
    (layer_result,) = call(
        output_body,
        [low_shape(rows, model)],
        (length,),
        (permute, hidden_two, partial, swap_tensor(partial)),
        flops=2 * unit,
    )

    attention_scratch = [
        pltpu.VMEM((rows, model), LOW),
        pltpu.VMEM((model, rows), LOW),
    ] + [pltpu.VMEM((rows, inner), LOW)] * 4
    outs = call(
        cross_backward_body,
        [
            full_shape(rows, model),
            full_shape(1, model),
            low_shape(rows, model),
            low_shape(half, model),
            low_shape(half, model),
        ]
        + group_shapes(2 * inner),
        (),
        (
            hidden_two,
            dpartial,
            swap_tensor(dpartial),
            gains,
            grad_three,
            normed_cross,
            memory,
            query_cross,
            key_cross,
            value_cross,
            mixed_cross,
            *cross_w,
        ),
        scratch=attention_scratch,
        flops=9 * unit,
        sent=range(5, 10),
    )
    grad_two, dgain_feed, dpartial, keep, away = outs[:5]
    dcross = outs[5:10]
    feed_terms, feed_merged = reduce_lower(
        dfeed, [after(one, dpartial) for one in feed_came], devices
    )
    cross_came = reduce_last(dcross, devices, feed_came)
    cross_terms, cross_merged = reduce_lower(dcross, cross_came, devices, feed_terms[1:])
    (encoder_half,) = call(
        encoder_body,
        [low_shape(half, model)],
        (),
        (permute, keep, swap_tensor(away)),
        flops=unit,
    )
    encoder_grad = deal(encoder_half, owner_of, devices)

    outs = call(
        self_backward_body,
        [
            full_shape(rows, model),
            full_shape(1, model),
            low_shape(rows, model),
            full_shape(heads, 2 * rows),
        ]
        + group_shapes(2 * inner),
        (length,),
        (
            bias_rows,
            hidden_one,
            dpartial,
            swap_tensor(dpartial),
            gains,
            after(grad_two, *feed_merged),
            normed_self,
            query_self,
            key_self,
            value_self,
            mixed_self,
            *self_w,
        ),
        scratch=attention_scratch,
        flops=10 * unit,
        sent=range(4, 9),
    )
    grad_one, dgain_cross, dpartial, diagonal = outs[:4]
    dself = outs[4:9]
    self_came = reduce_last(dself, devices, feed_terms[1:])
    self_terms, self_merged = reduce_lower(dself, self_came, devices)
    input_grad, dgains, dtable = call(
        finish_body,
        [low_shape(rows, model), full_shape(3, model), full_shape(buckets, heads)],
        (length,),
        (
            permute,
            masked_input,
            dpartial,
            swap_tensor(dpartial),
            gains,
            grad_one,
            dgain_cross,
            dgain_feed,
            onehot,
            diagonal,
        ),
        flops=2 * unit,
    )

    if across:
        down_terms = reduce_across(ddown, down_came, devices)
        feed_sums = reduce_upper(feed_terms, devices, down_terms[2:])
        down_sum = reduce_across_first(down_terms, devices)
    else:
        down_sum = reduce_upper(reduce_lower(ddown, down_came, devices)[0], devices)
        feed_sums = reduce_upper(feed_terms, devices)
    cross_sums = reduce_upper(cross_terms, devices, (feed_sums,))
    self_sums = reduce_upper(self_terms, devices, (cross_sums,))
    small = total_small(
        jnp.concatenate([dgains.reshape(-1), dtable.reshape(-1)]).reshape(-1, 128), devices
    ).reshape(-1)
    gain_sums = small[: 3 * model].reshape(3, model)
    table_sum = small[3 * model :].reshape(buckets, heads)

    def column(value, number, width):
        return value[:, number * width : (number + 1) * width]

    return (
        layer_result,
        input_grad,
        encoder_grad,
        table_sum,
        gain_sums[0],
        column(self_sums, 0, inner),
        column(self_sums, 1, inner),
        column(self_sums, 2, inner),
        column(self_sums, 3, inner),
        gain_sums[1],
        column(cross_sums, 2, inner),
        column(cross_sums, 0, inner),
        column(cross_sums, 1, inner),
        column(cross_sums, 3, inner),
        gain_sums[2],
        column(feed_sums, 0, feed),
        column(feed_sums, 1, feed),
        down_sum,
    )


def solution(mesh):
    in_specs = (
        P("dp", None),
        P("dp", None),
        P("dp", None),
        P(),
        P(),
        P(),
        P(None, "tensor"),
        P(),
        P("dp", "tensor"),
        P("dp", "tensor"),
        P("dp", "tensor"),
        P("dp", "tensor"),
        P(),
        P("dp", "tensor"),
        P("dp", "tensor"),
        P("dp", "tensor"),
        P("dp", "tensor"),
        P(),
        P("dp", "tensor"),
        P("dp", "tensor"),
        P("dp", "tensor"),
    )
    out_specs = (
        P("dp", None),
        P("dp", None),
        P(("dp", "tensor"), None),
        P(None, "tensor"),
        P(),
        P("dp", "tensor"),
        P("dp", "tensor"),
        P("dp", "tensor"),
        P("dp", "tensor"),
        P(),
        P("dp", "tensor"),
        P("dp", "tensor"),
        P("dp", "tensor"),
        P("dp", "tensor"),
        P(),
        P("dp", "tensor"),
        P("dp", "tensor"),
        P("dp", "tensor"),
    )
    return jax.shard_map(
        on_device, mesh=mesh, in_specs=in_specs, out_specs=out_specs, check_vma=False
    )
```

```python
import functools

import jax
import jax.numpy as jnp
import numpy as np
from jax import lax
from jax.experimental import pallas as pl
from jax.experimental.pallas import tpu as pltpu
from jax.sharding import PartitionSpec as P

EPSILON = 1e-06
MASKED = -1e30
HIGHEST = lax.Precision.HIGHEST
HEAD = 64
PAIR = 2 * HEAD
LOW = jnp.bfloat16
FULL = jnp.float32


def upper_masks(devices):
    if devices == 16:
        return [12, 4]
    return [1 << bit for bit in range(devices.bit_length() - 2, 1, -1)]


def block_offsets(masks):
    offsets = [0]
    for mask in masks:
        offsets = offsets + [offset ^ mask for offset in offsets]
    return offsets


def swap_dp(value, mask, devices):
    return lax.ppermute(value, "dp", [(one, one ^ mask) for one in range(devices)])


def swap_tensor(value):
    return lax.ppermute(value, "tensor", [(0, 1), (1, 0)])


def total_small(value, devices):
    mask = 1
    while mask < devices:
        value = value + swap_dp(value, mask, devices)
        mask = 2 * mask
    return value


def product_plain(left, right):
    return jnp.dot(left, right, preferred_element_type=FULL)


def product_right(left, right):
    return lax.dot_general(left, right, (((1,), (1,)), ((), ())), preferred_element_type=FULL)


def product_left(left, right):
    return lax.dot_general(left, right, (((0,), (0,)), ((), ())), preferred_element_type=FULL)


def quarter(ref, number):
    width = ref.shape[1] // 4
    return ref[:, number * width : (number + 1) * width]


def sides(refs):
    own, x_part, y_part, left, right = refs
    rows = left.shape[0]
    return (
        [own.at[:rows], x_part.at[:rows], y_part.at[:rows], left],
        [own.at[rows:], x_part.at[rows:], y_part.at[rows:], right],
    )


def after(value, *earlier):
    return lax.optimization_barrier((value, *earlier))[0]


def project_in(value_ref, pieces, columns):
    total = None
    for number, piece in enumerate(pieces):
        part = product_plain(quarter(value_ref, number), piece[:, columns])
        total = part if total is None else total + part
    return total


def inverse_root(value):
    return lax.rsqrt(jnp.mean(value * value, axis=-1, keepdims=True) + EPSILON)


def norm_backward(value, gain, upstream):
    root = inverse_root(value)
    weighted = upstream * gain
    inner_mean = jnp.mean(weighted * value, axis=-1, keepdims=True)
    grad = root * weighted - value * (root * root * root) * inner_mean
    return grad, jnp.sum(upstream * value * root, axis=0, keepdims=True)


def both(mine_ref, other_ref):
    return mine_ref[...].astype(FULL) + other_ref[...].astype(FULL)


def valid_column(length_ref, rows):
    return (lax.broadcasted_iota(jnp.int32, (rows, 1), 0) < length_ref[0]).astype(FULL)


def toeplitz_bias(row, rows):
    wide = jnp.broadcast_to(row, (rows, row.shape[1]))
    return pltpu.roll(wide, 0, 1, stride=1, stride_axis=0)[:, :rows]


def head_half(value, side, lanes):
    keep = lanes < HEAD if side == 0 else lanes >= HEAD
    return jnp.where(keep, value, jnp.zeros_like(value))


def masked_scores(query, key, length_ref, bias_ref, head):
    scores = product_right(query, key)
    if bias_ref is None:
        return scores
    rows, columns = scores.shape
    scores = scores + toeplitz_bias(bias_ref[pl.ds(head, 1), :], rows)
    at_row = lax.broadcasted_iota(jnp.int32, (rows, columns), 0)
    at_column = lax.broadcasted_iota(jnp.int32, (rows, columns), 1)
    allowed = (at_column <= at_row) & (at_column < length_ref[0])
    return jnp.where(allowed, scores, MASKED)


def softmax_rows(scores):
    exponent = jnp.exp(scores - jnp.max(scores, axis=-1, keepdims=True))
    return exponent * (1.0 / jnp.sum(exponent, axis=-1, keepdims=True))


def attention_forward(query_ref, key_ref, value_ref, out_ref, length_ref=None, bias_ref=None):
    rows, width = query_ref.shape
    lanes = lax.broadcasted_iota(jnp.int32, (rows, PAIR), 1)

    def one_pair(pair, carry):
        columns = pl.ds(pl.multiple_of(pair * PAIR, PAIR), PAIR)
        query, key, value = query_ref[:, columns], key_ref[:, columns], value_ref[:, columns]
        mixed = []
        for side in range(2):
            scores = masked_scores(
                head_half(query, side, lanes), key, length_ref, bias_ref, 2 * pair + side
            )
            mixed.append(product_plain(softmax_rows(scores).astype(LOW), value))
        out_ref[:, columns] = jnp.where(lanes < HEAD, mixed[0], mixed[1]).astype(LOW)
        return carry

    lax.fori_loop(0, width // PAIR, one_pair, 0)


def attention_backward(
    query_ref,
    key_ref,
    value_ref,
    grad_ref,
    dquery_ref,
    dkey_ref,
    dvalue_ref,
    length_ref=None,
    bias_ref=None,
    diagonal_ref=None,
):
    rows, width = query_ref.shape
    lanes = lax.broadcasted_iota(jnp.int32, (rows, PAIR), 1)
    if bias_ref is not None:
        flip = (
            lax.broadcasted_iota(jnp.int32, (rows, rows), 0)
            + lax.broadcasted_iota(jnp.int32, (rows, rows), 1)
            == rows - 1
        ).astype(LOW)

    def one_pair(pair, carry):
        columns = pl.ds(pl.multiple_of(pair * PAIR, PAIR), PAIR)
        query, key, value = query_ref[:, columns], key_ref[:, columns], value_ref[:, columns]
        grad = grad_ref[:, columns]
        dquery, dkey, dvalue = [], [], []
        for side in range(2):
            head = 2 * pair + side
            scores = masked_scores(head_half(query, side, lanes), key, length_ref, bias_ref, head)
            chance = softmax_rows(scores)
            chance_grad = product_right(head_half(grad, side, lanes), value)
            delta = jnp.sum(chance * chance_grad, axis=-1, keepdims=True)
            score_grad = (chance * (chance_grad - delta)).astype(LOW)
            dquery.append(product_plain(score_grad, key))
            dkey.append(product_left(score_grad, query))
            dvalue.append(product_left(chance.astype(LOW), grad))
            if bias_ref is not None:
                flipped = product_plain(flip, score_grad)
                wide = jnp.concatenate([flipped, jnp.zeros_like(flipped)], axis=1)
                skewed = pltpu.roll(wide, rows + 1, 1, stride=1, stride_axis=0)
                diagonal_ref[pl.ds(head, 1), :] = jnp.sum(skewed, axis=0, keepdims=True)
        left = lanes < HEAD
        dquery_ref[:, columns] = jnp.where(left, dquery[0], dquery[1]).astype(LOW)
        dkey_ref[:, columns] = jnp.where(left, dkey[0], dkey[1]).astype(LOW)
        dvalue_ref[:, columns] = jnp.where(left, dvalue[0], dvalue[1]).astype(LOW)
        return carry

    lax.fori_loop(0, width // PAIR, one_pair, 0)


def low_shape(*shape):
    return jax.ShapeDtypeStruct(shape, LOW)


def full_shape(*shape):
    return jax.ShapeDtypeStruct(shape, FULL)


def call(body, out_shape, scalars, arrays, scratch=(), flops=0, sent=()):
    vmem = pl.BlockSpec(memory_space=pltpu.VMEM)
    smem = pl.BlockSpec(memory_space=pltpu.SMEM)
    return pl.pallas_call(
        body,
        out_shape=list(out_shape),
        in_specs=[smem] * len(scalars) + [vmem] * len(arrays),
        out_specs=[
            pl.BlockSpec(one.shape, lambda step: (0, 0), pipeline_mode=pl.Buffered(1))
            if number in sent
            else vmem
            for number, one in enumerate(out_shape)
        ],
        grid=(1,) if sent else (),
        scratch_shapes=list(scratch),
        name=getattr(body, "func", body).__name__,
        cost_estimate=pl.CostEstimate(
            flops=int(flops * 1), transcendentals=0, bytes_accessed=1024
        ),
        compiler_params=pltpu.CompilerParams(vmem_limit_bytes=44 << 20),
    )(*scalars, *arrays)


def prepare_body(
    length_ref,
    tokens_ref,
    cotangent_ref,
    gains_ref,
    source_ref,
    permute_ref,
    input_ref,
    grad_ref,
    gains_out_ref,
    normed_ref,
):
    rows, width = tokens_ref.shape
    at_row = lax.broadcasted_iota(jnp.int32, (width, width), 0)
    permute_ref[...] = (at_row == source_ref[...]).astype(FULL).astype(LOW)
    permute = permute_ref[...]
    valid = valid_column(length_ref, rows)
    masked = product_plain(tokens_ref[...], permute) * valid
    input_ref[...] = masked.astype(LOW)
    grad_ref[...] = (product_plain(cotangent_ref[...], permute) * valid).astype(LOW)
    gains = gains_ref[...]
    high = gains.astype(LOW)
    middle = (gains - high.astype(FULL)).astype(LOW)
    low = (gains - high.astype(FULL) - middle.astype(FULL)).astype(LOW)
    gains_out_ref[...] = (
        product_plain(high, permute) + product_plain(middle, permute)
    ) + product_plain(low, permute)
    normed_ref[...] = (masked * inverse_root(masked) * gains_out_ref[0:1, :]).astype(LOW)


def self_forward_body(
    length_ref, bias_ref, normed_ref, *refs
):
    qk, vo = sides(refs[:5])
    query_ref, key_ref, value_ref, mixed_ref, partial_ref = refs[5:]
    inner = query_ref.shape[1]
    query_ref[...] = project_in(normed_ref, qk, slice(0, inner)).astype(LOW)
    key_ref[...] = project_in(normed_ref, qk, slice(inner, 2 * inner)).astype(LOW)
    value_ref[...] = project_in(normed_ref, vo, slice(0, inner)).astype(LOW)
    attention_forward(query_ref, key_ref, value_ref, mixed_ref, length_ref, bias_ref)
    width = partial_ref.shape[1] // 4
    for number in range(4):
        partial_ref[:, number * width : (number + 1) * width] = product_right(
            mixed_ref[...], vo[number][:, inner:]
        ).astype(LOW)


def memory_body(half_ref, other_ref, permute_ref, *refs):
    kv, _ = sides(refs[:5])
    memory_ref, key_ref, value_ref = refs[5:]
    inner = key_ref.shape[1]
    half = half_ref.shape[0]
    memory_ref[:half, :] = product_plain(half_ref[...], permute_ref[...]).astype(LOW)
    memory_ref[half:, :] = product_plain(other_ref[...], permute_ref[...]).astype(LOW)
    key_ref[...] = project_in(memory_ref, kv, slice(0, inner)).astype(LOW)
    value_ref[...] = project_in(memory_ref, kv, slice(inner, 2 * inner)).astype(LOW)


def cross_forward_body(input_ref, mine_ref, other_ref, gains_ref, key_ref, value_ref, *refs):
    _, qo = sides(refs[:5])
    hidden_ref, normed_ref, query_ref, mixed_ref, partial_ref = refs[5:]
    inner = query_ref.shape[1]
    hidden = input_ref[...].astype(FULL) + both(mine_ref, other_ref)
    hidden_ref[...] = hidden
    normed_ref[...] = (hidden * inverse_root(hidden) * gains_ref[1:2, :]).astype(LOW)
    query_ref[...] = project_in(normed_ref, qo, slice(0, inner)).astype(LOW)
    attention_forward(query_ref, key_ref, value_ref, mixed_ref)
    width = partial_ref.shape[1] // 4
    for number in range(4):
        partial_ref[:, number * width : (number + 1) * width] = product_right(
            mixed_ref[...], qo[number][:, inner:]
        ).astype(LOW)


GELU_SCALE = float(np.sqrt(2.0 / np.pi))
GELU_CUBE = 0.044715
CHUNK = 512


def feed_body(transposed, hidden_in_ref, mine_ref, other_ref, gains_ref, grad_ref, *refs):
    gate_w, lift_w = sides(refs[:5])
    down_w = refs[5:9]
    hidden_ref, partial_ref, dnormed_ref = refs[9:12]
    dgate_w, dlift_w = sides(refs[12:17])
    ddown_w = refs[17:21]
    normed_ref, normed_t_ref, grad_t_ref, down_ref, total_ref, dtotal_ref = refs[21:]
    rows, model = hidden_ref.shape
    width = model // 4
    block = width // 4
    feed = gate_w[0].shape[1]
    hidden = hidden_in_ref[...] + both(mine_ref, other_ref)
    hidden_ref[...] = hidden
    normed_ref[...] = (hidden * inverse_root(hidden) * gains_ref[2:3, :]).astype(LOW)
    normed_t_ref[...] = normed_ref[...].T
    grad_t_ref[...] = grad_ref[...].T
    for number in range(4):
        if transposed:
            for other in range(4):
                place = number * width + other * block
                down_ref[place : place + block, :] = down_w[other][
                    number * block : (number + 1) * block, :
                ]
        else:
            down_ref[number * width : (number + 1) * width, :] = down_w[number][...]
    total_ref[...] = jnp.zeros_like(total_ref)
    dtotal_ref[...] = jnp.zeros_like(dtotal_ref)

    def some_columns(columns):
        gate = project_in(normed_ref, gate_w, columns)
        lift = project_in(normed_ref, lift_w, columns)
        squared = gate * gate
        curve = jnp.tanh(GELU_SCALE * (gate + GELU_CUBE * squared * gate))
        half_up = 0.5 * (1.0 + curve)
        activated = gate * half_up
        product = (activated * lift).astype(LOW)
        down = down_ref[:, columns]
        dproduct = product_plain(grad_ref[...], down).astype(LOW).astype(FULL)
        slope = half_up + 0.5 * gate * (1.0 - curve * curve) * (
            GELU_SCALE * (1.0 + 3.0 * GELU_CUBE * squared)
        )
        dgate = (dproduct * lift * slope).astype(LOW)
        dlift = (dproduct * activated).astype(LOW)
        total_ref[...] += product_right(product, down)
        for number in range(4):
            part = slice(number * width, (number + 1) * width)
            normed_t = normed_t_ref[part, :]
            dgate_w[number][:, columns] = product_plain(normed_t, dgate).astype(LOW)
            dlift_w[number][:, columns] = product_plain(normed_t, dlift).astype(LOW)
            ddown = product_plain(grad_t_ref[part, :], product).astype(LOW)
            if transposed:
                for other in range(4):
                    ddown_w[other][number * block : (number + 1) * block, columns] = ddown[
                        other * block : (other + 1) * block, :
                    ]
            else:
                ddown_w[number][:, columns] = ddown
            dtotal_ref[:, part] += product_right(
                dgate, gate_w[number][:, columns]
            ) + product_right(dlift, lift_w[number][:, columns])

    def one_chunk(chunk, carry):
        some_columns(pl.ds(pl.multiple_of(chunk * CHUNK, CHUNK), CHUNK))
        return carry

    whole = feed // CHUNK
    lax.fori_loop(0, whole, one_chunk, 0)
    if feed % CHUNK:
        some_columns(pl.ds(whole * CHUNK, feed % CHUNK))
    partial_ref[...] = total_ref[...].astype(LOW)
    dnormed_ref[...] = dtotal_ref[...].astype(LOW)


def cross_backward_body(
    hidden_ref,
    mine_ref,
    other_ref,
    gains_ref,
    grad_ref,
    normed_ref,
    memory_ref,
    query_ref,
    key_ref,
    value_ref,
    mixed_ref,
    *refs,
):
    kv, qo = sides(refs[:5])
    grad_out_ref, dgain_ref, dnormed_ref, keep_ref, away_ref = refs[5:10]
    dkv, dqo = sides(refs[10:15])
    low_ref, transposed_ref, dmixed_ref, dquery_ref, dkey_ref, dvalue_ref = refs[15:]
    rows, model = hidden_ref.shape
    width = model // 4
    inner = query_ref.shape[1]
    half = rows // 2
    back, dgain_ref[...] = norm_backward(
        hidden_ref[...], gains_ref[2:3, :], both(mine_ref, other_ref)
    )
    grad = grad_ref[...].astype(FULL) + back
    grad_out_ref[...] = grad
    low_ref[...] = grad.astype(LOW)
    dmixed_ref[...] = project_in(low_ref, qo, slice(inner, 2 * inner)).astype(LOW)
    attention_backward(
        query_ref, key_ref, value_ref, dmixed_ref, dquery_ref, dkey_ref, dvalue_ref
    )
    for number in range(4):
        part = slice(number * width, (number + 1) * width)
        dnormed_ref[:, part] = product_right(dquery_ref[...], qo[number][:, :inner]).astype(LOW)
        partial = (
            product_right(dkey_ref[...], kv[number][:, :inner])
            + product_right(dvalue_ref[...], kv[number][:, inner:])
        ).astype(LOW)
        keep_ref[:, part] = partial[:half]
        away_ref[:, part] = partial[half:]
    transposed_ref[...] = memory_ref[...].T
    for number in range(4):
        part = slice(number * width, (number + 1) * width)
        dkv[number][:, :inner] = product_plain(transposed_ref[part, :], dkey_ref[...]).astype(LOW)
        dkv[number][:, inner:] = product_plain(transposed_ref[part, :], dvalue_ref[...]).astype(
            LOW
        )
    transposed_ref[...] = normed_ref[...].T
    for number in range(4):
        part = slice(number * width, (number + 1) * width)
        dqo[number][:, :inner] = product_plain(transposed_ref[part, :], dquery_ref[...]).astype(
            LOW
        )
    transposed_ref[...] = low_ref[...].T
    for number in range(4):
        part = slice(number * width, (number + 1) * width)
        dqo[number][:, inner:] = product_plain(transposed_ref[part, :], mixed_ref[...]).astype(LOW)


def self_backward_body(
    length_ref,
    bias_ref,
    hidden_ref,
    mine_ref,
    other_ref,
    gains_ref,
    grad_ref,
    normed_ref,
    query_ref,
    key_ref,
    value_ref,
    mixed_ref,
    *refs,
):
    qk, vo = sides(refs[:5])
    grad_out_ref, dgain_ref, dnormed_ref, diagonal_ref = refs[5:9]
    dqk, dvo = sides(refs[9:14])
    low_ref, transposed_ref, dmixed_ref, dquery_ref, dkey_ref, dvalue_ref = refs[14:]
    rows, model = hidden_ref.shape
    width = model // 4
    inner = query_ref.shape[1]
    back, dgain_ref[...] = norm_backward(
        hidden_ref[...], gains_ref[1:2, :], both(mine_ref, other_ref)
    )
    grad = grad_ref[...] + back
    grad_out_ref[...] = grad
    low_ref[...] = grad.astype(LOW)
    dmixed_ref[...] = project_in(low_ref, vo, slice(inner, 2 * inner)).astype(LOW)
    attention_backward(
        query_ref,
        key_ref,
        value_ref,
        dmixed_ref,
        dquery_ref,
        dkey_ref,
        dvalue_ref,
        length_ref,
        bias_ref,
        diagonal_ref,
    )
    for number in range(4):
        part = slice(number * width, (number + 1) * width)
        dnormed_ref[:, part] = (
            product_right(dquery_ref[...], qk[number][:, :inner])
            + product_right(dkey_ref[...], qk[number][:, inner:])
            + product_right(dvalue_ref[...], vo[number][:, :inner])
        ).astype(LOW)
    transposed_ref[...] = normed_ref[...].T
    for number in range(4):
        part = slice(number * width, (number + 1) * width)
        dqk[number][:, :inner] = product_plain(transposed_ref[part, :], dquery_ref[...]).astype(
            LOW
        )
        dqk[number][:, inner:] = product_plain(transposed_ref[part, :], dkey_ref[...]).astype(LOW)
        dvo[number][:, :inner] = product_plain(transposed_ref[part, :], dvalue_ref[...]).astype(
            LOW
        )
    transposed_ref[...] = low_ref[...].T
    for number in range(4):
        part = slice(number * width, (number + 1) * width)
        dvo[number][:, inner:] = product_plain(transposed_ref[part, :], mixed_ref[...]).astype(LOW)


def finish_body(
    length_ref,
    permute_ref,
    input_ref,
    mine_ref,
    other_ref,
    gains_ref,
    grad_ref,
    dgain_cross_ref,
    dgain_feed_ref,
    onehot_ref,
    diagonal_ref,
    out_ref,
    dgains_ref,
    table_ref,
):
    rows = input_ref.shape[0]
    permute = permute_ref[...]
    back, dgain = norm_backward(
        input_ref[...].astype(FULL), gains_ref[0:1, :], both(mine_ref, other_ref)
    )
    total = ((grad_ref[...] + back) * valid_column(length_ref, rows)).astype(LOW)
    out_ref[...] = product_right(total, permute).astype(LOW)
    dgains = jnp.concatenate([dgain, dgain_cross_ref[...], dgain_feed_ref[...]], axis=0)
    high = dgains.astype(LOW)
    middle = (dgains - high.astype(FULL)).astype(LOW)
    low = (dgains - high.astype(FULL) - middle.astype(FULL)).astype(LOW)
    dgains_ref[...] = (
        product_right(high, permute) + product_right(middle, permute)
    ) + product_right(low, permute)
    table_ref[...] = lax.dot_general(
        onehot_ref[...],
        diagonal_ref[...],
        (((1,), (1,)), ((), ())),
        precision=HIGHEST,
        preferred_element_type=FULL,
    )


def output_body(length_ref, permute_ref, hidden_ref, mine_ref, other_ref, out_ref):
    rows = hidden_ref.shape[0]
    total = (hidden_ref[...] + both(mine_ref, other_ref)) * valid_column(length_ref, rows)
    out_ref[...] = product_right(total.astype(LOW), permute_ref[...]).astype(LOW)


def encoder_body(permute_ref, mine_ref, other_ref, out_ref):
    total = both(mine_ref, other_ref).astype(LOW)
    out_ref[...] = product_right(total, permute_ref[...]).astype(LOW)


def fold_body(*refs):
    own, one, two = refs[:3]
    outs = refs[3:]
    width = own.shape[1]
    sides_held = outs[0].shape[1] // width
    block = outs[0].shape[0]
    for side in range(sides_held):
        for place in range(4):
            first = (4 * side + place) * block
            rows = slice(first, first + block)
            total = (
                own[rows, :].astype(FULL) + one[rows, :].astype(FULL) + two[rows, :].astype(FULL)
            )
            outs[place][:, side * width : (side + 1) * width] = total.astype(outs[place].dtype)


def fold_quarter(terms, sides_held):
    rows = terms[0].shape[0] // (4 * sides_held)
    width = terms[0].shape[1] * sides_held
    kinds = [full_shape, full_shape, low_shape, low_shape]
    return call(fold_body, [kind(rows, width) for kind in kinds], (), terms, sent=(2, 3))


def stack_body(*refs):
    parts, outs = refs[:4], refs[4:]
    block = parts[0].shape[0]
    first = 0
    for out in outs:
        width = out.shape[1]
        for side in range(out.shape[0] // (4 * block)):
            for place in range(4):
                row = (4 * side + place) * block
                out[row : row + block, :] = parts[place][:, first : first + width]
            first += width


def stack_quarter(parts, shapes):
    return call(
        stack_body, [low_shape(*shape) for shape in shapes], (), parts, sent=range(len(shapes))
    )


def merge_body(x_in, y_in, left, right, x_out, y_out):
    x_out[...] = (x_in[...].astype(FULL) + left[...].astype(FULL)).astype(LOW)
    y_out[...] = (y_in[...].astype(FULL) + right[...].astype(FULL)).astype(LOW)


def merge_quarters(x_part, y_part, left, right):
    rows, width = left.shape
    steps = 2
    part = rows // steps
    first = pl.BlockSpec((part, width), lambda step: (step, 0))
    second = pl.BlockSpec((part, width), lambda step: (steps + step, 0))
    at = [first, second]
    return pl.pallas_call(
        merge_body,
        out_shape=[low_shape(*x_part.shape), low_shape(*y_part.shape)],
        grid=(steps,),
        in_specs=at + [first, first],
        out_specs=at,
        input_output_aliases={0: 0, 1: 1},
        name="merge_body",
        cost_estimate=pl.CostEstimate(flops=1024, transcendentals=0, bytes_accessed=1024),
    )(x_part, y_part, left, right)


def gather_upper(value, devices, wait=()):
    masks = upper_masks(devices)
    if wait:
        value = after(value, *wait)
    if len(masks) == 2:
        one = swap_dp(value, masks[0], devices)
        two = swap_dp(value, masks[1], devices)
        return [value, one, two, swap_dp(after(one, two), masks[1], devices)]
    for mask in masks:
        value = jnp.concatenate([value, swap_dp(value, mask, devices)], axis=0)
    return [value]


def stack_sides(blocks, widths):
    if len(blocks) == 4:
        rows = 4 * blocks[0].shape[0]
        return stack_quarter(blocks, [(2 * rows, width) for width in widths])
    groups, first = [], 0
    for width in widths:
        middle, last = first + width, first + 2 * width
        groups.append(
            jnp.concatenate([blocks[0][:, first:middle], blocks[0][:, middle:last]], axis=0)
        )
        first = last
    return groups


def gather_lower(first, devices, x_wait=(), y_wait=(), last_wait=()):
    rows = first.shape[0] // 2
    x_part = swap_dp(after(first, *x_wait) if x_wait else first, 1, devices)
    y_part = swap_dp(after(first, *y_wait) if y_wait else first, 2, devices)
    left, right = x_part[:rows], y_part[rows:]
    if last_wait:
        left, right = after(left, *last_wait), after(right, *last_wait)
    return [first, x_part, y_part, swap_dp(left, 2, devices), swap_dp(right, 1, devices)]


def reduce_last(pieces, devices, wait=()):
    left, right = pieces[3:]
    if wait:
        left, right = after(left, *wait), after(right, *wait)
    return [swap_dp(left, 2, devices), swap_dp(right, 1, devices)]


def reduce_lower(pieces, came, devices, wait=()):
    merged = merge_quarters(*pieces[1:3], *came)
    x_part, y_part = merged
    if wait:
        x_part, y_part = after(x_part, *wait), after(y_part, *wait)
    return [pieces[0], swap_dp(x_part, 1, devices), swap_dp(y_part, 2, devices)], merged


def reduce_upper(terms, devices, wait=()):
    masks = upper_masks(devices)
    if len(masks) == 2:
        own, one, two, three = fold_quarter(terms, 2)
        if wait:
            two, three = after(two, *wait), after(three, *wait)
        one = (one + swap_dp(three, masks[1], devices).astype(FULL)).astype(LOW)
        two = swap_dp(two, masks[1], devices)
        return own + two.astype(FULL) + swap_dp(one, masks[0], devices).astype(FULL)
    value = terms[0].astype(FULL) + terms[1].astype(FULL) + terms[2].astype(FULL)
    rows = value.shape[0] // 2
    value = jnp.concatenate([value[:rows], value[rows:]], axis=1)
    for mask in masks[::-1]:
        half = value.shape[0] // 2
        away = swap_dp(value[half:].astype(LOW), mask, devices)
        value = value[:half] + away.astype(FULL)
    return value


def first_across(value, devices):
    x_part, y_part = swap_dp(value, 1, devices), swap_dp(value, 2, devices)
    return [value, x_part, y_part, swap_dp(x_part, 2, devices)]


def gather_across(blocks, devices, wait):
    masks = upper_masks(devices)
    rows, width = blocks[0].shape
    first = after(stack_quarter(blocks, [(4 * rows, width)])[0], *wait)
    one, two = swap_dp(first, masks[0], devices), swap_dp(first, masks[1], devices)
    return [first, one, two, swap_dp(one, masks[1], devices)]


def reduce_across_last(pieces, devices):
    mask = upper_masks(devices)[1]
    return [swap_dp(pieces[3], mask, devices), swap_dp(pieces[2], mask, devices)]


def reduce_across(pieces, came, devices):
    mask = upper_masks(devices)[0]
    one = (pieces[1].astype(FULL) + came[0].astype(FULL)).astype(LOW)
    return [pieces[0], came[1], swap_dp(one, mask, devices)]


def reduce_across_first(terms, devices):
    own, x_part, y_part, last = fold_quarter(terms, 1)
    x_part = (x_part + swap_dp(last, 2, devices).astype(FULL)).astype(LOW)
    return (
        own
        + swap_dp(y_part, 2, devices).astype(FULL)
        + swap_dp(x_part, 1, devices).astype(FULL)
    )


def deal(value, order, devices):
    rows, width = value.shape
    first = lax.all_to_all(
        value.reshape(devices, rows // devices, width), "dp", split_axis=0, concat_axis=0, tiled=True
    )
    second = lax.all_to_all(
        jnp.take(first, order, axis=0), "dp", split_axis=0, concat_axis=0, tiled=True
    )
    return second.reshape(rows, width)


def on_device(
    tokens,
    encoder_states,
    cotangent,
    lengths,
    deal_order,
    bucket_index,
    rel_table,
    gain_self,
    self_query,
    self_key,
    self_value,
    self_output,
    gain_cross,
    cross_query,
    cross_key,
    cross_value,
    cross_output,
    gain_feed,
    feed_gate,
    feed_value,
    feed_output,
):
    devices = lax.axis_size("dp")
    myself = lax.axis_index("dp")
    core = lax.axis_index("tensor")
    rows, model = tokens.shape
    block = model // devices
    buckets, heads = rel_table.shape
    inner = self_query.shape[1]
    feed = feed_gate.shape[1]
    across = devices == 16

    numbers = jnp.arange(devices, dtype=jnp.int32)
    owner_of = jnp.sum(
        jnp.where(deal_order[:, None] == numbers[None, :], numbers[:, None], 0), axis=0
    )
    length = jnp.sum(jnp.where(numbers == myself, lengths, 0)).reshape(1)

    self_own = jnp.concatenate([self_query, self_key, self_value, self_output], axis=1)
    cross_own = jnp.concatenate([cross_key, cross_value, cross_query, cross_output], axis=1)
    feed_own = jnp.concatenate([feed_gate, feed_value], axis=1)
    self_blocks = gather_upper(self_own, devices)
    if across:
        down_blocks = first_across(feed_output, devices)
        self_blocks[3] = after(self_blocks[3], *down_blocks[1:3])
    (self_first,) = stack_sides(self_blocks, [2 * inner])
    cross_blocks = gather_upper(cross_own, devices, self_blocks[1:3])
    self_w = gather_lower(self_first, devices)
    (cross_first,) = stack_sides(cross_blocks, [2 * inner])
    cross_w = gather_lower(cross_first, devices, self_w[1:3], self_w[1:3], self_w[3:])
    feed_blocks = gather_upper(feed_own, devices, cross_blocks[1:3])
    (feed_first,) = stack_sides(feed_blocks, [feed])
    if across:
        down = gather_across(down_blocks, devices, feed_blocks[1:3])
    else:
        down = gather_upper(feed_output, devices)[0]
        width = feed // 2
        down = gather_lower(
            jnp.concatenate([down[:, :width], down[:, width:]], axis=0), devices
        )
        middle = down[0].shape[0] // 2
        down = [
            jnp.concatenate([one[:middle], one[middle:]], axis=1) for one in down[:3]
        ] + [jnp.concatenate(down[3:], axis=1)]

    offsets = jnp.asarray(np.array(block_offsets(upper_masks(devices) + [1, 2]), np.int32))
    source = (
        ((myself ^ offsets) * block)[:, None] + jnp.arange(block, dtype=jnp.int32)[None, :]
    ).reshape(1, -1)
    permute, masked_input, grad_three, gains, normed_self = call(
        prepare_body,
        [
            low_shape(model, model),
            low_shape(rows, model),
            low_shape(rows, model),
            full_shape(3, model),
            low_shape(rows, model),
        ],
        (length,),
        (tokens, cotangent, jnp.stack([gain_self, gain_cross, gain_feed]), source),
        flops=4 * rows * model * model,
    )

    half = rows // 2
    memory_half = deal(
        lax.dynamic_slice_in_dim(encoder_states, core * half, half, axis=0), deal_order, devices
    )
    memory_other = swap_tensor(memory_half)

    skewed_bucket = jnp.concatenate(
        [bucket_index[:1], jnp.full((rows,), -1, jnp.int32), bucket_index[::-1][: rows - 1]]
    )
    onehot = (jnp.arange(buckets, dtype=jnp.int32)[:, None] == skewed_bucket[None, :]).astype(FULL)
    bias_rows = jnp.dot(rel_table.T, onehot, precision=HIGHEST)

    unit = 2 * rows * model * inner
    query_self, key_self, value_self, mixed_self, self_partial = call(
        self_forward_body,
        [low_shape(rows, inner)] * 4 + [low_shape(rows, model)],
        (length,),
        (bias_rows, normed_self, *self_w),
        flops=5 * unit,
    )
    memory, key_cross, value_cross = call(
        memory_body,
        [low_shape(rows, model)] + [low_shape(rows, inner)] * 2,
        (),
        (memory_half, memory_other, permute, *cross_w),
        flops=4 * unit,
    )
    hidden_one, normed_cross, query_cross, mixed_cross, partial = call(
        cross_forward_body,
        [full_shape(rows, model), low_shape(rows, model)]
        + [low_shape(rows, inner)] * 2
        + [low_shape(rows, model)],
        (),
        (
            masked_input,
            self_partial,
            swap_tensor(self_partial),
            gains,
            key_cross,
            value_cross,
            *cross_w,
        ),
        flops=3 * unit,
    )
    quarter_rows = model // 4
    feed_w = gather_lower(
        feed_first,
        devices,
        (cross_w[1], self_partial),
        (cross_w[2], self_partial),
        (partial,),
    )

    def group_shapes(width):
        return [low_shape(2 * quarter_rows, width)] * 3 + [low_shape(quarter_rows, width)] * 2

    feed_grads = group_shapes(feed) + [low_shape(quarter_rows, feed)] * 4
    outs = call(
        functools.partial(feed_body, across),
        [full_shape(rows, model), low_shape(rows, model), low_shape(rows, model)] + feed_grads,
        (),
        (hidden_one, partial, swap_tensor(partial), gains, grad_three, *feed_w, *down),
        scratch=[
            pltpu.VMEM((rows, model), LOW),
            pltpu.VMEM((model, rows), LOW),
            pltpu.VMEM((model, rows), LOW),
            pltpu.VMEM((model, feed), LOW),
            pltpu.VMEM((rows, model), FULL),
            pltpu.VMEM((rows, model), FULL),
        ],
        flops=18 * rows * model * feed,
        sent=range(3, 12),
    )
    hidden_two, partial, dpartial = outs[:3]
    dfeed, ddown = outs[3:8], outs[8:12]
    feed_came = reduce_last(dfeed, devices)
    if across:
        down_came = reduce_across_last(ddown, devices)
    else:
        width = feed // 2
        ddown = [
            jnp.concatenate([one[:, :width], one[:, width:]], axis=0) for one in ddown[:3]
        ] + [ddown[3][:, :width], ddown[3][:, width:]]
        down_came = reduce_last(ddown, devices)
    (layer_result,) = call(
        output_body,
        [low_shape(rows, model)],
        (length,),
        (permute, hidden_two, partial, swap_tensor(partial)),
        flops=2 * unit,
    )

    attention_scratch = [
        pltpu.VMEM((rows, model), LOW),
        pltpu.VMEM((model, rows), LOW),
    ] + [pltpu.VMEM((rows, inner), LOW)] * 4
    outs = call(
        cross_backward_body,
        [
            full_shape(rows, model),
            full_shape(1, model),
            low_shape(rows, model),
            low_shape(half, model),
            low_shape(half, model),
        ]
        + group_shapes(2 * inner),
        (),
        (
            hidden_two,
            dpartial,
            swap_tensor(dpartial),
            gains,
            grad_three,
            normed_cross,
            memory,
            query_cross,
            key_cross,
            value_cross,
            mixed_cross,
            *cross_w,
        ),
        scratch=attention_scratch,
        flops=9 * unit,
        sent=range(5, 10),
    )
    grad_two, dgain_feed, dpartial, keep, away = outs[:5]
    dcross = outs[5:10]
    feed_terms, feed_merged = reduce_lower(
        dfeed, [after(one, dpartial) for one in feed_came], devices
    )
    cross_came = reduce_last(dcross, devices, feed_came)
    cross_terms, cross_merged = reduce_lower(dcross, cross_came, devices, feed_terms[1:])
    (encoder_half,) = call(
        encoder_body,
        [low_shape(half, model)],
        (),
        (permute, keep, swap_tensor(away)),
        flops=unit,
    )
    encoder_grad = deal(encoder_half, owner_of, devices)

    outs = call(
        self_backward_body,
        [
            full_shape(rows, model),
            full_shape(1, model),
            low_shape(rows, model),
            full_shape(heads, 2 * rows),
        ]
        + group_shapes(2 * inner),
        (length,),
        (
            bias_rows,
            hidden_one,
            dpartial,
            swap_tensor(dpartial),
            gains,
            after(grad_two, *feed_merged),
            normed_self,
            query_self,
            key_self,
            value_self,
            mixed_self,
            *self_w,
        ),
        scratch=attention_scratch,
        flops=10 * unit,
        sent=range(4, 9),
    )
    grad_one, dgain_cross, dpartial, diagonal = outs[:4]
    dself = outs[4:9]
    self_came = reduce_last(dself, devices, feed_terms[1:])
    self_terms, self_merged = reduce_lower(dself, self_came, devices)
    input_grad, dgains, dtable = call(
        finish_body,
        [low_shape(rows, model), full_shape(3, model), full_shape(buckets, heads)],
        (length,),
        (
            permute,
            masked_input,
            dpartial,
            swap_tensor(dpartial),
            gains,
            grad_one,
            dgain_cross,
            dgain_feed,
            onehot,
            diagonal,
        ),
        flops=2 * unit,
    )

    if across:
        down_terms = reduce_across(ddown, down_came, devices)
        feed_sums = reduce_upper(feed_terms, devices, down_terms[2:])
        down_sum = reduce_across_first(down_terms, devices)
    else:
        down_sum = reduce_upper(reduce_lower(ddown, down_came, devices)[0], devices)
        feed_sums = reduce_upper(feed_terms, devices)
    cross_sums = reduce_upper(cross_terms, devices, (feed_sums,))
    self_sums = reduce_upper(self_terms, devices, (cross_sums,))
    small = total_small(
        jnp.concatenate([dgains.reshape(-1), dtable.reshape(-1)]).reshape(-1, 128), devices
    ).reshape(-1)
    gain_sums = small[: 3 * model].reshape(3, model)
    table_sum = small[3 * model :].reshape(buckets, heads)

    def column(value, number, width):
        return value[:, number * width : (number + 1) * width]

    return (
        layer_result,
        input_grad,
        encoder_grad,
        table_sum,
        gain_sums[0],
        column(self_sums, 0, inner),
        column(self_sums, 1, inner),
        column(self_sums, 2, inner),
        column(self_sums, 3, inner),
        gain_sums[1],
        column(cross_sums, 2, inner),
        column(cross_sums, 0, inner),
        column(cross_sums, 1, inner),
        column(cross_sums, 3, inner),
        gain_sums[2],
        column(feed_sums, 0, feed),
        column(feed_sums, 1, feed),
        down_sum,
    )


def solution(mesh):
    in_specs = (
        P("dp", None),
        P("dp", None),
        P("dp", None),
        P(),
        P(),
        P(),
        P(None, "tensor"),
        P(),
        P("dp", "tensor"),
        P("dp", "tensor"),
        P("dp", "tensor"),
        P("dp", "tensor"),
        P(),
        P("dp", "tensor"),
        P("dp", "tensor"),
        P("dp", "tensor"),
        P("dp", "tensor"),
        P(),
        P("dp", "tensor"),
        P("dp", "tensor"),
        P("dp", "tensor"),
    )
    out_specs = (
        P("dp", None),
        P("dp", None),
        P(("dp", "tensor"), None),
        P(None, "tensor"),
        P(),
        P("dp", "tensor"),
        P("dp", "tensor"),
        P("dp", "tensor"),
        P("dp", "tensor"),
        P(),
        P("dp", "tensor"),
        P("dp", "tensor"),
        P("dp", "tensor"),
        P("dp", "tensor"),
        P(),
        P("dp", "tensor"),
        P("dp", "tensor"),
        P("dp", "tensor"),
    )
    return jax.shard_map(
        on_device, mesh=mesh, in_specs=in_specs, out_specs=out_specs, check_vma=False
    )
```
